128 devices in a mesh: wide: 16 (over z, x), narrow: 8 (over y, core).
Axes of the slice: x: 4, y: 4, z: 4, core: 2. Of those that a mesh axis runs over, the one named last changes fastest.
Arguments:
- recording: bfloat16 [131072, 512], P(('wide', 'narrow')), may hold values from -6 to 6
- conv_weight: bfloat16 [3, 3, 512, 512], replicated, may hold values from -0.15625 to 0.15625
- conv_bias: float32 [3, 512], replicated, may hold values from -3 to 3
- projection: bfloat16 [512, 64], replicated, may hold values from -0.25 to 0.25
Outputs:
- path_points: bfloat16 [131072, 64], P(('wide', 'narrow'))
- level_one: float32 [16, 64], P('wide')
- level_two: float32 [16, 4096], P('wide')
- level_three: float32 [16, 64, 4096], P('wide', 'narrow')
The draws below stay inside these ranges and needn't reach their ends.
All inputs are finite; a program needn't handle non-finite values.
Results may differ from the reference program's by a relative error of at most 0.0075.
Values may be sent and summed in bfloat16 or wider, within the bound.
A program may use at most 64 MiB of HBM per device.

```python
import jax
import jax.numpy as jnp
from jax import lax

C = 512
PATH = 64
LAYERS = 3
TAPS = 3
TD = 1024
TOTAL = 131072
N_WIDE = 16
N_NARROW = 8


def levels(own_key, shape, shards, smallest, largest):
    level = 1.0
    for position, shards_of in shards:
        heights = jax.random.uniform(jax.random.fold_in(jax.random.fold_in(own_key, 6), position), (shards_of,), jnp.float32, smallest / len(shards), largest / len(shards))
        level = level * jnp.repeat(jnp.exp(heights), shape[position] // shards_of).reshape((-1,) + (1,) * (len(shape) - 1 - position))
    return level


def noise(stream_key, shape, scale, most, cuts=(), held_as=jnp.bfloat16):
    entries = scale * jax.random.normal(stream_key, shape, jnp.float32)
    if cuts:
        entries = entries * levels(stream_key, shape, cuts, -0.22, 0.18)
    return jnp.clip(entries, -most, most).astype(held_as)


def setup_inputs(seed: int = 0) -> dict:
    key_of = jax.random.split(jax.random.key(seed), 5)
    return {
        "recording": noise(key_of[0], (TOTAL, C), 1.0, 6.0, ((0, 128),)),
        "conv_weight": noise(key_of[1], (LAYERS, TAPS, C, C), (TAPS * C) ** -0.5, 0.15625),
        "conv_bias": noise(key_of[2], (LAYERS, C), 0.5, 3.0, (), jnp.float32),
        "projection": noise(key_of[3], (C, PATH), C ** -0.5, 0.25),
    }


PRECISE = lax.Precision.HIGHEST


def conv_layer(hidden, weights, layer_bias, dilation):
    padded = jnp.pad(hidden, ((dilation, dilation), (0, 0)))
    length = hidden.shape[0]
    totals = layer_bias.astype(jnp.float32)[None, :]
    for tap_idx in range(3):
        window = padded[tap_idx * dilation: tap_idx * dilation + length]
        totals = totals + jnp.dot(window, weights[tap_idx], preferred_element_type=jnp.float32)
    return (hidden.astype(jnp.float32) + jax.nn.silu(totals)).astype(jnp.bfloat16)


def sig_update(signature, increments, row_start, row_count):
    first_level, second_level, third_level = signature
    path_width = increments.shape[1]
    step_count = increments.shape[0]
    running = jnp.cumsum(increments, axis=0)
    totals = running[-1]
    before = first_level[None, :] + running - increments
    remaining = totals[None, :] - running
    before_rows = lax.dynamic_slice_in_dim(before, row_start, row_count, 1)
    step_rows = lax.dynamic_slice_in_dim(increments, row_start, row_count, 1)
    second_terms = ((before_rows + 0.5 * step_rows)[:, :, None] * increments[:, None, :]).reshape(step_count, row_count * path_width)
    third_terms = ((0.5 * before_rows + step_rows / 6.0)[:, :, None] * increments[:, None, :]).reshape(step_count, row_count * path_width)
    gained = jnp.einsum('nm,nk->mk', second_terms, remaining, precision=PRECISE)
    gained = gained + jnp.einsum('nm,nk->mk', third_terms, increments, precision=PRECISE)
    second_rows = lax.dynamic_slice_in_dim(second_level, row_start, row_count, 0)
    carried = (second_rows[:, :, None] * totals[None, None, :]).reshape(row_count, path_width * path_width)
    third_level = third_level + carried + gained.reshape(row_count, path_width * path_width)
    second_level = second_level + jnp.einsum('ni,nj->ij', before, increments, precision=PRECISE)
    second_level = second_level + 0.5 * jnp.einsum('ni,nj->ij', increments, increments, precision=PRECISE)
    first_level = first_level + totals
    return first_level, second_level, third_level


def reference(recording, conv_weight, conv_bias, projection):
    hidden = recording
    for layer_idx in range(LAYERS):
        hidden = conv_layer(hidden, conv_weight[layer_idx], conv_bias[layer_idx], 2 ** layer_idx)
    path_points = jnp.dot(hidden, projection, preferred_element_type=jnp.float32).astype(jnp.bfloat16)
    points = path_points.astype(jnp.float32)
    earlier = jnp.concatenate([jnp.zeros((1, PATH), jnp.float32), points[:-1]], axis=0)
    increments = (points - earlier) * (TOTAL ** -0.2)
    blocks = increments.reshape(N_WIDE, N_NARROW, TD, PATH)
    empty_state = (jnp.zeros((PATH,), jnp.float32), jnp.zeros((PATH, PATH), jnp.float32),
                   jnp.zeros((PATH, PATH * PATH), jnp.float32))

    def inner(signature, piece):
        return sig_update(signature, piece, 0, PATH), None

    def outer(signature, wide_block):
        signature, unused = lax.scan(inner, signature, wide_block)
        return signature, signature

    unused_final, stacked = lax.scan(outer, empty_state, blocks)
    return (path_points, stacked[0], stacked[1].reshape(N_WIDE, PATH * PATH),
            stacked[2].reshape(N_WIDE, PATH, PATH * PATH))
```

```python
import functools

import jax
import jax.numpy as jnp
from jax import lax
from jax.experimental import pallas as pl
from jax.experimental.pallas import tpu as pltpu
from jax.sharding import PartitionSpec as P

C = 512
PATH = 64
TD = 1024
OFF = 32
ROWS = OFF + TD + 32
NX = 4
NZ = 4
NY = 4
TILE = 256
PAY = 256 + 64 + 16
MESH = pl.DeviceIdType.MESH
BF = jnp.bfloat16
F32 = jnp.float32


def silu(v):
    half = 0.5 * v
    return half + half * jnp.tanh(half)


def nt_dot(a, b):
    return lax.dot_general(a, b, (((1,), (1,)), ((), ())), preferred_element_type=F32)


def kernel(
    total_steps,
    rec_hbm,
    weight_hbm,
    bias_ref,
    proj_ref,
    path_ref,
    third_ref,
    second_ref,
    first_ref,
    weights,
    h0,
    h1,
    h2,
    seg,
    mid,
    step,
    centre,
    acc,
    level2,
    mine,
    partner_out,
    partner_in,
    out_x,
    in_x,
    out_z,
    in_z,
    w_sem,
    r_sem,
    halo_send,
    halo_recv,
    y_send,
    y_recv,
    p_send,
    p_recv,
    x_send,
    x_recv,
    z_send,
    z_recv,
):
    w = lax.axis_index("wide")
    n = lax.axis_index("narrow")
    z, x = lax.div(w, NX), lax.rem(w, NX)
    y, core = lax.div(n, 2), lax.rem(n, 2)
    g = w * 8 + n
    last_g = NX * NZ * 8 - 1
    has_left = g > 0
    has_right = g < last_g
    left = (lax.div(g + last_g, 8) % (NX * NZ), lax.rem(g + last_g, 8))
    right = (lax.div(g + 1, 8) % (NX * NZ), lax.rem(g + 1, 8))

    def y_peer(by):
        return (w, lax.rem(y + by, NY) * 2 + core)

    def x_peer(by):
        return (z * NX + lax.rem(x + by, NX), n)

    def z_peer(by):
        return ((z + by) * NX + x, n)

    partner = (w, y * 2 + 1 - core)

    weight_copies = [
        pltpu.make_async_copy(weight_hbm.at[l], weights.at[l], w_sem.at[l]) for l in range(3)
    ]
    own_copy = pltpu.make_async_copy(rec_hbm, h0.at[pl.ds(OFF, TD)], r_sem)
    own_copy.start()
    for copy in weight_copies:
        copy.start()

    barrier = pltpu.get_barrier_semaphore()

    @pl.when(has_left)
    def _():
        pl.semaphore_signal(barrier, inc=1, device_id=left, device_id_type=MESH)

    @pl.when(has_right)
    def _():
        pl.semaphore_signal(barrier, inc=1, device_id=right, device_id_type=MESH)

    for by in range(1, 4):
        pl.semaphore_signal(barrier, inc=1, device_id=y_peer(by), device_id_type=MESH)
        pl.semaphore_signal(barrier, inc=1, device_id=x_peer(by), device_id_type=MESH)

        @pl.when(z >= by)
        def _():
            pl.semaphore_signal(barrier, inc=1, device_id=z_peer(-by), device_id_type=MESH)

    pl.semaphore_signal(barrier, inc=1, device_id=partner, device_id_type=MESH)
    copied_to = has_left.astype(jnp.int32) + has_right.astype(jnp.int32) + 7 + (NZ - 1 - z)
    pl.semaphore_wait(barrier, copied_to)

    def remote(src, dst, send, recv, device):
        return pltpu.make_async_remote_copy(
            src_ref=src,
            dst_ref=dst,
            send_sem=send,
            recv_sem=recv,
            device_id=device,
            device_id_type=MESH,
        )

    to_left = remote(
        rec_hbm.at[pl.ds(0, 16)],
        h0.at[pl.ds(OFF + TD, 16)],
        halo_send.at[0],
        halo_recv.at[0],
        left,
    )
    to_right = remote(
        rec_hbm.at[pl.ds(TD - 16, 16)],
        h0.at[pl.ds(OFF - 16, 16)],
        halo_send.at[1],
        halo_recv.at[1],
        right,
    )

    @pl.when(has_left)
    def _():
        to_left.start()

    @pl.when(has_right)
    def _():
        to_right.start()

    def conv(layer, src, begin, end):
        d = 2**layer
        xs = [src[pl.ds(begin + (k - 1) * d, end - begin), :] for k in range(3)]
        centre_rows = xs[1].astype(F32)
        both = jnp.concatenate(xs, axis=1)
        totals = jnp.dot(both, weights[layer], preferred_element_type=F32)
        return (centre_rows + silu(totals + bias_ref[pl.ds(layer, 1), :])).astype(BF)

    first_tile, last_tile = (OFF - 16, OFF + 128), (OFF + TD - 128, OFF + TD + 16)
    tiles = [first_tile] + [(OFF + 128 * i, OFF + 128 * i + 128) for i in range(1, 7)] + [last_tile]

    def put(dst, rows, i):
        begin, end = tiles[i]
        dst[pl.ds(begin, end - begin), :] = rows
        if i == 0:
            dst[pl.ds(OFF - 16, 16), :] = jnp.where(has_left, rows[:16], jnp.zeros_like(rows[:16]))
        if i == 7:
            dst[pl.ds(OFF + TD, 16), :] = jnp.where(
                has_right, rows[128:], jnp.zeros_like(rows[128:])
            )

    own_copy.wait()
    weight_copies[0].wait()
    for i in range(1, 7):
        put(h1, conv(0, h0, *tiles[i]), i)

    @pl.when(has_left)
    def _():
        to_right.wait_recv()

    @pl.when(jnp.logical_not(has_left))
    def _():
        h0[pl.ds(OFF - 16, 16), :] = jnp.zeros((16, C), BF)

    @pl.when(has_right)
    def _():
        to_left.wait_recv()

    @pl.when(jnp.logical_not(has_right))
    def _():
        h0[pl.ds(OFF + TD, 16), :] = jnp.zeros((16, C), BF)

    put(h1, conv(0, h0, *tiles[7]), 7)
    put(h1, conv(0, h0, *tiles[0]), 0)

    y_copies = []

    def send_tile(t):
        lanes = pl.ds(0, 384) if t == 0 else pl.ds(128 + TILE * t, TILE)
        for slot, by in ((1, 1), (2, 3), (3, 2)):
            copy = remote(
                seg.at[0, :, lanes],
                seg.at[slot, :, lanes],
                y_send.at[slot - 1, t],
                y_recv.at[slot - 1, t],
                y_peer(by),
            )
            copy.start()
            y_copies.append(copy)

    def finish(i):
        begin, end = tiles[i]
        end = min(end, OFF + TD)
        rows = conv(2, h2, begin, end)
        points = jnp.dot(rows, proj_ref[...], preferred_element_type=F32).astype(BF)
        if i == 0:
            edge = points[:16].astype(F32)
            edge = jnp.where(has_left, edge, jnp.zeros_like(edge))
            edge = jnp.concatenate([jnp.zeros((112, PATH), F32), edge], axis=0)
            seg[0, :, pl.ds(0, 128)] = edge.T.astype(BF)
            points = points[16:]
        path_ref[pl.ds(128 * i, 128), :] = points
        seg[0, :, pl.ds(128 + 128 * i, 128)] = points.astype(F32).T.astype(BF)
        if i % 2 == 1:
            send_tile(i // 2)

    weight_copies[1].wait()
    put(h2, conv(1, h1, *tiles[0]), 0)
    put(h2, conv(1, h1, *tiles[1]), 1)
    weight_copies[2].wait()
    finish(0)
    for i in range(2, 8):
        put(h2, conv(1, h1, *tiles[i]), i)
        finish(i - 1)
    finish(7)

    own_points = seg[0, :, pl.ds(128, TD)].astype(F32)
    mean = jnp.sum(own_points, axis=1, keepdims=True) * (1.0 / TD)
    centre[...] = jnp.broadcast_to(mean, (PATH, 128))

    def prepare(slot, t):
        window = seg[slot, :, pl.ds(pl.multiple_of(TILE * t, TILE), 384)].astype(F32)
        now, before = window[:, 128:], window[:, 127:383]
        step[...] = now - before
        wide_centre = jnp.concatenate([centre[...]] * 2, axis=1)
        mid[...] = 0.5 * (now + before) - wide_centre

    def step_columns():
        d = step[...]
        high = d.astype(BF)
        low = (d - high.astype(F32)).astype(BF)
        return jnp.concatenate([high, low], axis=0)

    def add_rows(at, row_begin, columns):
        m = mid[...]
        d = step[...] * (1.0 / 12.0)
        rows = []
        for r in range(8):
            m_row = mid[pl.ds(row_begin + r, 1), :]
            d_row = step[pl.ds(row_begin + r, 1), :]
            rows.append((m_row * m + d_row * d).astype(BF))
        acc[pl.ds(at, 512), :] += nt_dot(jnp.concatenate(rows, axis=0), columns)

    def add_level2(columns):
        m = mid[...]
        high = m.astype(BF)
        low = (m - high.astype(F32)).astype(BF)
        ones = jnp.ones((16, TILE), BF)
        acc[pl.ds(1024, 144), :] += nt_dot(jnp.concatenate([high, low, ones], axis=0), columns)

    their_rows = y * 16 + (1 - core) * 8
    my_rows = y * 16 + core * 8
    acc[...] = jnp.zeros_like(acc)

    def wait_tile(slot, t):
        lanes = pl.ds(0, 384) if t == 0 else pl.ds(128 + TILE * t, TILE)
        remote(
            seg.at[0, :, lanes],
            seg.at[slot, :, lanes],
            y_send.at[slot - 1, t],
            y_recv.at[slot - 1, t],
            y_peer(1),
        ).wait_recv()

    def everything(slot, t):
        prepare(slot, t)
        columns = step_columns()
        add_rows(0, their_rows, columns)
        add_level2(columns)
        add_rows(512, my_rows, columns)

    def own_step(t, carry):
        everything(0, t)
        return carry

    lax.fori_loop(0, 4, own_step, 0)
    for t in range(3):
        for slot in range(1, 4):
            wait_tile(slot, t)

        def slot_step(slot, carry, t=t):
            everything(slot, t)
            return carry

        lax.fori_loop(1, 4, slot_step, 0)

    for slot in range(1, 4):
        wait_tile(slot, 3)

    def their_step(slot, carry):
        prepare(slot, 3)
        columns = step_columns()
        add_rows(0, their_rows, columns)
        add_level2(columns)
        return carry

    lax.fori_loop(1, 4, their_step, 0)

    lane = lax.broadcasted_iota(jnp.int32, (32, 128), 1)
    low_half = lane < 64

    def both_halves(v):
        return v + pltpu.roll(v, 64, 1)

    def packed(v):
        return jnp.where(low_half, v[:32], v[32:])

    local2 = both_halves(acc[pl.ds(1024, 64), :] + acc[pl.ds(1088, 64), :])
    delta = both_halves(acc[pl.ds(1152, 8), :])
    middle = centre[...]
    own2 = local2 + middle * delta[:1]
    level2[pl.ds(0, 64), :] = own2

    def third_rows(at, row_begin, dst):
        for r in range(8):
            block = both_halves(acc[pl.ds(at + 64 * r, 64), :])
            c_row = centre[pl.ds(row_begin + r, 1), :]
            s_row = level2[pl.ds(row_begin + r, 1), :]
            dst[pl.ds(32 * r, 32), :] = packed(block + c_row * local2 + middle * s_row)

    third_rows(0, their_rows, partner_out)
    partner_out[pl.ds(256, 32), :] = packed(own2)
    partner_out[pl.ds(288, 8), :] = delta
    swap = remote(partner_out, partner_in, p_send, p_recv, partner)
    swap.start()

    def my_step(slot, carry):
        prepare(slot, 3)
        add_rows(512, my_rows, step_columns())
        return carry

    lax.fori_loop(1, 4, my_step, 0)
    third_rows(512, my_rows, mine)
    mine[pl.ds(256, 32), :] = packed(own2)
    mine[pl.ds(288, 8), :] = delta
    swap.wait_recv()
    mine[...] += partner_in[...]

    def pack(dst, src):
        dst[pl.ds(0, 256), :] = src[pl.ds(0, 256), :].astype(BF)
        exact = src[pl.ds(256, 32), :]
        high = exact.astype(BF)
        dst[pl.ds(256, 32), :] = high
        dst[pl.ds(288, 32), :] = (exact - high.astype(F32)).astype(BF)
        exact = src[pl.ds(288, 8), :]
        high = exact.astype(BF).astype(F32)
        dst[pl.ds(320, 16), :] = jnp.concatenate([high, exact - high], axis=0).astype(BF)

    def unpack(src):
        third = src[pl.ds(0, 256), :].astype(F32)
        second = src[pl.ds(256, 32), :].astype(F32) + src[pl.ds(288, 32), :].astype(F32)
        pair = src[pl.ds(320, 16), :].astype(F32)
        return jnp.concatenate([third, second, pair[:8] + pair[8:]], axis=0)

    pack(out_x, mine)
    x_copies = []
    for by in range(1, 4):
        copy = remote(out_x, in_x.at[by - 1], x_send.at[by - 1], x_recv.at[by - 1], x_peer(by))
        copy.start()
        x_copies.append(copy)
    for copy in x_copies:
        copy.wait_recv()
    swap.wait_send()
    total = mine[...]
    upto = mine[...]
    for by in range(1, 4):
        other = unpack(in_x.at[by - 1])
        total = total + other
        upto = upto + jnp.where(x >= by, other, jnp.zeros_like(other))
    partner_out[...] = total
    mine[...] = upto
    pack(out_z, partner_out)
    z_copies = []
    for by in range(1, 4):
        z_copies.append(
            remote(out_z, in_z.at[by - 1], z_send.at[by - 1], z_recv.at[by - 1], z_peer(by))
        )

    for by in range(1, 4):

        @pl.when(z + by < NZ)
        def _():
            z_copies[by - 1].start()

    for by in range(1, 4):

        @pl.when(z >= by)
        def _():
            z_copies[by - 1].wait_recv()
            mine[...] += unpack(in_z.at[by - 1])

    scale = total_steps ** (-0.2)
    ends = mine[pl.ds(288, 8), :]
    columns = ends.T
    ends_k = jnp.where(
        low_half,
        jnp.broadcast_to(columns[:32, :1], (32, 128)),
        jnp.broadcast_to(columns[32:64, :1], (32, 128)),
    )
    first_ref[...] = ends * scale
    second_ref[...] = mine[pl.ds(256, 32), :] * scale**2
    in_high = n >= 4
    row_of = lax.rem(n, 4) * 8
    for r in range(8):
        row = mine[pl.ds(256 + row_of + r, 1), :]
        turned = pltpu.roll(row, 64, 1)
        low = lane[:1] < 64
        row = jnp.where(jnp.logical_xor(low, in_high), row, turned)
        third_ref[pl.ds(32 * r, 32), :] = (
            row * ends_k - mine[pl.ds(32 * r, 32), :]
        ) * scale**3

    @pl.when(has_left)
    def _():
        to_left.wait_send()

    @pl.when(has_right)
    def _():
        to_right.wait_send()

    for copy in y_copies + x_copies:
        copy.wait_send()
    for by in range(1, 4):

        @pl.when(z + by < NZ)
        def _():
            z_copies[by - 1].wait_send()


def per_device(total_steps, recording, conv_weight, conv_bias, projection):
    vmem = pl.BlockSpec(memory_space=pltpu.VMEM)
    anywhere = pl.BlockSpec(memory_space=pl.ANY)
    path_points, third, second, first = pl.pallas_call(
        functools.partial(kernel, total_steps),
        out_shape=(
            jax.ShapeDtypeStruct((TD, PATH), BF),
            jax.ShapeDtypeStruct((256, 128), F32),
            jax.ShapeDtypeStruct((32, 128), F32),
            jax.ShapeDtypeStruct((8, 128), F32),
        ),
        in_specs=[anywhere, anywhere, vmem, vmem],
        out_specs=(vmem, vmem, vmem, vmem),
        scratch_shapes=[
            pltpu.VMEM((3, 3 * C, C), BF),
            pltpu.VMEM((ROWS, C), BF),
            pltpu.VMEM((ROWS, C), BF),
            pltpu.VMEM((ROWS, C), BF),
            pltpu.VMEM((4, PATH, 128 + TD), BF),
            pltpu.VMEM((PATH, TILE), F32),
            pltpu.VMEM((PATH, TILE), F32),
            pltpu.VMEM((PATH, 128), F32),
            pltpu.VMEM((1168, 128), F32),
            pltpu.VMEM((64, 128), F32),
            pltpu.VMEM((296, 128), F32),
            pltpu.VMEM((296, 128), F32),
            pltpu.VMEM((296, 128), F32),
            pltpu.VMEM((PAY, 128), BF),
            pltpu.VMEM((3, PAY, 128), BF),
            pltpu.VMEM((PAY, 128), BF),
            pltpu.VMEM((3, PAY, 128), BF),
            pltpu.SemaphoreType.DMA((3,)),
            pltpu.SemaphoreType.DMA,
            pltpu.SemaphoreType.DMA((2,)),
            pltpu.SemaphoreType.DMA((2,)),
            pltpu.SemaphoreType.DMA((3, 4)),
            pltpu.SemaphoreType.DMA((3, 4)),
            pltpu.SemaphoreType.DMA,
            pltpu.SemaphoreType.DMA,
            pltpu.SemaphoreType.DMA((3,)),
            pltpu.SemaphoreType.DMA((3,)),
            pltpu.SemaphoreType.DMA((3,)),
            pltpu.SemaphoreType.DMA((3,)),
        ],
        compiler_params=pltpu.CompilerParams(
            collective_id=0, has_side_effects=True, vmem_limit_bytes=48 << 20
        ),
    )(recording, conv_weight.reshape(3, 3 * C, C), conv_bias, projection)
    second = second.reshape(32, 2, PATH).transpose(1, 0, 2).reshape(1, PATH * PATH)
    third = third.reshape(8, 32, 2, PATH).transpose(0, 3, 2, 1).reshape(1, 8, PATH * PATH)
    return path_points, first[:1, :PATH], second, third


def solution(mesh):
    total_steps = TD * mesh.shape["wide"] * mesh.shape["narrow"]
    return jax.shard_map(
        functools.partial(per_device, total_steps),
        mesh=mesh,
        in_specs=(P(("wide", "narrow"), None), P(), P(), P()),
        out_specs=(
            P(("wide", "narrow"), None),
            P("wide", None),
            P("wide", None),
            P("wide", "narrow", None),
        ),
        check_vma=False,
    )
```

```python
import functools

import jax
import jax.numpy as jnp
from jax import lax
from jax.experimental import pallas as pl
from jax.experimental.pallas import tpu as pltpu
from jax.sharding import PartitionSpec as P

C = 512
PATH = 64
TD = 1024
OFF = 32
ROWS = OFF + TD + 32
NX = 4
NZ = 4
NY = 4
TILE = 256
PAY = 256 + 64 + 16
MESH = pl.DeviceIdType.MESH
BF = jnp.bfloat16
F32 = jnp.float32


def silu(v):
    half = 0.5 * v
    return half + half * jnp.tanh(half)


def nt_dot(a, b):
    return lax.dot_general(a, b, (((1,), (1,)), ((), ())), preferred_element_type=F32)


def kernel(
    total_steps,
    rec_hbm,
    weight_hbm,
    bias_hbm,
    proj_hbm,
    path_ref,
    third_ref,
    second_ref,
    first_ref,
    weights,
    bias_ref,
    proj_ref,
    h0,
    h1,
    h2,
    seg,
    mid,
    step,
    centre,
    acc,
    level2,
    mine,
    turned,
    partner_out,
    partner_in,
    out_x,
    in_x,
    out_z,
    in_z,
    w_sem,
    small_sem,
    r_sem,
    halo_send,
    halo_recv,
    y_send,
    y_recv,
    p_send,
    p_recv,
    x_send,
    x_recv,
    z_send,
    z_recv,
):
    w = lax.axis_index("wide")
    n = lax.axis_index("narrow")
    z, x = lax.div(w, NX), lax.rem(w, NX)
    y, core = lax.div(n, 2), lax.rem(n, 2)
    g = w * 8 + n
    last_g = NX * NZ * 8 - 1
    has_left = g > 0
    has_right = g < last_g
    left = (lax.div(g + last_g, 8) % (NX * NZ), lax.rem(g + last_g, 8))
    right = (lax.div(g + 1, 8) % (NX * NZ), lax.rem(g + 1, 8))

    def y_peer(by):
        return (w, lax.rem(y + by, NY) * 2 + core)

    def x_peer(by):
        return (z * NX + lax.rem(x + by, NX), n)

    def z_peer(by):
        return ((z + by) * NX + x, n)

    partner = (w, y * 2 + 1 - core)

    weight_copies = [
        pltpu.make_async_copy(weight_hbm.at[l], weights.at[l], w_sem.at[l]) for l in range(3)
    ]
    own_copy = pltpu.make_async_copy(rec_hbm, h0.at[pl.ds(OFF, TD)], r_sem)
    small_copies = [
        pltpu.make_async_copy(bias_hbm, bias_ref, small_sem.at[0]),
        pltpu.make_async_copy(proj_hbm, proj_ref, small_sem.at[1]),
    ]
    own_copy.start()
    small_copies[0].start()
    for copy in weight_copies:
        copy.start()
    small_copies[1].start()

    barrier = pltpu.get_barrier_semaphore()

    @pl.when(has_left)
    def _():
        pl.semaphore_signal(barrier, inc=1, device_id=left, device_id_type=MESH)

    @pl.when(has_right)
    def _():
        pl.semaphore_signal(barrier, inc=1, device_id=right, device_id_type=MESH)

    for by in range(1, 4):
        pl.semaphore_signal(barrier, inc=1, device_id=y_peer(by), device_id_type=MESH)
        pl.semaphore_signal(barrier, inc=1, device_id=x_peer(by), device_id_type=MESH)

        @pl.when(z >= by)
        def _():
            pl.semaphore_signal(barrier, inc=1, device_id=z_peer(-by), device_id_type=MESH)

    pl.semaphore_signal(barrier, inc=1, device_id=partner, device_id_type=MESH)
    copied_to = has_left.astype(jnp.int32) + has_right.astype(jnp.int32) + 7 + (NZ - 1 - z)
    pl.semaphore_wait(barrier, copied_to)

    def remote(src, dst, send, recv, device):
        return pltpu.make_async_remote_copy(
            src_ref=src,
            dst_ref=dst,
            send_sem=send,
            recv_sem=recv,
            device_id=device,
            device_id_type=MESH,
        )

    to_left = remote(
        rec_hbm.at[pl.ds(0, 16)],
        h0.at[pl.ds(OFF + TD, 16)],
        halo_send.at[0],
        halo_recv.at[0],
        left,
    )
    to_right = remote(
        rec_hbm.at[pl.ds(TD - 16, 16)],
        h0.at[pl.ds(OFF - 16, 16)],
        halo_send.at[1],
        halo_recv.at[1],
        right,
    )

    @pl.when(has_left)
    def _():
        to_left.start()

    @pl.when(has_right)
    def _():
        to_right.start()

    def conv(layer, src, begin, end):
        d = 2**layer
        xs = [src[pl.ds(begin + (k - 1) * d, end - begin), :] for k in range(3)]
        centre_rows = xs[1].astype(F32)
        both = jnp.concatenate(xs, axis=1)
        totals = jnp.dot(both, weights[layer], preferred_element_type=F32)
        return (centre_rows + silu(totals + bias_ref[pl.ds(layer, 1), :])).astype(BF)

    first_tile, last_tile = (OFF - 16, OFF + 128), (OFF + TD - 128, OFF + TD + 16)
    tiles = [first_tile] + [(OFF + 128 * i, OFF + 128 * i + 128) for i in range(1, 7)] + [last_tile]

    def put(dst, rows, i):
        begin, end = tiles[i]
        dst[pl.ds(begin, end - begin), :] = rows
        if i == 0:
            dst[pl.ds(OFF - 16, 16), :] = jnp.where(has_left, rows[:16], jnp.zeros_like(rows[:16]))
        if i == 7:
            dst[pl.ds(OFF + TD, 16), :] = jnp.where(
                has_right, rows[128:], jnp.zeros_like(rows[128:])
            )

    own_copy.wait()
    small_copies[0].wait()
    weight_copies[0].wait()
    for i in range(1, 7):
        put(h1, conv(0, h0, *tiles[i]), i)

    @pl.when(has_left)
    def _():
        to_right.wait_recv()

    @pl.when(jnp.logical_not(has_left))
    def _():
        h0[pl.ds(OFF - 16, 16), :] = jnp.zeros((16, C), BF)

    @pl.when(has_right)
    def _():
        to_left.wait_recv()

    @pl.when(jnp.logical_not(has_right))
    def _():
        h0[pl.ds(OFF + TD, 16), :] = jnp.zeros((16, C), BF)

    put(h1, conv(0, h0, *tiles[7]), 7)
    put(h1, conv(0, h0, *tiles[0]), 0)

    y_copies = []

    def send_tile(t):
        lanes = pl.ds(0, 384) if t == 0 else pl.ds(128 + TILE * t, TILE)
        for slot, by in ((1, 1), (2, 3), (3, 2)):
            copy = remote(
                seg.at[0, :, lanes],
                seg.at[slot, :, lanes],
                y_send.at[slot - 1, t],
                y_recv.at[slot - 1, t],
                y_peer(by),
            )
            copy.start()
            y_copies.append(copy)

    def finish(i):
        begin, end = tiles[i]
        end = min(end, OFF + TD)
        rows = conv(2, h2, begin, end)
        points = nt_dot(proj_ref[...], rows)
        if i == 0:
            edge = jnp.where(has_left, points[:, 15:16], jnp.zeros((PATH, 1), F32))
            seg[0, :, pl.ds(0, 128)] = jnp.broadcast_to(edge, (PATH, 128)).astype(BF)
            points = points[:, 16:]
        points = points.astype(BF)
        path_ref[:, pl.ds(128 * i, 128)] = points
        seg[0, :, pl.ds(128 + 128 * i, 128)] = points
        if i % 2 == 1:
            send_tile(i // 2)

    weight_copies[1].wait()
    put(h2, conv(1, h1, *tiles[0]), 0)
    put(h2, conv(1, h1, *tiles[1]), 1)
    weight_copies[2].wait()
    small_copies[1].wait()
    finish(0)
    for i in range(2, 8):
        put(h2, conv(1, h1, *tiles[i]), i)
        finish(i - 1)
    finish(7)

    own_points = seg[0, :, pl.ds(128, TD)].astype(F32)
    mean = jnp.sum(own_points, axis=1, keepdims=True) * (1.0 / TD)
    centre[...] = jnp.broadcast_to(mean, (PATH, 128))

    def prepare(slot, t, buf):
        window = seg[slot, :, pl.ds(TILE * t, 384)].astype(F32)
        now, before = window[:, 128:], window[:, 127:383]
        step[buf] = now - before
        wide_centre = jnp.concatenate([centre[...]] * 2, axis=1)
        mid[buf] = 0.5 * (now + before) - wide_centre

    def step_columns(buf):
        d = step[buf]
        high = d.astype(BF)
        low = (d - high.astype(F32)).astype(BF)
        return jnp.concatenate([high, low], axis=0)

    def add_rows(at, row_begin, buf, columns):
        m = mid[buf]
        d = step[buf] * (1.0 / 12.0)
        rows = []
        for r in range(8):
            m_row = mid[buf, pl.ds(row_begin + r, 1), :]
            d_row = step[buf, pl.ds(row_begin + r, 1), :]
            rows.append((m_row * m + d_row * d).astype(BF))
        acc[pl.ds(at, 512), :] += nt_dot(jnp.concatenate(rows, axis=0), columns)

    def add_level2(buf, columns):
        m = mid[buf]
        high = m.astype(BF)
        low = (m - high.astype(F32)).astype(BF)
        ones = jnp.ones((16, TILE), BF)
        acc[pl.ds(1024, 144), :] += nt_dot(jnp.concatenate([high, low, ones], axis=0), columns)

    their_rows = y * 16 + (1 - core) * 8
    my_rows = y * 16 + core * 8
    acc[...] = jnp.zeros_like(acc)

    def wait_tile(slot, t):
        lanes = pl.ds(0, 384) if t == 0 else pl.ds(128 + TILE * t, TILE)
        remote(
            seg.at[0, :, lanes],
            seg.at[slot, :, lanes],
            y_send.at[slot - 1, t],
            y_recv.at[slot - 1, t],
            y_peer(1),
        ).wait_recv()

    def everything(steps):
        for at, (slot, t) in enumerate(steps):
            prepare(slot, t, at % 4)
            columns = step_columns(at % 4)
            add_rows(0, their_rows, at % 4, columns)
            add_level2(at % 4, columns)
            add_rows(512, my_rows, at % 4, columns)

    everything([(0, t) for t in range(4)])
    for group in ((0, 1), (2,)):
        for t in group:
            for slot in range(1, 4):
                wait_tile(slot, t)
        everything([(slot, t) for t in group for slot in range(1, 4)])
    for slot in range(1, 4):
        wait_tile(slot, 3)
    for slot in range(1, 4):
        prepare(slot, 3, slot)
        columns = step_columns(slot)
        add_rows(0, their_rows, slot, columns)
        add_level2(slot, columns)

    low_half = lax.broadcasted_iota(jnp.int32, (64, 128), 1) < 64

    def both_halves(v):
        return v + pltpu.roll(v, 64, 1)

    def packed_level2():
        even, odd = level2[pl.ds(0, 32, stride=2), :], level2[pl.ds(1, 32, stride=2), :]
        return jnp.where(low_half[:32], even, odd)

    local2 = both_halves(acc[pl.ds(1024, 64), :] + acc[pl.ds(1088, 64), :])
    delta = both_halves(acc[pl.ds(1152, 8), :])
    middle = centre[...]
    own2 = local2 + middle * delta[:1]
    level2[pl.ds(0, 64), :] = own2

    def third_rows(at, row_begin, dst):
        def block(r):
            rows = both_halves(acc[pl.ds(at + 64 * r, 64), :])
            c_row = centre[pl.ds(row_begin + r, 1), :]
            s_row = level2[pl.ds(row_begin + r, 1), :]
            return rows + c_row * local2 + middle * s_row

        for r in range(4):
            dst[pl.ds(64 * r, 64), :] = jnp.where(low_half, block(r), block(r + 4))

    third_rows(0, their_rows, partner_out)
    partner_out[pl.ds(256, 32), :] = packed_level2()
    partner_out[pl.ds(288, 8), :] = delta
    swap = remote(partner_out, partner_in, p_send, p_recv, partner)
    swap.start()

    for slot in range(1, 4):
        add_rows(512, my_rows, slot, step_columns(slot))
    third_rows(512, my_rows, mine)
    mine[pl.ds(256, 32), :] = packed_level2()
    mine[pl.ds(288, 8), :] = delta
    swap.wait_recv()
    mine[...] += partner_in[...]

    def pack(dst, src):
        dst[pl.ds(0, 256), :] = src[pl.ds(0, 256), :].astype(BF)
        exact = src[pl.ds(256, 32), :]
        high = exact.astype(BF)
        dst[pl.ds(256, 32), :] = high
        dst[pl.ds(288, 32), :] = (exact - high.astype(F32)).astype(BF)
        exact = src[pl.ds(288, 8), :]
        high = exact.astype(BF).astype(F32)
        dst[pl.ds(320, 16), :] = jnp.concatenate([high, exact - high], axis=0).astype(BF)

    def unpack(src):
        third = src[pl.ds(0, 256), :].astype(F32)
        second = src[pl.ds(256, 32), :].astype(F32) + src[pl.ds(288, 32), :].astype(F32)
        pair = src[pl.ds(320, 16), :].astype(F32)
        return jnp.concatenate([third, second, pair[:8] + pair[8:]], axis=0)

    pack(out_x, mine)
    x_copies = []
    for by in range(1, 4):
        copy = remote(out_x, in_x.at[by - 1], x_send.at[by - 1], x_recv.at[by - 1], x_peer(by))
        copy.start()
        x_copies.append(copy)
    for copy in x_copies:
        copy.wait_recv()
    swap.wait_send()
    total = mine[...]
    upto = mine[...]
    for by in range(1, 4):
        other = unpack(in_x.at[by - 1])
        total = total + other
        upto = upto + jnp.where(x >= by, other, jnp.zeros_like(other))
    partner_out[...] = total
    mine[...] = upto
    pack(out_z, partner_out)
    z_copies = []
    for by in range(1, 4):
        z_copies.append(
            remote(out_z, in_z.at[by - 1], z_send.at[by - 1], z_recv.at[by - 1], z_peer(by))
        )

    for by in range(1, 4):

        @pl.when(z + by < NZ)
        def _():
            z_copies[by - 1].start()

    for by in range(1, 4):

        @pl.when(z >= by)
        def _():
            z_copies[by - 1].wait_recv()
            mine[...] += unpack(in_z.at[by - 1])

    scale = total_steps ** (-0.2)
    ends = mine[pl.ds(288, 8), :]
    ends_k = jnp.broadcast_to(ends.T[:64, :1], (64, 128))
    first_ref[...] = ends[:1, :64] * scale
    second_ref[...] = mine[pl.ds(256, 32), :] * scale**2

    def level2_row(r):
        row = mine[pl.ds(256 + 4 * n + r // 2, 1), :]
        other = pltpu.roll(row, 64, 1)
        low = low_half[:1]
        return jnp.where(low, row, other) if r % 2 == 0 else jnp.where(low, other, row)

    for r in range(4):
        row = jnp.where(low_half[:1], level2_row(r), level2_row(r + 4))
        values = ((row * ends_k - mine[pl.ds(64 * r, 64), :]) * scale**3).T
        turned[pl.ds(r, 64, stride=8), :] = values[:64]
        turned[pl.ds(4 + r, 64, stride=8), :] = values[64:]
    for pair in range(32):
        both = [turned[pl.ds(16 * pair + 8 * k, 8), :] for k in range(2)]
        third_ref[:, pl.ds(128 * pair, 128)] = jnp.concatenate(both, axis=1)

    @pl.when(has_left)
    def _():
        to_left.wait_send()

    @pl.when(has_right)
    def _():
        to_right.wait_send()

    for copy in y_copies + x_copies:
        copy.wait_send()
    for by in range(1, 4):

        @pl.when(z + by < NZ)
        def _():
            z_copies[by - 1].wait_send()


def per_device(total_steps, recording, conv_weight, conv_bias, projection):
    vmem = pl.BlockSpec(memory_space=pltpu.VMEM)
    hbm = pl.BlockSpec(memory_space=pltpu.HBM)
    path_points, third, second, first = pl.pallas_call(
        functools.partial(kernel, total_steps),
        out_shape=(
            jax.ShapeDtypeStruct((PATH, TD), BF),
            jax.ShapeDtypeStruct((8, PATH * PATH), F32),
            jax.ShapeDtypeStruct((32, 128), F32),
            jax.ShapeDtypeStruct((1, PATH), F32),
        ),
        in_specs=[hbm, hbm, hbm, hbm],
        out_specs=(vmem, vmem, vmem, vmem),
        scratch_shapes=[
            pltpu.VMEM((3, 3 * C, C), BF),
            pltpu.VMEM((3, C), F32),
            pltpu.VMEM((PATH, C), BF),
            pltpu.VMEM((ROWS, C), BF),
            pltpu.VMEM((ROWS, C), BF),
            pltpu.VMEM((ROWS, C), BF),
            pltpu.VMEM((4, PATH, 128 + TD), BF),
            pltpu.VMEM((4, PATH, TILE), F32),
            pltpu.VMEM((4, PATH, TILE), F32),
            pltpu.VMEM((PATH, 128), F32),
            pltpu.VMEM((1168, 128), F32),
            pltpu.VMEM((64, 128), F32),
            pltpu.VMEM((296, 128), F32),
            pltpu.VMEM((512, PATH), F32),
            pltpu.VMEM((296, 128), F32),
            pltpu.VMEM((296, 128), F32),
            pltpu.VMEM((PAY, 128), BF),
            pltpu.VMEM((3, PAY, 128), BF),
            pltpu.VMEM((PAY, 128), BF),
            pltpu.VMEM((3, PAY, 128), BF),
            pltpu.SemaphoreType.DMA((3,)),
            pltpu.SemaphoreType.DMA((2,)),
            pltpu.SemaphoreType.DMA,
            pltpu.SemaphoreType.DMA((2,)),
            pltpu.SemaphoreType.DMA((2,)),
            pltpu.SemaphoreType.DMA((3, 4)),
            pltpu.SemaphoreType.DMA((3, 4)),
            pltpu.SemaphoreType.DMA,
            pltpu.SemaphoreType.DMA,
            pltpu.SemaphoreType.DMA((3,)),
            pltpu.SemaphoreType.DMA((3,)),
            pltpu.SemaphoreType.DMA((3,)),
            pltpu.SemaphoreType.DMA((3,)),
        ],
        compiler_params=pltpu.CompilerParams(
            collective_id=0, has_side_effects=True, vmem_limit_bytes=67043328
        ),
    )(recording, conv_weight.reshape(3, 3 * C, C), conv_bias, projection.T)
    return path_points.T, first, second.reshape(1, PATH * PATH), third[None]


def solution(mesh):
    total_steps = TD * mesh.shape["wide"] * mesh.shape["narrow"]
    return jax.shard_map(
        functools.partial(per_device, total_steps),
        mesh=mesh,
        in_specs=(P(("wide", "narrow"), None), P(), P(), P()),
        out_specs=(
            P(("wide", "narrow"), None),
            P("wide", None),
            P("wide", None),
            P("wide", "narrow", None),
        ),
        check_vma=False,
    )
```

```python
import functools

import jax
import jax.numpy as jnp
from jax import lax
from jax.experimental import pallas as pl
from jax.experimental.pallas import tpu as pltpu
from jax.sharding import PartitionSpec as P

C = 512
PATH = 64
TD = 1024
OFF = 32
ROWS = OFF + TD + 32
NX = 4
NZ = 4
NY = 4
TILE = 256
PAY = 256 + 64 + 16
MESH = pl.DeviceIdType.MESH
BF = jnp.bfloat16
F32 = jnp.float32


def silu(v):
    half = 0.5 * v
    return half + half * jnp.tanh(half)


def nt_dot(a, b):
    return lax.dot_general(a, b, (((1,), (1,)), ((), ())), preferred_element_type=F32)


def kernel(
    total_steps,
    rec_hbm,
    weight_hbm,
    bias_hbm,
    proj_hbm,
    path_ref,
    third_ref,
    second_ref,
    first_ref,
    weights,
    bias_ref,
    proj_ref,
    h0,
    h1,
    h2,
    seg,
    mid,
    step,
    centre,
    acc,
    level2,
    mine,
    turned,
    partner_out,
    partner_in,
    out_x,
    in_x,
    out_z,
    in_z,
    w_sem,
    small_sem,
    r_sem,
    halo_send,
    halo_recv,
    y_send,
    y_recv,
    p_send,
    p_recv,
    x_send,
    x_recv,
    z_send,
    z_recv,
):
    w = lax.axis_index("wide")
    n = lax.axis_index("narrow")
    z, x = lax.div(w, NX), lax.rem(w, NX)
    y, core = lax.div(n, 2), lax.rem(n, 2)
    g = w * 8 + n
    last_g = NX * NZ * 8 - 1
    has_left = g > 0
    has_right = g < last_g
    left = (lax.div(g + last_g, 8) % (NX * NZ), lax.rem(g + last_g, 8))
    right = (lax.div(g + 1, 8) % (NX * NZ), lax.rem(g + 1, 8))

    def y_peer(by):
        return (w, lax.rem(y + by, NY) * 2 + core)

    def x_peer(by):
        return (z * NX + lax.rem(x + by, NX), n)

    def z_peer(by):
        return ((z + by) * NX + x, n)

    partner = (w, y * 2 + 1 - core)

    weight_copies = [
        pltpu.make_async_copy(weight_hbm.at[l], weights.at[l], w_sem.at[l]) for l in range(3)
    ]
    own_copy = pltpu.make_async_copy(rec_hbm, h0.at[pl.ds(OFF, TD)], r_sem)
    small_copies = [
        pltpu.make_async_copy(bias_hbm, bias_ref, small_sem.at[0]),
        pltpu.make_async_copy(proj_hbm, proj_ref, small_sem.at[1]),
    ]
    own_copy.start()
    small_copies[0].start()
    for copy in weight_copies:
        copy.start()
    small_copies[1].start()

    barrier = pltpu.get_barrier_semaphore()

    @pl.when(has_left)
    def _():
        pl.semaphore_signal(barrier, inc=1, device_id=left, device_id_type=MESH)

    @pl.when(has_right)
    def _():
        pl.semaphore_signal(barrier, inc=1, device_id=right, device_id_type=MESH)

    for by in range(1, 4):
        pl.semaphore_signal(barrier, inc=1, device_id=y_peer(by), device_id_type=MESH)
        pl.semaphore_signal(barrier, inc=1, device_id=x_peer(by), device_id_type=MESH)

        @pl.when(z >= by)
        def _():
            pl.semaphore_signal(barrier, inc=1, device_id=z_peer(-by), device_id_type=MESH)

    pl.semaphore_signal(barrier, inc=1, device_id=partner, device_id_type=MESH)
    copied_to = has_left.astype(jnp.int32) + has_right.astype(jnp.int32) + 7 + (NZ - 1 - z)
    pl.semaphore_wait(barrier, copied_to)

    def remote(src, dst, send, recv, device):
        return pltpu.make_async_remote_copy(
            src_ref=src,
            dst_ref=dst,
            send_sem=send,
            recv_sem=recv,
            device_id=device,
            device_id_type=MESH,
        )

    to_left = remote(
        rec_hbm.at[pl.ds(0, 16)],
        h0.at[pl.ds(OFF + TD, 16)],
        halo_send.at[0],
        halo_recv.at[0],
        left,
    )
    to_right = remote(
        rec_hbm.at[pl.ds(TD - 16, 16)],
        h0.at[pl.ds(OFF - 16, 16)],
        halo_send.at[1],
        halo_recv.at[1],
        right,
    )

    @pl.when(has_left)
    def _():
        to_left.start()

    @pl.when(has_right)
    def _():
        to_right.start()

    def conv(layer, src, begin, end):
        d = 2**layer
        xs = [src[pl.ds(begin + (k - 1) * d, end - begin), :] for k in range(3)]
        centre_rows = xs[1].astype(F32)
        both = jnp.concatenate(xs, axis=1)
        totals = jnp.dot(both, weights[layer], preferred_element_type=F32)
        return (centre_rows + silu(totals + bias_ref[pl.ds(layer, 1), :])).astype(BF)

    first_tile, last_tile = (OFF - 16, OFF + 128), (OFF + TD - 128, OFF + TD + 16)
    tiles = [first_tile] + [(OFF + 128 * i, OFF + 128 * i + 128) for i in range(1, 7)] + [last_tile]

    def put(dst, rows, i):
        begin, end = tiles[i]
        dst[pl.ds(begin, end - begin), :] = rows
        if i == 0:
            dst[pl.ds(OFF - 16, 16), :] = jnp.where(has_left, rows[:16], jnp.zeros_like(rows[:16]))
        if i == 7:
            dst[pl.ds(OFF + TD, 16), :] = jnp.where(
                has_right, rows[128:], jnp.zeros_like(rows[128:])
            )

    own_copy.wait()
    small_copies[0].wait()
    weight_copies[0].wait()
    for i in range(1, 7):
        put(h1, conv(0, h0, *tiles[i]), i)

    @pl.when(has_left)
    def _():
        to_right.wait_recv()

    @pl.when(jnp.logical_not(has_left))
    def _():
        h0[pl.ds(OFF - 16, 16), :] = jnp.zeros((16, C), BF)

    @pl.when(has_right)
    def _():
        to_left.wait_recv()

    @pl.when(jnp.logical_not(has_right))
    def _():
        h0[pl.ds(OFF + TD, 16), :] = jnp.zeros((16, C), BF)

    put(h1, conv(0, h0, *tiles[7]), 7)
    put(h1, conv(0, h0, *tiles[0]), 0)

    y_copies = []

    def send_tile(t):
        lanes = pl.ds(0, 384) if t == 0 else pl.ds(128 + TILE * t, TILE)
        for slot, by in ((1, 1), (2, 3), (3, 2)):
            copy = remote(
                seg.at[0, :, lanes],
                seg.at[slot, :, lanes],
                y_send.at[slot - 1, t],
                y_recv.at[slot - 1, t],
                y_peer(by),
            )
            copy.start()
            y_copies.append(copy)

    def finish(i):
        begin, end = tiles[i]
        end = min(end, OFF + TD)
        rows = conv(2, h2, begin, end)
        points = nt_dot(proj_ref[...], rows)
        if i == 0:
            edge = jnp.where(has_left, points[:, 15:16], jnp.zeros((PATH, 1), F32))
            seg[0, :, pl.ds(0, 128)] = jnp.broadcast_to(edge, (PATH, 128)).astype(BF)
            points = points[:, 16:]
        points = points.astype(BF)
        path_ref[:, pl.ds(128 * i, 128)] = points
        seg[0, :, pl.ds(128 + 128 * i, 128)] = points
        if i % 2 == 1:
            send_tile(i // 2)

    weight_copies[1].wait()
    put(h2, conv(1, h1, *tiles[0]), 0)
    put(h2, conv(1, h1, *tiles[1]), 1)
    weight_copies[2].wait()
    small_copies[1].wait()
    finish(0)
    for i in range(2, 8):
        put(h2, conv(1, h1, *tiles[i]), i)
        finish(i - 1)
    finish(7)

    own_points = seg[0, :, pl.ds(128, TD)].astype(F32)
    mean = jnp.sum(own_points, axis=1, keepdims=True) * (1.0 / TD)
    centre[...] = jnp.broadcast_to(mean, (PATH, 128))

    def prepare(slot, t, buf):
        window = seg[slot, :, pl.ds(TILE * t, 384)].astype(F32)
        now, before = window[:, 128:], window[:, 127:383]
        step[buf] = now - before
        wide_centre = jnp.concatenate([centre[...]] * 2, axis=1)
        mid[buf] = 0.5 * (now + before) - wide_centre

    def step_columns(buf):
        d = step[buf]
        high = d.astype(BF)
        low = (d - high.astype(F32)).astype(BF)
        return jnp.concatenate([high, low], axis=0)

    def add_rows(at, row_begin, buf, columns):
        m = mid[buf]
        d = step[buf] * (1.0 / 12.0)
        rows = []
        for r in range(8):
            m_row = mid[buf, pl.ds(row_begin + r, 1), :]
            d_row = step[buf, pl.ds(row_begin + r, 1), :]
            rows.append((m_row * m + d_row * d).astype(BF))
        acc[pl.ds(at, 512), :] += nt_dot(jnp.concatenate(rows, axis=0), columns)

    def add_level2(buf, columns):
        m = mid[buf]
        high = m.astype(BF)
        low = (m - high.astype(F32)).astype(BF)
        ones = jnp.ones((16, TILE), BF)
        acc[pl.ds(1024, 144), :] += nt_dot(jnp.concatenate([high, low, ones], axis=0), columns)

    their_rows = y * 16 + (1 - core) * 8
    my_rows = y * 16 + core * 8
    acc[...] = jnp.zeros_like(acc)

    def wait_tile(slot, t):
        lanes = pl.ds(0, 384) if t == 0 else pl.ds(128 + TILE * t, TILE)
        remote(
            seg.at[0, :, lanes],
            seg.at[slot, :, lanes],
            y_send.at[slot - 1, t],
            y_recv.at[slot - 1, t],
            y_peer(1),
        ).wait_recv()

    def everything(steps):
        for at, (slot, t) in enumerate(steps):
            prepare(slot, t, at % 4)
            columns = step_columns(at % 4)
            add_rows(0, their_rows, at % 4, columns)
            add_level2(at % 4, columns)
            add_rows(512, my_rows, at % 4, columns)

    everything([(0, t) for t in range(4)])
    for group in ((0, 1), (2,)):
        for t in group:
            for slot in range(1, 4):
                wait_tile(slot, t)
        everything([(slot, t) for t in group for slot in range(1, 4)])
    for slot in range(1, 4):
        wait_tile(slot, 3)
    for slot in range(1, 4):
        prepare(slot, 3, slot)
        columns = step_columns(slot)
        add_rows(0, their_rows, slot, columns)
        add_level2(slot, columns)

    low_half = lax.broadcasted_iota(jnp.int32, (64, 128), 1) < 64

    def both_halves(v):
        return v + pltpu.roll(v, 64, 1)

    def packed_level2():
        even, odd = level2[pl.ds(0, 32, stride=2), :], level2[pl.ds(1, 32, stride=2), :]
        return jnp.where(low_half[:32], even, odd)

    local2 = both_halves(acc[pl.ds(1024, 64), :] + acc[pl.ds(1088, 64), :])
    delta = both_halves(acc[pl.ds(1152, 8), :])
    middle = centre[...]
    own2 = local2 + middle * delta[:1]
    level2[pl.ds(0, 64), :] = own2

    def third_rows(at, row_begin, dst):
        def block(r):
            rows = both_halves(acc[pl.ds(at + 64 * r, 64), :])
            c_row = centre[pl.ds(row_begin + r, 1), :]
            s_row = level2[pl.ds(row_begin + r, 1), :]
            return rows + c_row * local2 + middle * s_row

        for r in range(4):
            dst[pl.ds(64 * r, 64), :] = jnp.where(low_half, block(r), block(r + 4))

    third_rows(0, their_rows, partner_out)
    partner_out[pl.ds(256, 32), :] = packed_level2()
    partner_out[pl.ds(288, 8), :] = delta
    swap = remote(partner_out, partner_in, p_send, p_recv, partner)
    swap.start()

    for slot in range(1, 4):
        add_rows(512, my_rows, slot, step_columns(slot))
    third_rows(512, my_rows, mine)
    mine[pl.ds(256, 32), :] = packed_level2()
    mine[pl.ds(288, 8), :] = delta
    swap.wait_recv()
    mine[...] += partner_in[...]

    def pack(dst, src):
        dst[pl.ds(0, 256), :] = src[pl.ds(0, 256), :].astype(BF)
        exact = src[pl.ds(256, 32), :]
        high = exact.astype(BF)
        dst[pl.ds(256, 32), :] = high
        dst[pl.ds(288, 32), :] = (exact - high.astype(F32)).astype(BF)
        exact = src[pl.ds(288, 8), :]
        high = exact.astype(BF).astype(F32)
        dst[pl.ds(320, 16), :] = jnp.concatenate([high, exact - high], axis=0).astype(BF)

    def unpack(src):
        third = src[pl.ds(0, 256), :].astype(F32)
        second = src[pl.ds(256, 32), :].astype(F32) + src[pl.ds(288, 32), :].astype(F32)
        pair = src[pl.ds(320, 16), :].astype(F32)
        return jnp.concatenate([third, second, pair[:8] + pair[8:]], axis=0)

    pack(out_x, mine)
    x_copies = []
    for by in range(1, 4):
        copy = remote(out_x, in_x.at[by - 1], x_send.at[by - 1], x_recv.at[by - 1], x_peer(by))
        copy.start()
        x_copies.append(copy)
    for copy in x_copies:
        copy.wait_recv()
    swap.wait_send()
    total = mine[...]
    upto = mine[...]
    for by in range(1, 4):
        other = unpack(in_x.at[by - 1])
        total = total + other
        upto = upto + jnp.where(x >= by, other, jnp.zeros_like(other))
    partner_out[...] = total
    mine[...] = upto
    pack(out_z, partner_out)
    z_copies = []
    for by in range(1, 4):
        z_copies.append(
            remote(out_z, in_z.at[by - 1], z_send.at[by - 1], z_recv.at[by - 1], z_peer(by))
        )

    for by in range(1, 4):

        @pl.when(z + by < NZ)
        def _():
            z_copies[by - 1].start()

    for by in range(1, 4):

        @pl.when(z >= by)
        def _():
            z_copies[by - 1].wait_recv()
            mine[...] += unpack(in_z.at[by - 1])

    scale = total_steps ** (-0.2)
    ends = mine[pl.ds(288, 8), :]
    ends_k = jnp.broadcast_to(ends.T[:64, :1], (64, 128))
    first_ref[...] = ends[:1, :64] * scale
    second_ref[...] = mine[pl.ds(256, 32), :] * scale**2

    def level2_row(r):
        row = mine[pl.ds(256 + 4 * n + r // 2, 1), :]
        other = pltpu.roll(row, 64, 1)
        low = low_half[:1]
        return jnp.where(low, row, other) if r % 2 == 0 else jnp.where(low, other, row)

    for r in range(4):
        row = jnp.where(low_half[:1], level2_row(r), level2_row(r + 4))
        values = ((row * ends_k - mine[pl.ds(64 * r, 64), :]) * scale**3).T
        turned[pl.ds(r, 64, stride=8), :] = values[:64]
        turned[pl.ds(4 + r, 64, stride=8), :] = values[64:]
    for pair in range(32):
        both = [turned[pl.ds(16 * pair + 8 * k, 8), :] for k in range(2)]
        third_ref[:, pl.ds(128 * pair, 128)] = jnp.concatenate(both, axis=1)

    @pl.when(has_left)
    def _():
        to_left.wait_send()

    @pl.when(has_right)
    def _():
        to_right.wait_send()

    for copy in y_copies + x_copies:
        copy.wait_send()
    for by in range(1, 4):

        @pl.when(z + by < NZ)
        def _():
            z_copies[by - 1].wait_send()


def per_device(total_steps, recording, conv_weight, conv_bias, projection):
    vmem = pl.BlockSpec(memory_space=pltpu.VMEM)
    hbm = pl.BlockSpec(memory_space=pltpu.HBM)
    operands = (recording, conv_weight.reshape(3, 3 * C, C), conv_bias, projection.T)
    operands = [pltpu.with_memory_space_constraint(a, pltpu.HBM) for a in operands]
    path_points, third, second, first = pl.pallas_call(
        functools.partial(kernel, total_steps),
        out_shape=(
            jax.ShapeDtypeStruct((PATH, TD), BF),
            jax.ShapeDtypeStruct((8, PATH * PATH), F32),
            jax.ShapeDtypeStruct((32, 128), F32),
            jax.ShapeDtypeStruct((1, PATH), F32),
        ),
        in_specs=[hbm, hbm, hbm, hbm],
        out_specs=(vmem, vmem, vmem, vmem),
        scratch_shapes=[
            pltpu.VMEM((3, 3 * C, C), BF),
            pltpu.VMEM((3, C), F32),
            pltpu.VMEM((PATH, C), BF),
            pltpu.VMEM((ROWS, C), BF),
            pltpu.VMEM((ROWS, C), BF),
            pltpu.VMEM((ROWS, C), BF),
            pltpu.VMEM((4, PATH, 128 + TD), BF),
            pltpu.VMEM((4, PATH, TILE), F32),
            pltpu.VMEM((4, PATH, TILE), F32),
            pltpu.VMEM((PATH, 128), F32),
            pltpu.VMEM((1168, 128), F32),
            pltpu.VMEM((64, 128), F32),
            pltpu.VMEM((296, 128), F32),
            pltpu.VMEM((512, PATH), F32),
            pltpu.VMEM((296, 128), F32),
            pltpu.VMEM((296, 128), F32),
            pltpu.VMEM((PAY, 128), BF),
            pltpu.VMEM((3, PAY, 128), BF),
            pltpu.VMEM((PAY, 128), BF),
            pltpu.VMEM((3, PAY, 128), BF),
            pltpu.SemaphoreType.DMA((3,)),
            pltpu.SemaphoreType.DMA((2,)),
            pltpu.SemaphoreType.DMA,
            pltpu.SemaphoreType.DMA((2,)),
            pltpu.SemaphoreType.DMA((2,)),
            pltpu.SemaphoreType.DMA((3, 4)),
            pltpu.SemaphoreType.DMA((3, 4)),
            pltpu.SemaphoreType.DMA,
            pltpu.SemaphoreType.DMA,
            pltpu.SemaphoreType.DMA((3,)),
            pltpu.SemaphoreType.DMA((3,)),
            pltpu.SemaphoreType.DMA((3,)),
            pltpu.SemaphoreType.DMA((3,)),
        ],
        compiler_params=pltpu.CompilerParams(
            collective_id=0, has_side_effects=True, vmem_limit_bytes=48 << 20
        ),
    )(*operands)
    return path_points.T, first, second.reshape(1, PATH * PATH), third[None]


def solution(mesh):
    total_steps = TD * mesh.shape["wide"] * mesh.shape["narrow"]
    return jax.shard_map(
        functools.partial(per_device, total_steps),
        mesh=mesh,
        in_specs=(P(("wide", "narrow"), None), P(), P(), P()),
        out_specs=(
            P(("wide", "narrow"), None),
            P("wide", None),
            P("wide", None),
            P("wide", "narrow", None),
        ),
        check_vma=False,
    )
```

```python
import functools

import jax
import jax.numpy as jnp
from jax import lax
from jax.experimental import pallas as pl
from jax.experimental.pallas import tpu as pltpu
from jax.sharding import PartitionSpec as P

C = 512
PATH = 64
TD = 1024
OFF = 32
ROWS = OFF + TD + 32
NX = 4
NZ = 4
NY = 4
TILE = 256
PART = 128 + 16 + 8
PAY = 128 + 32 + 16
MESH = pl.DeviceIdType.MESH
BF = jnp.bfloat16
F32 = jnp.float32


def silu(v):
    half = 0.5 * v
    return half + half * jnp.tanh(half)


def nt_dot(a, b):
    return lax.dot_general(a, b, (((1,), (1,)), ((), ())), preferred_element_type=F32)


def kernel(
    total_steps,
    rec_hbm,
    weight_hbm,
    bias_hbm,
    proj_hbm,
    path_ref,
    third_ref,
    second_ref,
    first_ref,
    weights,
    bias_ref,
    proj_ref,
    h0,
    h1,
    h2,
    seg,
    mid,
    step,
    centre,
    acc,
    level2,
    mine,
    turned,
    partner_out,
    partner_in,
    out_1,
    out_2,
    out_low,
    in_x,
    in_z,
    w_sem,
    small_sem,
    r_sem,
    halo_send,
    halo_recv,
    y_send,
    y_recv,
    p_send,
    p_recv,
    x_send,
    x_recv,
    z_send,
    z_recv,
    z_ready,
):
    w = lax.axis_index("wide")
    n = lax.axis_index("narrow")
    z, x = lax.div(w, NX), lax.rem(w, NX)
    y, core = lax.div(n, 2), lax.rem(n, 2)
    g = w * 8 + n
    last_g = NX * NZ * 8 - 1
    has_left = g > 0
    has_right = g < last_g
    left = (lax.div(g + last_g, 8) % (NX * NZ), lax.rem(g + last_g, 8))
    right = (lax.div(g + 1, 8) % (NX * NZ), lax.rem(g + 1, 8))

    def y_peer(by):
        return (w, lax.rem(y + by, NY) * 2 + core)

    def x_peer(by):
        return (z * NX + lax.rem(x + by, NX), n)

    def z_peer(by):
        return ((z + by) * NX + x, n)

    partner = (w, y * 2 + 1 - core)

    weight_copies = [
        pltpu.make_async_copy(weight_hbm.at[l], weights.at[l], w_sem.at[l]) for l in range(3)
    ]
    own_copy = pltpu.make_async_copy(rec_hbm, h0.at[pl.ds(OFF, TD)], r_sem)
    small_copies = [
        pltpu.make_async_copy(bias_hbm, bias_ref, small_sem.at[0]),
        pltpu.make_async_copy(proj_hbm, proj_ref, small_sem.at[1]),
    ]
    own_copy.start()
    small_copies[0].start()
    for copy in weight_copies:
        copy.start()
    small_copies[1].start()

    barrier = pltpu.get_barrier_semaphore()

    @pl.when(has_left)
    def _():
        pl.semaphore_signal(barrier, inc=1, device_id=left, device_id_type=MESH)

    @pl.when(has_right)
    def _():
        pl.semaphore_signal(barrier, inc=1, device_id=right, device_id_type=MESH)

    for by in range(1, 4):
        pl.semaphore_signal(barrier, inc=1, device_id=y_peer(by), device_id_type=MESH)
        pl.semaphore_signal(barrier, inc=1, device_id=x_peer(by), device_id_type=MESH)

        @pl.when(z + by < NZ)
        def _():
            pl.semaphore_signal(barrier, inc=1, device_id=z_peer(by), device_id_type=MESH)

    pl.semaphore_signal(barrier, inc=1, device_id=partner, device_id_type=MESH)
    greeted = has_left.astype(jnp.int32) + has_right.astype(jnp.int32) + 7 + z
    pl.semaphore_wait(barrier, greeted)
    for by in range(1, 4):

        @pl.when(z >= by)
        def _():
            pl.semaphore_signal(z_ready, inc=1, device_id=z_peer(-by), device_id_type=MESH)

    def remote(src, dst, send, recv, device):
        return pltpu.make_async_remote_copy(
            src_ref=src,
            dst_ref=dst,
            send_sem=send,
            recv_sem=recv,
            device_id=device,
            device_id_type=MESH,
        )

    to_left = remote(
        rec_hbm.at[pl.ds(0, 16)],
        h0.at[pl.ds(OFF + TD, 16)],
        halo_send.at[0],
        halo_recv.at[0],
        left,
    )
    to_right = remote(
        rec_hbm.at[pl.ds(TD - 16, 16)],
        h0.at[pl.ds(OFF - 16, 16)],
        halo_send.at[1],
        halo_recv.at[1],
        right,
    )

    @pl.when(has_left)
    def _():
        to_left.start()

    @pl.when(has_right)
    def _():
        to_right.start()

    def conv(layer, src, begin, end):
        d = 2**layer
        xs = [src[pl.ds(begin + (k - 1) * d, end - begin), :] for k in range(3)]
        centre_rows = xs[1].astype(F32)
        both = jnp.concatenate(xs, axis=1)
        totals = jnp.dot(both, weights[layer], preferred_element_type=F32)
        return (centre_rows + silu(totals + bias_ref[pl.ds(layer, 1), :])).astype(BF)

    first_tile, last_tile = (OFF - 16, OFF + 128), (OFF + TD - 128, OFF + TD + 16)
    tiles = [first_tile] + [(OFF + 128 * i, OFF + 128 * i + 128) for i in range(1, 7)] + [last_tile]

    def put(dst, rows, i):
        begin, end = tiles[i]
        dst[pl.ds(begin, end - begin), :] = rows
        if i == 0:
            dst[pl.ds(OFF - 16, 16), :] = jnp.where(has_left, rows[:16], jnp.zeros_like(rows[:16]))
        if i == 7:
            dst[pl.ds(OFF + TD, 16), :] = jnp.where(
                has_right, rows[128:], jnp.zeros_like(rows[128:])
            )

    own_copy.wait()
    small_copies[0].wait()
    weight_copies[0].wait()
    for i in range(1, 7):
        put(h1, conv(0, h0, *tiles[i]), i)

    @pl.when(has_left)
    def _():
        to_right.wait_recv()

    @pl.when(jnp.logical_not(has_left))
    def _():
        h0[pl.ds(OFF - 16, 16), :] = jnp.zeros((16, C), BF)

    @pl.when(has_right)
    def _():
        to_left.wait_recv()

    @pl.when(jnp.logical_not(has_right))
    def _():
        h0[pl.ds(OFF + TD, 16), :] = jnp.zeros((16, C), BF)

    put(h1, conv(0, h0, *tiles[7]), 7)
    put(h1, conv(0, h0, *tiles[0]), 0)

    y_copies = []

    def send_tile(t):
        lanes = pl.ds(0, 384) if t == 0 else pl.ds(128 + TILE * t, TILE)
        for slot, by in ((1, 1), (2, 3), (3, 2)):
            copy = remote(
                seg.at[0, :, lanes],
                seg.at[slot, :, lanes],
                y_send.at[slot - 1, t],
                y_recv.at[slot - 1, t],
                y_peer(by),
            )
            copy.start()
            y_copies.append(copy)

    def finish(i):
        begin, end = tiles[i]
        end = min(end, OFF + TD)
        rows = conv(2, h2, begin, end)
        points = nt_dot(proj_ref[...], rows)
        if i == 0:
            edge = jnp.where(has_left, points[:, 15:16], jnp.zeros((PATH, 1), F32))
            seg[0, :, pl.ds(0, 128)] = jnp.broadcast_to(edge, (PATH, 128)).astype(BF)
            points = points[:, 16:]
        points = points.astype(BF)
        path_ref[:, pl.ds(128 * i, 128)] = points
        seg[0, :, pl.ds(128 + 128 * i, 128)] = points
        if i % 2 == 1:
            send_tile(i // 2)

    weight_copies[1].wait()
    put(h2, conv(1, h1, *tiles[0]), 0)
    put(h2, conv(1, h1, *tiles[1]), 1)
    weight_copies[2].wait()
    small_copies[1].wait()
    finish(0)
    for i in range(2, 8):
        put(h2, conv(1, h1, *tiles[i]), i)
        finish(i - 1)
    finish(7)

    own_points = seg[0, :, pl.ds(128, TD)].astype(F32)
    mean = jnp.sum(own_points, axis=1, keepdims=True) * (1.0 / TD)
    centre[...] = jnp.broadcast_to(mean, (PATH, 128))

    def prepare(slot, t, buf):
        window = seg[slot, :, pl.ds(TILE * t, 384)].astype(F32)
        now, before = window[:, 128:], window[:, 127:383]
        step[buf] = now - before
        wide_centre = jnp.concatenate([centre[...]] * 2, axis=1)
        mid[buf] = 0.5 * (now + before) - wide_centre

    def step_columns(buf):
        d = step[buf]
        high = d.astype(BF)
        low = (d - high.astype(F32)).astype(BF)
        return jnp.concatenate([high, low], axis=0)

    def add_rows(at, row_begin, buf, columns):
        m = mid[buf]
        d = step[buf] * (1.0 / 12.0)
        rows = []
        for r in range(8):
            m_row = mid[buf, pl.ds(row_begin + r, 1), :]
            d_row = step[buf, pl.ds(row_begin + r, 1), :]
            rows.append((m_row * m + d_row * d).astype(BF))
        acc[pl.ds(at, 512), :] += nt_dot(jnp.concatenate(rows, axis=0), columns)

    def add_level2(buf, columns):
        m = mid[buf]
        high = m.astype(BF)
        low = (m - high.astype(F32)).astype(BF)
        ones = jnp.ones((16, TILE), BF)
        acc[pl.ds(1024, 144), :] += nt_dot(jnp.concatenate([high, low, ones], axis=0), columns)

    their_rows = y * 16 + (1 - core) * 8
    my_rows = y * 16 + core * 8
    acc[...] = jnp.zeros_like(acc)

    def wait_tile(slot, t):
        lanes = pl.ds(0, 384) if t == 0 else pl.ds(128 + TILE * t, TILE)
        remote(
            seg.at[0, :, lanes],
            seg.at[slot, :, lanes],
            y_send.at[slot - 1, t],
            y_recv.at[slot - 1, t],
            y_peer(1),
        ).wait_recv()

    def everything(steps):
        for at, (slot, t) in enumerate(steps):
            prepare(slot, t, at % 4)
            columns = step_columns(at % 4)
            add_rows(0, their_rows, at % 4, columns)
            add_level2(at % 4, columns)
            add_rows(512, my_rows, at % 4, columns)

    everything([(0, t) for t in range(4)])
    for group in ((0, 1), (2,)):
        for t in group:
            for slot in range(1, 4):
                wait_tile(slot, t)
        everything([(slot, t) for t in group for slot in range(1, 4)])
    for slot in range(1, 4):
        wait_tile(slot, 3)
    for slot in range(1, 4):
        prepare(slot, 3, slot)
        columns = step_columns(slot)
        add_rows(0, their_rows, slot, columns)
        add_level2(slot, columns)

    low_half = lax.broadcasted_iota(jnp.int32, (64, 128), 1) < 64

    def both_halves(v):
        return v + pltpu.roll(v, 64, 1)

    def packed_level2():
        even, odd = level2[pl.ds(0, 32, stride=2), :], level2[pl.ds(1, 32, stride=2), :]
        return jnp.where(low_half[:32], even, odd)

    local2 = both_halves(acc[pl.ds(1024, 64), :] + acc[pl.ds(1088, 64), :])
    delta = both_halves(acc[pl.ds(1152, 8), :])
    middle = centre[...]
    own2 = local2 + middle * delta[:1]
    level2[pl.ds(0, 64), :] = own2

    def third_rows(at, row_begin, dst):
        def block(r):
            rows = both_halves(acc[pl.ds(at + 64 * r, 64), :])
            c_row = centre[pl.ds(row_begin + r, 1), :]
            s_row = level2[pl.ds(row_begin + r, 1), :]
            return rows + c_row * local2 + middle * s_row

        for r in range(4):
            dst[r // 2, pl.ds(64 * (r % 2), 64), :] = jnp.where(low_half, block(r), block(r + 4))

    def low_levels(dst):
        pairs = packed_level2()
        for half in range(2):
            dst[half, pl.ds(128, 16), :] = pairs[16 * half : 16 * half + 16]
            dst[half, pl.ds(144, 8), :] = delta

    third_rows(0, their_rows, partner_out)
    low_levels(partner_out)
    swap = remote(partner_out, partner_in, p_send, p_recv, partner)
    swap.start()

    for slot in range(1, 4):
        add_rows(512, my_rows, slot, step_columns(slot))
    third_rows(512, my_rows, mine)
    low_levels(mine)
    swap.wait_recv()
    mine[...] += partner_in[...]

    def pack(dst, value):
        dst[pl.ds(0, 128), :] = value[:128].astype(BF)
        exact = value[128:144]
        high = exact.astype(BF)
        dst[pl.ds(128, 16), :] = high
        dst[pl.ds(144, 16), :] = (exact - high.astype(F32)).astype(BF)
        exact = value[144:152]
        high = exact.astype(BF).astype(F32)
        dst[pl.ds(160, 16), :] = jnp.concatenate([high, exact - high], axis=0).astype(BF)

    def unpack(src):
        second = src[pl.ds(128, 16), :].astype(F32) + src[pl.ds(144, 16), :].astype(F32)
        pair = src[pl.ds(160, 16), :].astype(F32)
        third = src[pl.ds(0, 128), :].astype(F32)
        return jnp.concatenate([third, second, pair[:8] + pair[8:]], axis=0)

    def x_copy(src, half, by):
        at = 3 * half + by - 1
        return remote(src, in_x.at[at], x_send.at[at], x_recv.at[at], x_peer(by))

    def z_copy(src, half, by):
        at = 3 * half + by - 1
        return remote(src, in_z.at[at], z_send.at[at], z_recv.at[at], z_peer(by))

    def up_z(src, half):
        for by in range(1, 4):

            @pl.when(z + by < NZ)
            def _():
                z_copy(src, half, by).start()

    def add_lower_z(dst, half):
        for by in range(1, 4):

            @pl.when(z >= by)
            def _():
                z_copy(out_2, half, by).wait_recv()
                dst[...] += unpack(in_z.at[3 * half + by - 1])

    pack(out_1.at[0], mine[0])
    pack(out_1.at[1], mine[1])
    for by in range(1, 4):
        x_copy(out_1.at[0], 0, by).start()
    @pl.when(z < NZ - 1)
    def _():
        pl.semaphore_wait(z_ready, NZ - 1 - z)

    up_z(out_1.at[1], 1)
    swap.wait_send()

    below = partner_out.at[1]
    below[...] = jnp.zeros((PART, 128), F32)
    add_lower_z(below, 1)
    pack(out_low, below[...])
    mine[1] += below[...]
    pack(out_2.at[1], mine[1])
    for by in range(1, 4):

        @pl.when(x + by < NX)
        def _():
            x_copy(out_2.at[1], 1, by).start()

        @pl.when(x + by >= NX)
        def _():
            x_copy(out_low, 1, by).start()

    total = upto = mine[0]
    for by in range(1, 4):
        x_copy(out_1.at[0], 0, by).wait_recv()
        other = unpack(in_x.at[by - 1])
        total = total + other
        upto = upto + jnp.where(x >= by, other, jnp.zeros_like(other))
    pack(out_2.at[0], total)
    up_z(out_2.at[0], 0)
    mine[0] = upto

    for by in range(1, 4):
        x_copy(out_low, 1, by).wait_recv()
        mine[1] += unpack(in_x.at[3 + by - 1])
    add_lower_z(mine.at[0], 0)

    scale = total_steps ** (-0.2)
    ends = mine[0, pl.ds(144, 8), :]
    ends_k = jnp.broadcast_to(ends.T[:64, :1], (64, 128))
    first_ref[...] = ends[:1, :64] * scale
    for half in range(2):
        second_ref[pl.ds(16 * half, 16), :] = mine[half, pl.ds(128, 16), :] * scale**2

    def level2_row(r):
        row = mine[lax.div(n, 4), pl.ds(128 + 4 * lax.rem(n, 4) + r // 2, 1), :]
        other = pltpu.roll(row, 64, 1)
        low = low_half[:1]
        return jnp.where(low, row, other) if r % 2 == 0 else jnp.where(low, other, row)

    for r in range(4):
        row = jnp.where(low_half[:1], level2_row(r), level2_row(r + 4))
        values = ((row * ends_k - mine[r // 2, pl.ds(64 * (r % 2), 64), :]) * scale**3).T
        turned[pl.ds(r, 64, stride=8), :] = values[:64]
        turned[pl.ds(4 + r, 64, stride=8), :] = values[64:]
    for pair in range(32):
        both = [turned[pl.ds(16 * pair + 8 * k, 8), :] for k in range(2)]
        third_ref[:, pl.ds(128 * pair, 128)] = jnp.concatenate(both, axis=1)

    @pl.when(has_left)
    def _():
        to_left.wait_send()

    @pl.when(has_right)
    def _():
        to_right.wait_send()

    for copy in y_copies:
        copy.wait_send()
    for by in range(1, 4):
        for half in range(2):
            x_copy(out_low, half, by).wait_send()

            @pl.when(z + by < NZ)
            def _():
                z_copy(out_low, half, by).wait_send()


def emit(*refs):
    copies = [
        pltpu.make_async_copy(src, dst, refs[8].at[k])
        for k, (src, dst) in enumerate(zip(refs[:4], refs[4:8]))
    ]
    for copy in copies:
        copy.start()
    for copy in copies:
        copy.wait()


def per_device(total_steps, recording, conv_weight, conv_bias, projection):
    vmem = pl.BlockSpec(memory_space=pltpu.VMEM)
    hbm = pl.BlockSpec(memory_space=pltpu.HBM)
    operands = (recording, conv_weight.reshape(3, 3 * C, C), conv_bias, projection.T)
    operands = [pltpu.with_memory_space_constraint(a, pltpu.HBM) for a in operands]
    out_shape = (
        jax.ShapeDtypeStruct((PATH, TD), BF),
        jax.ShapeDtypeStruct((8, PATH * PATH), F32),
        jax.ShapeDtypeStruct((32, 128), F32),
        jax.ShapeDtypeStruct((1, PATH), F32),
    )
    results = pl.pallas_call(
        functools.partial(kernel, total_steps),
        out_shape=out_shape,
        in_specs=[hbm, hbm, hbm, hbm],
        out_specs=(vmem, vmem, vmem, vmem),
        scratch_shapes=[
            pltpu.VMEM((3, 3 * C, C), BF),
            pltpu.VMEM((3, C), F32),
            pltpu.VMEM((PATH, C), BF),
            pltpu.VMEM((ROWS, C), BF),
            pltpu.VMEM((ROWS, C), BF),
            pltpu.VMEM((ROWS, C), BF),
            pltpu.VMEM((4, PATH, 128 + TD), BF),
            pltpu.VMEM((4, PATH, TILE), F32),
            pltpu.VMEM((4, PATH, TILE), F32),
            pltpu.VMEM((PATH, 128), F32),
            pltpu.VMEM((1168, 128), F32),
            pltpu.VMEM((64, 128), F32),
            pltpu.VMEM((2, PART, 128), F32),
            pltpu.VMEM((512, PATH), F32),
            pltpu.VMEM((2, PART, 128), F32),
            pltpu.VMEM((2, PART, 128), F32),
            pltpu.VMEM((2, PAY, 128), BF),
            pltpu.VMEM((2, PAY, 128), BF),
            pltpu.VMEM((PAY, 128), BF),
            pltpu.VMEM((6, PAY, 128), BF),
            pltpu.VMEM((6, PAY, 128), BF),
            pltpu.SemaphoreType.DMA((3,)),
            pltpu.SemaphoreType.DMA((2,)),
            pltpu.SemaphoreType.DMA,
            pltpu.SemaphoreType.DMA((2,)),
            pltpu.SemaphoreType.DMA((2,)),
            pltpu.SemaphoreType.DMA((3, 4)),
            pltpu.SemaphoreType.DMA((3, 4)),
            pltpu.SemaphoreType.DMA,
            pltpu.SemaphoreType.DMA,
            pltpu.SemaphoreType.DMA((6,)),
            pltpu.SemaphoreType.DMA((6,)),
            pltpu.SemaphoreType.DMA((6,)),
            pltpu.SemaphoreType.DMA((6,)),
            pltpu.SemaphoreType.REGULAR,
        ],
        compiler_params=pltpu.CompilerParams(
            collective_id=0, has_side_effects=True, vmem_limit_bytes=48 << 20
        ),
    )(*operands)
    path_points, third, second, first = pl.pallas_call(
        emit,
        out_shape=out_shape,
        in_specs=[vmem] * 4,
        out_specs=[hbm] * 4,
        scratch_shapes=[pltpu.SemaphoreType.DMA((4,))],
        compiler_params=pltpu.CompilerParams(vmem_limit_bytes=1 << 20),
    )(*results)
    return path_points.T, first, second.reshape(1, PATH * PATH), third[None]


def solution(mesh):
    total_steps = TD * mesh.shape["wide"] * mesh.shape["narrow"]
    return jax.shard_map(
        functools.partial(per_device, total_steps),
        mesh=mesh,
        in_specs=(P(("wide", "narrow"), None), P(), P(), P()),
        out_specs=(
            P(("wide", "narrow"), None),
            P("wide", None),
            P("wide", None),
            P("wide", "narrow", None),
        ),
        check_vma=False,
    )
```

```python
import functools

import jax
import jax.numpy as jnp
from jax import lax
from jax.experimental import pallas as pl
from jax.experimental.pallas import tpu as pltpu
from jax.sharding import PartitionSpec as P

C = 512
PATH = 64
TD = 1024
OFF = 32
ROWS = OFF + TD + 32
NX = 4
NZ = 4
NY = 4
TILE = 256
PART = 128 + 16 + 8
PAY = 128 + 32 + 16
MESH = pl.DeviceIdType.MESH
BF = jnp.bfloat16
F32 = jnp.float32


def silu(v):
    half = 0.5 * v
    return half + half * jnp.tanh(half)


def nt_dot(a, b):
    return lax.dot_general(a, b, (((1,), (1,)), ((), ())), preferred_element_type=F32)


def kernel(
    total_steps,
    rec_hbm,
    weight_hbm,
    bias_hbm,
    proj_hbm,
    path_ref,
    third_ref,
    second_ref,
    first_ref,
    weights,
    bias_ref,
    proj_ref,
    h0,
    h1,
    h2,
    seg,
    mid,
    step,
    centre,
    acc,
    level2,
    mine,
    turned,
    partner_out,
    partner_in,
    out_1,
    out_2,
    out_low,
    in_x,
    in_z,
    w_sem,
    small_sem,
    r_sem,
    halo_send,
    halo_recv,
    y_send,
    y_recv,
    p_send,
    p_recv,
    x_send,
    x_recv,
    z_send,
    z_recv,
    z_ready,
):
    w = lax.axis_index("wide")
    n = lax.axis_index("narrow")
    z, x = lax.div(w, NX), lax.rem(w, NX)
    y, core = lax.div(n, 2), lax.rem(n, 2)
    g = w * 8 + n
    last_g = NX * NZ * 8 - 1
    has_left = g > 0
    has_right = g < last_g
    left = (lax.div(g + last_g, 8) % (NX * NZ), lax.rem(g + last_g, 8))
    right = (lax.div(g + 1, 8) % (NX * NZ), lax.rem(g + 1, 8))

    def y_peer(by):
        return (w, lax.rem(y + by, NY) * 2 + core)

    def x_peer(by):
        return (z * NX + lax.rem(x + by, NX), n)

    def z_peer(by):
        return ((z + by) * NX + x, n)

    partner = (w, y * 2 + 1 - core)

    weight_copies = [
        pltpu.make_async_copy(weight_hbm.at[l], weights.at[l], w_sem.at[l]) for l in range(3)
    ]
    own_copy = pltpu.make_async_copy(rec_hbm, h0.at[pl.ds(OFF, TD)], r_sem)
    small_copies = [
        pltpu.make_async_copy(bias_hbm, bias_ref, small_sem.at[0]),
        pltpu.make_async_copy(proj_hbm, proj_ref, small_sem.at[1]),
    ]
    own_copy.start()
    small_copies[0].start()
    weight_copies[0].start()

    barrier = pltpu.get_barrier_semaphore()

    @pl.when(has_left)
    def _():
        pl.semaphore_signal(barrier, inc=1, device_id=left, device_id_type=MESH)

    @pl.when(has_right)
    def _():
        pl.semaphore_signal(barrier, inc=1, device_id=right, device_id_type=MESH)

    for by in range(1, 4):
        pl.semaphore_signal(barrier, inc=1, device_id=y_peer(by), device_id_type=MESH)
        pl.semaphore_signal(barrier, inc=1, device_id=x_peer(by), device_id_type=MESH)

        @pl.when(z + by < NZ)
        def _():
            pl.semaphore_signal(barrier, inc=1, device_id=z_peer(by), device_id_type=MESH)

    pl.semaphore_signal(barrier, inc=1, device_id=partner, device_id_type=MESH)
    greeted = has_left.astype(jnp.int32) + has_right.astype(jnp.int32) + 7 + z
    pl.semaphore_wait(barrier, greeted)
    for by in range(1, 4):

        @pl.when(z >= by)
        def _():
            pl.semaphore_signal(z_ready, inc=1, device_id=z_peer(-by), device_id_type=MESH)

    def remote(src, dst, send, recv, device):
        return pltpu.make_async_remote_copy(
            src_ref=src,
            dst_ref=dst,
            send_sem=send,
            recv_sem=recv,
            device_id=device,
            device_id_type=MESH,
        )

    to_left = remote(
        rec_hbm.at[pl.ds(0, 16)],
        h0.at[pl.ds(OFF + TD, 16)],
        halo_send.at[0],
        halo_recv.at[0],
        left,
    )
    to_right = remote(
        rec_hbm.at[pl.ds(TD - 16, 16)],
        h0.at[pl.ds(OFF - 16, 16)],
        halo_send.at[1],
        halo_recv.at[1],
        right,
    )

    @pl.when(has_left)
    def _():
        to_left.start()

    @pl.when(has_right)
    def _():
        to_right.start()

    def conv(layer, src, begin, end):
        d = 2**layer
        xs = [src[pl.ds(begin + (k - 1) * d, end - begin), :] for k in range(3)]
        centre_rows = xs[1].astype(F32)
        both = jnp.concatenate(xs, axis=1)
        totals = jnp.dot(both, weights[layer], preferred_element_type=F32)
        return (centre_rows + silu(totals + bias_ref[pl.ds(layer, 1), :])).astype(BF)

    first_tile, last_tile = (OFF - 16, OFF + 128), (OFF + TD - 128, OFF + TD + 16)
    tiles = [first_tile] + [(OFF + 128 * i, OFF + 128 * i + 128) for i in range(1, 7)] + [last_tile]

    def put(dst, rows, i):
        begin, end = tiles[i]
        dst[pl.ds(begin, end - begin), :] = rows
        if i == 0:
            dst[pl.ds(OFF - 16, 16), :] = jnp.where(has_left, rows[:16], jnp.zeros_like(rows[:16]))
        if i == 7:
            dst[pl.ds(OFF + TD, 16), :] = jnp.where(
                has_right, rows[128:], jnp.zeros_like(rows[128:])
            )

    own_copy.wait()
    small_copies[0].wait()
    weight_copies[0].wait()
    weight_copies[1].start()
    small_copies[1].start()
    weight_copies[2].start()
    for i in range(1, 7):
        put(h1, conv(0, h0, *tiles[i]), i)

    @pl.when(has_left)
    def _():
        to_right.wait_recv()

    @pl.when(jnp.logical_not(has_left))
    def _():
        h0[pl.ds(OFF - 16, 16), :] = jnp.zeros((16, C), BF)

    @pl.when(has_right)
    def _():
        to_left.wait_recv()

    @pl.when(jnp.logical_not(has_right))
    def _():
        h0[pl.ds(OFF + TD, 16), :] = jnp.zeros((16, C), BF)

    put(h1, conv(0, h0, *tiles[7]), 7)
    put(h1, conv(0, h0, *tiles[0]), 0)

    y_copies = []

    def send_tile(t):
        lanes = pl.ds(0, 384) if t == 0 else pl.ds(128 + TILE * t, TILE)
        for slot, by in ((1, 1), (2, 3), (3, 2)):
            copy = remote(
                seg.at[0, :, lanes],
                seg.at[slot, :, lanes],
                y_send.at[slot - 1, t],
                y_recv.at[slot - 1, t],
                y_peer(by),
            )
            copy.start()
            y_copies.append(copy)

    def finish(i):
        begin, end = tiles[i]
        end = min(end, OFF + TD)
        rows = conv(2, h2, begin, end)
        points = nt_dot(proj_ref[...], rows)
        if i == 0:
            edge = jnp.where(has_left, points[:, 15:16], jnp.zeros((PATH, 1), F32))
            seg[0, :, pl.ds(0, 128)] = jnp.broadcast_to(edge, (PATH, 128)).astype(BF)
            points = points[:, 16:]
        points = points.astype(BF)
        path_ref[:, pl.ds(128 * i, 128)] = points
        seg[0, :, pl.ds(128 + 128 * i, 128)] = points
        if i % 2 == 1:
            send_tile(i // 2)

    weight_copies[1].wait()
    put(h2, conv(1, h1, *tiles[0]), 0)
    put(h2, conv(1, h1, *tiles[1]), 1)
    put(h2, conv(1, h1, *tiles[2]), 2)
    weight_copies[2].wait()
    small_copies[1].wait()
    for i in range(3, 8):
        put(h2, conv(1, h1, *tiles[i]), i)
        finish(i - 3)
    finish(5)
    known = seg[0, :, pl.ds(128, 640)].astype(F32)
    mean = jnp.sum(known, axis=1, keepdims=True) * (1.0 / 640)
    centre[...] = jnp.broadcast_to(mean, (PATH, 128))
    finish(6)
    finish(7)

    def prepare(slot, t, buf):
        window = seg[slot, :, pl.ds(TILE * t, 384)].astype(F32)
        now, before = window[:, 128:], window[:, 127:383]
        step[buf] = now - before
        wide_centre = jnp.concatenate([centre[...]] * 2, axis=1)
        mid[buf] = 0.5 * (now + before) - wide_centre

    def step_columns(buf):
        d = step[buf]
        high = d.astype(BF)
        low = (d - high.astype(F32)).astype(BF)
        return jnp.concatenate([high, low], axis=0)

    def add_rows(at, row_begin, buf, columns):
        m = mid[buf].astype(BF)
        d = (step[buf] * (1.0 / 12.0)).astype(BF)

        def spread(ref, r):
            row = jnp.broadcast_to(ref[buf, pl.ds(row_begin + r, 1), :], (16, TILE)).astype(BF)
            return jnp.concatenate([row] * 4, axis=0)

        rows = [spread(mid, r) * m + spread(step, r) * d for r in range(8)]
        acc[pl.ds(at, 512), :] += nt_dot(jnp.concatenate(rows, axis=0), columns)

    def add_level2(buf, columns):
        m = mid[buf]
        high = m.astype(BF)
        low = (m - high.astype(F32)).astype(BF)
        ones = jnp.ones((16, TILE), BF)
        acc[pl.ds(1024, 144), :] += nt_dot(jnp.concatenate([high, low, ones], axis=0), columns)

    their_rows = y * 16 + (1 - core) * 8
    my_rows = y * 16 + core * 8
    acc[...] = jnp.zeros_like(acc)

    def wait_tile(slot, t):
        lanes = pl.ds(0, 384) if t == 0 else pl.ds(128 + TILE * t, TILE)
        remote(
            seg.at[0, :, lanes],
            seg.at[slot, :, lanes],
            y_send.at[slot - 1, t],
            y_recv.at[slot - 1, t],
            y_peer(1),
        ).wait_recv()

    def everything(steps):
        for at, (slot, t) in enumerate(steps):
            prepare(slot, t, at % 4)
            columns = step_columns(at % 4)
            add_rows(0, their_rows, at % 4, columns)
            add_level2(at % 4, columns)
            add_rows(512, my_rows, at % 4, columns)

    steps = [(0, t) for t in range(4)]
    for group in ((0, 1), (2,)):
        for t in group:
            for slot in range(1, 4):
                wait_tile(slot, t)
        everything(steps + [(slot, t) for t in group for slot in range(1, 4)])
        steps = []
    for slot in range(1, 4):
        wait_tile(slot, 3)
    for slot in range(1, 4):
        prepare(slot, 3, slot)
        columns = step_columns(slot)
        add_rows(0, their_rows, slot, columns)
        add_level2(slot, columns)

    low_half = lax.broadcasted_iota(jnp.int32, (64, 128), 1) < 64

    def both_halves(v):
        return v + pltpu.roll(v, 64, 1)

    def packed_level2():
        even, odd = level2[pl.ds(0, 32, stride=2), :], level2[pl.ds(1, 32, stride=2), :]
        return jnp.where(low_half[:32], even, odd)

    local2 = both_halves(acc[pl.ds(1024, 64), :] + acc[pl.ds(1088, 64), :])
    delta = both_halves(acc[pl.ds(1152, 8), :])
    middle = centre[...]
    own2 = local2 + middle * delta[:1]
    level2[pl.ds(0, 64), :] = own2

    def third_rows(at, row_begin, dst):
        def block(r):
            rows = both_halves(acc[pl.ds(at + 64 * r, 64), :])
            c_row = centre[pl.ds(row_begin + r, 1), :]
            s_row = level2[pl.ds(row_begin + r, 1), :]
            return rows + c_row * local2 + middle * s_row

        for r in range(4):
            dst[r // 2, pl.ds(64 * (r % 2), 64), :] = jnp.where(low_half, block(r), block(r + 4))

    def low_levels(dst):
        pairs = packed_level2()
        for half in range(2):
            dst[half, pl.ds(128, 16), :] = pairs[16 * half : 16 * half + 16]
            dst[half, pl.ds(144, 8), :] = delta

    third_rows(0, their_rows, partner_out)
    low_levels(partner_out)
    swap = remote(partner_out, partner_in, p_send, p_recv, partner)
    swap.start()

    for slot in range(1, 4):
        add_rows(512, my_rows, slot, step_columns(slot))
    third_rows(512, my_rows, mine)
    low_levels(mine)
    swap.wait_recv()
    mine[...] += partner_in[...]

    def pack(dst, value):
        dst[pl.ds(0, 128), :] = value[:128].astype(BF)
        exact = value[128:144]
        high = exact.astype(BF)
        dst[pl.ds(128, 16), :] = high
        dst[pl.ds(144, 16), :] = (exact - high.astype(F32)).astype(BF)
        exact = value[144:152]
        high = exact.astype(BF).astype(F32)
        dst[pl.ds(160, 16), :] = jnp.concatenate([high, exact - high], axis=0).astype(BF)

    def unpack(src):
        second = src[pl.ds(128, 16), :].astype(F32) + src[pl.ds(144, 16), :].astype(F32)
        pair = src[pl.ds(160, 16), :].astype(F32)
        third = src[pl.ds(0, 128), :].astype(F32)
        return jnp.concatenate([third, second, pair[:8] + pair[8:]], axis=0)

    def x_copy(src, half, by):
        at = 3 * half + by - 1
        return remote(src, in_x.at[at], x_send.at[at], x_recv.at[at], x_peer(by))

    def z_copy(src, half, by):
        at = 3 * half + by - 1
        return remote(src, in_z.at[at], z_send.at[at], z_recv.at[at], z_peer(by))

    def up_z(src, half):
        for by in range(1, 4):

            @pl.when(z + by < NZ)
            def _():
                z_copy(src, half, by).start()

    def add_lower_z(dst, half):
        for by in range(1, 4):

            @pl.when(z >= by)
            def _():
                z_copy(out_2, half, by).wait_recv()
                dst[...] += unpack(in_z.at[3 * half + by - 1])

    pack(out_1.at[0], mine[0])
    pack(out_1.at[1], mine[1])
    for by in range(1, 4):
        x_copy(out_1.at[0], 0, by).start()
    @pl.when(z < NZ - 1)
    def _():
        pl.semaphore_wait(z_ready, NZ - 1 - z)

    up_z(out_1.at[1], 1)
    swap.wait_send()

    below = partner_out.at[1]
    below[...] = jnp.zeros((PART, 128), F32)
    add_lower_z(below, 1)
    pack(out_low, below[...])
    mine[1] += below[...]
    pack(out_2.at[1], mine[1])
    for by in range(1, 4):

        @pl.when(x + by < NX)
        def _():
            x_copy(out_2.at[1], 1, by).start()

        @pl.when(x + by >= NX)
        def _():
            x_copy(out_low, 1, by).start()

    total = upto = mine[0]
    for by in range(1, 4):
        x_copy(out_1.at[0], 0, by).wait_recv()
        other = unpack(in_x.at[by - 1])
        total = total + other
        upto = upto + jnp.where(x >= by, other, jnp.zeros_like(other))
    pack(out_2.at[0], total)
    up_z(out_2.at[0], 0)
    mine[0] = upto

    for by in range(1, 4):
        x_copy(out_low, 1, by).wait_recv()
        mine[1] += unpack(in_x.at[3 + by - 1])
    add_lower_z(mine.at[0], 0)

    scale = total_steps ** (-0.2)
    ends = mine[0, pl.ds(144, 8), :]
    ends_k = jnp.broadcast_to(ends.T[:64, :1], (64, 128))
    first_ref[...] = ends[:1, :64] * scale
    for half in range(2):
        second_ref[pl.ds(16 * half, 16), :] = mine[half, pl.ds(128, 16), :] * scale**2

    def level2_row(r):
        row = mine[lax.div(n, 4), pl.ds(128 + 4 * lax.rem(n, 4) + r // 2, 1), :]
        other = pltpu.roll(row, 64, 1)
        low = low_half[:1]
        return jnp.where(low, row, other) if r % 2 == 0 else jnp.where(low, other, row)

    for r in range(4):
        row = jnp.where(low_half[:1], level2_row(r), level2_row(r + 4))
        values = ((row * ends_k - mine[r // 2, pl.ds(64 * (r % 2), 64), :]) * scale**3).T
        turned[pl.ds(r, 64, stride=8), :] = values[:64]
        turned[pl.ds(4 + r, 64, stride=8), :] = values[64:]
    for pair in range(32):
        both = [turned[pl.ds(16 * pair + 8 * k, 8), :] for k in range(2)]
        third_ref[:, pl.ds(128 * pair, 128)] = jnp.concatenate(both, axis=1)

    @pl.when(has_left)
    def _():
        to_left.wait_send()

    @pl.when(has_right)
    def _():
        to_right.wait_send()

    for copy in y_copies:
        copy.wait_send()
    for by in range(1, 4):
        for half in range(2):
            x_copy(out_low, half, by).wait_send()

            @pl.when(z + by < NZ)
            def _():
                z_copy(out_low, half, by).wait_send()


def emit(*refs):
    copies = [
        pltpu.make_async_copy(src, dst, refs[8].at[k])
        for k, (src, dst) in enumerate(zip(refs[:4], refs[4:8]))
    ]
    for copy in copies:
        copy.start()
    for copy in copies:
        copy.wait()


def per_device(total_steps, recording, conv_weight, conv_bias, projection):
    vmem = pl.BlockSpec(memory_space=pltpu.VMEM)
    hbm = pl.BlockSpec(memory_space=pltpu.HBM)
    operands = (recording, conv_weight.reshape(3, 3 * C, C), conv_bias, projection.T)
    operands = [pltpu.with_memory_space_constraint(a, pltpu.HBM) for a in operands]
    out_shape = (
        jax.ShapeDtypeStruct((PATH, TD), BF),
        jax.ShapeDtypeStruct((8, PATH * PATH), F32),
        jax.ShapeDtypeStruct((32, 128), F32),
        jax.ShapeDtypeStruct((1, PATH), F32),
    )
    results = pl.pallas_call(
        functools.partial(kernel, total_steps),
        out_shape=out_shape,
        in_specs=[hbm, hbm, hbm, hbm],
        out_specs=(vmem, vmem, vmem, vmem),
        scratch_shapes=[
            pltpu.VMEM((3, 3 * C, C), BF),
            pltpu.VMEM((3, C), F32),
            pltpu.VMEM((PATH, C), BF),
            pltpu.VMEM((ROWS, C), BF),
            pltpu.VMEM((ROWS, C), BF),
            pltpu.VMEM((ROWS, C), BF),
            pltpu.VMEM((4, PATH, 128 + TD), BF),
            pltpu.VMEM((4, PATH, TILE), F32),
            pltpu.VMEM((4, PATH, TILE), F32),
            pltpu.VMEM((PATH, 128), F32),
            pltpu.VMEM((1168, 128), F32),
            pltpu.VMEM((64, 128), F32),
            pltpu.VMEM((2, PART, 128), F32),
            pltpu.VMEM((512, PATH), F32),
            pltpu.VMEM((2, PART, 128), F32),
            pltpu.VMEM((2, PART, 128), F32),
            pltpu.VMEM((2, PAY, 128), BF),
            pltpu.VMEM((2, PAY, 128), BF),
            pltpu.VMEM((PAY, 128), BF),
            pltpu.VMEM((6, PAY, 128), BF),
            pltpu.VMEM((6, PAY, 128), BF),
            pltpu.SemaphoreType.DMA((3,)),
            pltpu.SemaphoreType.DMA((2,)),
            pltpu.SemaphoreType.DMA,
            pltpu.SemaphoreType.DMA((2,)),
            pltpu.SemaphoreType.DMA((2,)),
            pltpu.SemaphoreType.DMA((3, 4)),
            pltpu.SemaphoreType.DMA((3, 4)),
            pltpu.SemaphoreType.DMA,
            pltpu.SemaphoreType.DMA,
            pltpu.SemaphoreType.DMA((6,)),
            pltpu.SemaphoreType.DMA((6,)),
            pltpu.SemaphoreType.DMA((6,)),
            pltpu.SemaphoreType.DMA((6,)),
            pltpu.SemaphoreType.REGULAR,
        ],
        compiler_params=pltpu.CompilerParams(
            collective_id=0, has_side_effects=True, vmem_limit_bytes=48 << 20
        ),
    )(*operands)
    path_points, third, second, first = pl.pallas_call(
        emit,
        out_shape=out_shape,
        in_specs=[vmem] * 4,
        out_specs=[hbm] * 4,
        scratch_shapes=[pltpu.SemaphoreType.DMA((4,))],
        compiler_params=pltpu.CompilerParams(vmem_limit_bytes=1 << 20),
    )(*results)
    return path_points.T, first, second.reshape(1, PATH * PATH), third[None]


def solution(mesh):
    total_steps = TD * mesh.shape["wide"] * mesh.shape["narrow"]
    return jax.shard_map(
        functools.partial(per_device, total_steps),
        mesh=mesh,
        in_specs=(P(("wide", "narrow"), None), P(), P(), P()),
        out_specs=(
            P(("wide", "narrow"), None),
            P("wide", None),
            P("wide", None),
            P("wide", "narrow", None),
        ),
        check_vma=False,
    )
```

```python
import functools

import jax
import jax.numpy as jnp
from jax import lax
from jax.experimental import pallas as pl
from jax.experimental.pallas import tpu as pltpu
from jax.sharding import PartitionSpec as P

C = 512
PATH = 64
TD = 1024
OFF = 32
ROWS = OFF + TD + 32
NX = 4
NZ = 4
NY = 4
TILE = 256
PART = 128 + 16 + 8
PAY = 128 + 32 + 16
MESH = pl.DeviceIdType.MESH
BF = jnp.bfloat16
F32 = jnp.float32


def silu(v):
    half = 0.5 * v
    return half + half * jnp.tanh(half)


def nt_dot(a, b):
    return lax.dot_general(a, b, (((1,), (1,)), ((), ())), preferred_element_type=F32)


def kernel(
    total_steps,
    rec_hbm,
    weight_hbm,
    bias_hbm,
    proj_hbm,
    path_ref,
    third_ref,
    second_ref,
    first_ref,
    weights,
    bias_ref,
    proj_ref,
    h0,
    h1,
    h2,
    seg,
    mid,
    step,
    centre,
    acc,
    level2,
    mine,
    turned,
    partner_out,
    partner_in,
    out_1,
    out_2,
    out_low,
    in_x,
    in_z,
    w_sem,
    small_sem,
    r_sem,
    halo_send,
    halo_recv,
    y_send,
    y_recv,
    p_send,
    p_recv,
    x_send,
    x_recv,
    z_send,
    z_recv,
    z_ready,
):
    w = lax.axis_index("wide")
    n = lax.axis_index("narrow")
    z, x = lax.div(w, NX), lax.rem(w, NX)
    y, core = lax.div(n, 2), lax.rem(n, 2)
    g = w * 8 + n
    last_g = NX * NZ * 8 - 1
    has_left = g > 0
    has_right = g < last_g
    left = (lax.div(g + last_g, 8) % (NX * NZ), lax.rem(g + last_g, 8))
    right = (lax.div(g + 1, 8) % (NX * NZ), lax.rem(g + 1, 8))

    def y_peer(by):
        return (w, lax.rem(y + by, NY) * 2 + core)

    def x_peer(by):
        return (z * NX + lax.rem(x + by, NX), n)

    def z_peer(by):
        return ((z + by) * NX + x, n)

    partner = (w, y * 2 + 1 - core)

    weight_copies = [
        pltpu.make_async_copy(weight_hbm.at[l], weights.at[l], w_sem.at[l]) for l in range(3)
    ]
    own_copy = pltpu.make_async_copy(rec_hbm, h0.at[pl.ds(OFF, TD)], r_sem)
    small_copies = [
        pltpu.make_async_copy(bias_hbm, bias_ref, small_sem.at[0]),
        pltpu.make_async_copy(proj_hbm, proj_ref, small_sem.at[1]),
    ]
    own_copy.start()
    small_copies[0].start()
    weight_copies[0].start()

    barrier = pltpu.get_barrier_semaphore()

    @pl.when(has_left)
    def _():
        pl.semaphore_signal(barrier, inc=1, device_id=left, device_id_type=MESH)

    @pl.when(has_right)
    def _():
        pl.semaphore_signal(barrier, inc=1, device_id=right, device_id_type=MESH)

    for by in range(1, 4):
        if by != 2:
            pl.semaphore_signal(barrier, inc=1, device_id=y_peer(by), device_id_type=MESH)
        pl.semaphore_signal(barrier, inc=1, device_id=x_peer(by), device_id_type=MESH)

        @pl.when(z + by < NZ)
        def _():
            pl.semaphore_signal(barrier, inc=1, device_id=z_peer(by), device_id_type=MESH)

    pl.semaphore_signal(barrier, inc=1, device_id=partner, device_id_type=MESH)
    greeted = has_left.astype(jnp.int32) + has_right.astype(jnp.int32) + 6 + z
    pl.semaphore_wait(barrier, greeted)
    for by in range(1, 4):

        @pl.when(z >= by)
        def _():
            pl.semaphore_signal(z_ready, inc=1, device_id=z_peer(-by), device_id_type=MESH)

    def remote(src, dst, send, recv, device):
        return pltpu.make_async_remote_copy(
            src_ref=src,
            dst_ref=dst,
            send_sem=send,
            recv_sem=recv,
            device_id=device,
            device_id_type=MESH,
        )

    to_left = remote(
        rec_hbm.at[pl.ds(0, 16)],
        h0.at[pl.ds(OFF + TD, 16)],
        halo_send.at[0],
        halo_recv.at[0],
        left,
    )
    to_right = remote(
        rec_hbm.at[pl.ds(TD - 16, 16)],
        h0.at[pl.ds(OFF - 16, 16)],
        halo_send.at[1],
        halo_recv.at[1],
        right,
    )

    @pl.when(has_left)
    def _():
        to_left.start()

    @pl.when(has_right)
    def _():
        to_right.start()

    def conv(layer, src, begin, end):
        d = 2**layer
        xs = [src[pl.ds(begin + (k - 1) * d, end - begin), :] for k in range(3)]
        centre_rows = xs[1].astype(F32)
        both = jnp.concatenate(xs, axis=1)
        totals = jnp.dot(both, weights[layer], preferred_element_type=F32)
        return (centre_rows + silu(totals + bias_ref[pl.ds(layer, 1), :])).astype(BF)

    first_tile, last_tile = (OFF - 16, OFF + 128), (OFF + TD - 128, OFF + TD + 16)
    tiles = [first_tile] + [(OFF + 128 * i, OFF + 128 * i + 128) for i in range(1, 7)] + [last_tile]

    def put(dst, rows, i):
        begin, end = tiles[i]
        dst[pl.ds(begin, end - begin), :] = rows
        if i == 0:
            dst[pl.ds(OFF - 16, 16), :] = jnp.where(has_left, rows[:16], jnp.zeros_like(rows[:16]))
        if i == 7:
            dst[pl.ds(OFF + TD, 16), :] = jnp.where(
                has_right, rows[128:], jnp.zeros_like(rows[128:])
            )

    own_copy.wait()
    small_copies[0].wait()
    weight_copies[0].wait()
    weight_copies[1].start()
    small_copies[1].start()
    weight_copies[2].start()
    for i in range(1, 7):
        put(h1, conv(0, h0, *tiles[i]), i)

    @pl.when(has_left)
    def _():
        to_right.wait_recv()

    @pl.when(jnp.logical_not(has_left))
    def _():
        h0[pl.ds(OFF - 16, 16), :] = jnp.zeros((16, C), BF)

    @pl.when(has_right)
    def _():
        to_left.wait_recv()

    @pl.when(jnp.logical_not(has_right))
    def _():
        h0[pl.ds(OFF + TD, 16), :] = jnp.zeros((16, C), BF)

    put(h1, conv(0, h0, *tiles[7]), 7)
    put(h1, conv(0, h0, *tiles[0]), 0)

    y_copies = []

    def tile_copy(way, t):
        begin, end = (0, 384) if t == 0 else (128 + TILE * t, 128 + TILE * (t + 1))
        half = end - 128
        lanes = [(begin, end), (begin, end), (begin, half), (half, end)][way]
        lanes = pl.ds(lanes[0], lanes[1] - lanes[0])
        return remote(
            seg.at[(0, 0, 1, 2)[way], :, lanes],
            seg.at[(1, 2, 3, 3)[way], :, lanes],
            y_send.at[way, t],
            y_recv.at[way, t],
            y_peer((1, 3, 1, 3)[way]),
        )

    def send(way, t):
        copy = tile_copy(way, t)
        copy.start()
        y_copies.append(copy)

    def send_tile(t):
        send(0, t)
        send(1, t)

    def relay(t):
        for way in (0, 1):
            tile_copy(way, t).wait_recv()
            send(way + 2, t)

    def finish(i):
        begin, end = tiles[i]
        end = min(end, OFF + TD)
        rows = conv(2, h2, begin, end)
        points = nt_dot(proj_ref[...], rows)
        if i == 0:
            edge = jnp.where(has_left, points[:, 15:16], jnp.zeros((PATH, 1), F32))
            seg[0, :, pl.ds(0, 128)] = jnp.broadcast_to(edge, (PATH, 128)).astype(BF)
            points = points[:, 16:]
        points = points.astype(BF)
        path_ref[:, pl.ds(128 * i, 128)] = points
        seg[0, :, pl.ds(128 + 128 * i, 128)] = points
        if i % 2 == 1:
            send_tile(i // 2)
            if i > 1:
                relay(i // 2 - 1)

    weight_copies[1].wait()
    put(h2, conv(1, h1, *tiles[0]), 0)
    put(h2, conv(1, h1, *tiles[1]), 1)
    weight_copies[2].wait()
    small_copies[1].wait()
    for i in range(2, 8):
        put(h2, conv(1, h1, *tiles[i]), i)
        finish(i - 2)
    known = seg[0, :, pl.ds(128, 640)].astype(F32)
    mean = jnp.sum(known, axis=1, keepdims=True) * (1.0 / 640)
    centre[...] = jnp.broadcast_to(mean, (PATH, 128))
    finish(6)
    finish(7)

    def prepare(slot, t, buf):
        window = seg[slot, :, pl.ds(TILE * t, 384)].astype(F32)
        now, before = window[:, 128:], window[:, 127:383]
        step[buf] = now - before
        wide_centre = jnp.concatenate([centre[...]] * 2, axis=1)
        mid[buf] = 0.5 * (now + before) - wide_centre

    def step_columns(buf):
        d = step[buf]
        high = d.astype(BF)
        low = (d - high.astype(F32)).astype(BF)
        return jnp.concatenate([high, low], axis=0)

    def add_rows(at, row_begin, buf, columns):
        m = mid[buf].astype(BF)
        d = (step[buf] * (1.0 / 12.0)).astype(BF)

        def spread(ref, r):
            row = jnp.broadcast_to(ref[buf, pl.ds(row_begin + r, 1), :], (16, TILE)).astype(BF)
            return jnp.concatenate([row] * 4, axis=0)

        rows = [spread(mid, r) * m + spread(step, r) * d for r in range(8)]
        acc[pl.ds(at, 512), :] += nt_dot(jnp.concatenate(rows, axis=0), columns)

    def add_level2(buf, columns):
        m = mid[buf]
        high = m.astype(BF)
        low = (m - high.astype(F32)).astype(BF)
        ones = jnp.ones((16, TILE), BF)
        acc[pl.ds(1024, 144), :] += nt_dot(jnp.concatenate([high, low, ones], axis=0), columns)

    their_rows = y * 16 + (1 - core) * 8
    my_rows = y * 16 + core * 8
    acc[...] = jnp.zeros_like(acc)

    def wait_relayed(t):
        tile_copy(2, t).wait_recv()
        tile_copy(3, t).wait_recv()

    def everything(steps):
        for at, (slot, t) in enumerate(steps):
            prepare(slot, t, at % 4)
            columns = step_columns(at % 4)
            add_rows(0, their_rows, at % 4, columns)
            add_level2(at % 4, columns)
            add_rows(512, my_rows, at % 4, columns)

    wait_relayed(0)
    everything([(0, t) for t in range(4)] + [(slot, 0) for slot in range(1, 4)] + [(1, 1)])
    relay(3)
    wait_relayed(1)
    wait_relayed(2)
    everything([(2, 1), (3, 1), (1, 2), (2, 2), (3, 2)])

    def their_step(slot):
        prepare(slot, 3, slot)
        columns = step_columns(slot)
        add_rows(0, their_rows, slot, columns)
        add_level2(slot, columns)

    their_step(1)
    their_step(2)
    wait_relayed(3)
    their_step(3)

    low_half = lax.broadcasted_iota(jnp.int32, (64, 128), 1) < 64

    def both_halves(v):
        return v + pltpu.roll(v, 64, 1)

    def packed_level2():
        even, odd = level2[pl.ds(0, 32, stride=2), :], level2[pl.ds(1, 32, stride=2), :]
        return jnp.where(low_half[:32], even, odd)

    local2 = both_halves(acc[pl.ds(1024, 64), :] + acc[pl.ds(1088, 64), :])
    delta = both_halves(acc[pl.ds(1152, 8), :])
    middle = centre[...]
    own2 = local2 + middle * delta[:1]
    level2[pl.ds(0, 64), :] = own2

    def third_rows(at, row_begin, dst):
        def block(r):
            rows = both_halves(acc[pl.ds(at + 64 * r, 64), :])
            c_row = centre[pl.ds(row_begin + r, 1), :]
            s_row = level2[pl.ds(row_begin + r, 1), :]
            return rows + c_row * local2 + middle * s_row

        for r in range(4):
            dst[r // 2, pl.ds(64 * (r % 2), 64), :] = jnp.where(low_half, block(r), block(r + 4))

    def low_levels(dst):
        pairs = packed_level2()
        for half in range(2):
            dst[half, pl.ds(128, 16), :] = pairs[16 * half : 16 * half + 16]
            dst[half, pl.ds(144, 8), :] = delta

    third_rows(0, their_rows, partner_out)
    low_levels(partner_out)
    swap = remote(partner_out, partner_in, p_send, p_recv, partner)
    swap.start()

    for slot in range(1, 4):
        add_rows(512, my_rows, slot, step_columns(slot))
    third_rows(512, my_rows, mine)
    low_levels(mine)
    swap.wait_recv()
    mine[...] += partner_in[...]

    def pack(dst, value):
        dst[pl.ds(0, 128), :] = value[:128].astype(BF)
        exact = value[128:144]
        high = exact.astype(BF)
        dst[pl.ds(128, 16), :] = high
        dst[pl.ds(144, 16), :] = (exact - high.astype(F32)).astype(BF)
        exact = value[144:152]
        high = exact.astype(BF).astype(F32)
        dst[pl.ds(160, 16), :] = jnp.concatenate([high, exact - high], axis=0).astype(BF)

    def unpack(src):
        second = src[pl.ds(128, 16), :].astype(F32) + src[pl.ds(144, 16), :].astype(F32)
        pair = src[pl.ds(160, 16), :].astype(F32)
        third = src[pl.ds(0, 128), :].astype(F32)
        return jnp.concatenate([third, second, pair[:8] + pair[8:]], axis=0)

    def x_copy(src, half, by):
        at = 3 * half + by - 1
        return remote(src, in_x.at[at], x_send.at[at], x_recv.at[at], x_peer(by))

    def z_copy(src, half, by):
        at = 3 * half + by - 1
        return remote(src, in_z.at[at], z_send.at[at], z_recv.at[at], z_peer(by))

    def up_z(src, half):
        for by in range(1, 4):

            @pl.when(z + by < NZ)
            def _():
                z_copy(src, half, by).start()

    def add_lower_z(dst, half):
        for by in range(1, 4):

            @pl.when(z >= by)
            def _():
                z_copy(out_2, half, by).wait_recv()
                dst[...] += unpack(in_z.at[3 * half + by - 1])

    pack(out_1.at[0], mine[0])
    pack(out_1.at[1], mine[1])
    for by in range(1, 4):
        x_copy(out_1.at[0], 0, by).start()
    @pl.when(z < NZ - 1)
    def _():
        pl.semaphore_wait(z_ready, NZ - 1 - z)

    up_z(out_1.at[1], 1)
    swap.wait_send()

    below = partner_out.at[1]
    below[...] = jnp.zeros((PART, 128), F32)
    add_lower_z(below, 1)
    pack(out_low, below[...])
    mine[1] += below[...]
    pack(out_2.at[1], mine[1])
    for by in range(1, 4):

        @pl.when(x + by < NX)
        def _():
            x_copy(out_2.at[1], 1, by).start()

        @pl.when(x + by >= NX)
        def _():
            x_copy(out_low, 1, by).start()

    total = upto = mine[0]
    for by in range(1, 4):
        x_copy(out_1.at[0], 0, by).wait_recv()
        other = unpack(in_x.at[by - 1])
        total = total + other
        upto = upto + jnp.where(x >= by, other, jnp.zeros_like(other))
    pack(out_2.at[0], total)
    up_z(out_2.at[0], 0)
    mine[0] = upto

    for by in range(1, 4):
        x_copy(out_low, 1, by).wait_recv()
        mine[1] += unpack(in_x.at[3 + by - 1])
    add_lower_z(mine.at[0], 0)

    scale = total_steps ** (-0.2)
    ends = mine[0, pl.ds(144, 8), :]
    ends_k = jnp.broadcast_to(ends.T[:64, :1], (64, 128))
    first_ref[...] = ends[:1, :64] * scale
    for half in range(2):
        second_ref[pl.ds(16 * half, 16), :] = mine[half, pl.ds(128, 16), :] * scale**2

    def level2_row(r):
        row = mine[lax.div(n, 4), pl.ds(128 + 4 * lax.rem(n, 4) + r // 2, 1), :]
        other = pltpu.roll(row, 64, 1)
        low = low_half[:1]
        return jnp.where(low, row, other) if r % 2 == 0 else jnp.where(low, other, row)

    for r in range(4):
        row = jnp.where(low_half[:1], level2_row(r), level2_row(r + 4))
        values = ((row * ends_k - mine[r // 2, pl.ds(64 * (r % 2), 64), :]) * scale**3).T
        turned[pl.ds(r, 64, stride=8), :] = values[:64]
        turned[pl.ds(4 + r, 64, stride=8), :] = values[64:]
    for pair in range(32):
        both = [turned[pl.ds(16 * pair + 8 * k, 8), :] for k in range(2)]
        third_ref[:, pl.ds(128 * pair, 128)] = jnp.concatenate(both, axis=1)

    @pl.when(has_left)
    def _():
        to_left.wait_send()

    @pl.when(has_right)
    def _():
        to_right.wait_send()

    for copy in y_copies:
        copy.wait_send()
    for by in range(1, 4):
        for half in range(2):
            x_copy(out_low, half, by).wait_send()

            @pl.when(z + by < NZ)
            def _():
                z_copy(out_low, half, by).wait_send()


def emit(*refs):
    copies = [
        pltpu.make_async_copy(src, dst, refs[8].at[k])
        for k, (src, dst) in enumerate(zip(refs[:4], refs[4:8]))
    ]
    for copy in copies:
        copy.start()
    for copy in copies:
        copy.wait()


def per_device(total_steps, recording, conv_weight, conv_bias, projection):
    vmem = pl.BlockSpec(memory_space=pltpu.VMEM)
    hbm = pl.BlockSpec(memory_space=pltpu.HBM)
    operands = (recording, conv_weight.reshape(3, 3 * C, C), conv_bias, projection.T)
    operands = [pltpu.with_memory_space_constraint(a, pltpu.HBM) for a in operands]
    out_shape = (
        jax.ShapeDtypeStruct((PATH, TD), BF),
        jax.ShapeDtypeStruct((8, PATH * PATH), F32),
        jax.ShapeDtypeStruct((32, 128), F32),
        jax.ShapeDtypeStruct((1, PATH), F32),
    )
    results = pl.pallas_call(
        functools.partial(kernel, total_steps),
        out_shape=out_shape,
        in_specs=[hbm, hbm, hbm, hbm],
        out_specs=(vmem, vmem, vmem, vmem),
        scratch_shapes=[
            pltpu.VMEM((3, 3 * C, C), BF),
            pltpu.VMEM((3, C), F32),
            pltpu.VMEM((PATH, C), BF),
            pltpu.VMEM((ROWS, C), BF),
            pltpu.VMEM((ROWS, C), BF),
            pltpu.VMEM((ROWS, C), BF),
            pltpu.VMEM((4, PATH, 128 + TD), BF),
            pltpu.VMEM((4, PATH, TILE), F32),
            pltpu.VMEM((4, PATH, TILE), F32),
            pltpu.VMEM((PATH, 128), F32),
            pltpu.VMEM((1168, 128), F32),
            pltpu.VMEM((64, 128), F32),
            pltpu.VMEM((2, PART, 128), F32),
            pltpu.VMEM((512, PATH), F32),
            pltpu.VMEM((2, PART, 128), F32),
            pltpu.VMEM((2, PART, 128), F32),
            pltpu.VMEM((2, PAY, 128), BF),
            pltpu.VMEM((2, PAY, 128), BF),
            pltpu.VMEM((PAY, 128), BF),
            pltpu.VMEM((6, PAY, 128), BF),
            pltpu.VMEM((6, PAY, 128), BF),
            pltpu.SemaphoreType.DMA((3,)),
            pltpu.SemaphoreType.DMA((2,)),
            pltpu.SemaphoreType.DMA,
            pltpu.SemaphoreType.DMA((2,)),
            pltpu.SemaphoreType.DMA((2,)),
            pltpu.SemaphoreType.DMA((4, 4)),
            pltpu.SemaphoreType.DMA((4, 4)),
            pltpu.SemaphoreType.DMA,
            pltpu.SemaphoreType.DMA,
            pltpu.SemaphoreType.DMA((6,)),
            pltpu.SemaphoreType.DMA((6,)),
            pltpu.SemaphoreType.DMA((6,)),
            pltpu.SemaphoreType.DMA((6,)),
            pltpu.SemaphoreType.REGULAR,
        ],
        compiler_params=pltpu.CompilerParams(
            collective_id=0, has_side_effects=True, vmem_limit_bytes=48 << 20
        ),
    )(*operands)
    path_points, third, second, first = pl.pallas_call(
        emit,
        out_shape=out_shape,
        in_specs=[vmem] * 4,
        out_specs=[hbm] * 4,
        scratch_shapes=[pltpu.SemaphoreType.DMA((4,))],
        compiler_params=pltpu.CompilerParams(vmem_limit_bytes=1 << 20),
    )(*results)
    return path_points.T, first, second.reshape(1, PATH * PATH), third[None]


def solution(mesh):
    total_steps = TD * mesh.shape["wide"] * mesh.shape["narrow"]
    return jax.shard_map(
        functools.partial(per_device, total_steps),
        mesh=mesh,
        in_specs=(P(("wide", "narrow"), None), P(), P(), P()),
        out_specs=(
            P(("wide", "narrow"), None),
            P("wide", None),
            P("wide", None),
            P("wide", "narrow", None),
        ),
        check_vma=False,
    )
```

```python
import functools

import jax
import jax.numpy as jnp
from jax import lax
from jax.experimental import pallas as pl
from jax.experimental.pallas import tpu as pltpu
from jax.sharding import PartitionSpec as P

C = 512
PATH = 64
TD = 1024
OFF = 32
ROWS = OFF + TD + 32
NX = 4
NZ = 4
NY = 4
TILE = 256
PART = 128 + 16 + 8
PAY = 128 + 32 + 16
MESH = pl.DeviceIdType.MESH
BF = jnp.bfloat16
F32 = jnp.float32


def silu(v):
    half = 0.5 * v
    return half + half * jnp.tanh(half)


def nt_dot(a, b):
    return lax.dot_general(a, b, (((1,), (1,)), ((), ())), preferred_element_type=F32)


def kernel(
    total_steps,
    rec_hbm,
    weight_hbm,
    bias_hbm,
    proj_hbm,
    path_ref,
    third_ref,
    second_ref,
    first_ref,
    weights,
    bias_ref,
    proj_ref,
    h0,
    h1,
    h2,
    seg,
    mid,
    step,
    centre,
    acc,
    level2,
    mine,
    turned,
    partner_out,
    partner_in,
    out_1,
    out_2,
    out_low,
    in_x,
    in_z,
    w_sem,
    small_sem,
    r_sem,
    halo_send,
    halo_recv,
    y_send,
    y_recv,
    p_send,
    p_recv,
    x_send,
    x_recv,
    z_send,
    z_recv,
    z_ready,
):
    w = lax.axis_index("wide")
    n = lax.axis_index("narrow")
    z, x = lax.div(w, NX), lax.rem(w, NX)
    y, core = lax.div(n, 2), lax.rem(n, 2)
    g = w * 8 + n
    last_g = NX * NZ * 8 - 1
    has_left = g > 0
    has_right = g < last_g
    left = (lax.div(g + last_g, 8) % (NX * NZ), lax.rem(g + last_g, 8))
    right = (lax.div(g + 1, 8) % (NX * NZ), lax.rem(g + 1, 8))

    def y_peer(by):
        return (w, lax.rem(y + by, NY) * 2 + core)

    def x_peer(by):
        return (z * NX + lax.rem(x + by, NX), n)

    def z_peer(by):
        return ((z + by) * NX + x, n)

    partner = (w, y * 2 + 1 - core)

    weight_copies = [
        pltpu.make_async_copy(weight_hbm.at[l], weights.at[l], w_sem.at[l]) for l in range(3)
    ]
    own_copy = pltpu.make_async_copy(rec_hbm, h0.at[pl.ds(OFF, TD)], r_sem)
    small_copies = [
        pltpu.make_async_copy(bias_hbm, bias_ref, small_sem.at[0]),
        pltpu.make_async_copy(proj_hbm, proj_ref, small_sem.at[1]),
    ]
    own_copy.start()
    small_copies[0].start()
    weight_copies[0].start()

    barrier = pltpu.get_barrier_semaphore()

    @pl.when(has_left)
    def _():
        pl.semaphore_signal(barrier, inc=1, device_id=left, device_id_type=MESH)

    @pl.when(has_right)
    def _():
        pl.semaphore_signal(barrier, inc=1, device_id=right, device_id_type=MESH)

    for by in range(1, 4):
        if by != 2:
            pl.semaphore_signal(barrier, inc=1, device_id=y_peer(by), device_id_type=MESH)
        pl.semaphore_signal(barrier, inc=1, device_id=x_peer(by), device_id_type=MESH)

        @pl.when(z + by < NZ)
        def _():
            pl.semaphore_signal(barrier, inc=1, device_id=z_peer(by), device_id_type=MESH)

    pl.semaphore_signal(barrier, inc=1, device_id=partner, device_id_type=MESH)
    greeted = has_left.astype(jnp.int32) + has_right.astype(jnp.int32) + 6 + z
    pl.semaphore_wait(barrier, greeted)
    for by in range(1, 4):

        @pl.when(z >= by)
        def _():
            pl.semaphore_signal(z_ready, inc=1, device_id=z_peer(-by), device_id_type=MESH)

    def remote(src, dst, send, recv, device):
        return pltpu.make_async_remote_copy(
            src_ref=src,
            dst_ref=dst,
            send_sem=send,
            recv_sem=recv,
            device_id=device,
            device_id_type=MESH,
        )

    to_left = remote(
        rec_hbm.at[pl.ds(0, 16)],
        h0.at[pl.ds(OFF + TD, 16)],
        halo_send.at[0],
        halo_recv.at[0],
        left,
    )
    to_right = remote(
        rec_hbm.at[pl.ds(TD - 16, 16)],
        h0.at[pl.ds(OFF - 16, 16)],
        halo_send.at[1],
        halo_recv.at[1],
        right,
    )

    @pl.when(has_left)
    def _():
        to_left.start()

    @pl.when(has_right)
    def _():
        to_right.start()

    def conv(layer, src, begin, end):
        d = 2**layer
        xs = [src[pl.ds(begin + (k - 1) * d, end - begin), :] for k in range(3)]
        centre_rows = xs[1].astype(F32)
        both = jnp.concatenate(xs, axis=1)
        totals = jnp.dot(both, weights[layer], preferred_element_type=F32)
        return (centre_rows + silu(totals + bias_ref[pl.ds(layer, 1), :])).astype(BF)

    first_tile, last_tile = (OFF - 16, OFF + 128), (OFF + TD - 128, OFF + TD + 16)
    tiles = [first_tile] + [(OFF + 128 * i, OFF + 128 * i + 128) for i in range(1, 7)] + [last_tile]

    def put(dst, rows, i):
        begin, end = tiles[i]
        dst[pl.ds(begin, end - begin), :] = rows
        if i == 0:
            dst[pl.ds(OFF - 16, 16), :] = jnp.where(has_left, rows[:16], jnp.zeros_like(rows[:16]))
        if i == 7:
            dst[pl.ds(OFF + TD, 16), :] = jnp.where(
                has_right, rows[128:], jnp.zeros_like(rows[128:])
            )

    own_copy.wait()
    small_copies[0].wait()
    weight_copies[0].wait()
    weight_copies[1].start()
    small_copies[1].start()
    weight_copies[2].start()
    for i in range(1, 7):
        put(h1, conv(0, h0, *tiles[i]), i)

    @pl.when(has_left)
    def _():
        to_right.wait_recv()

    @pl.when(jnp.logical_not(has_left))
    def _():
        h0[pl.ds(OFF - 16, 16), :] = jnp.zeros((16, C), BF)

    @pl.when(has_right)
    def _():
        to_left.wait_recv()

    @pl.when(jnp.logical_not(has_right))
    def _():
        h0[pl.ds(OFF + TD, 16), :] = jnp.zeros((16, C), BF)

    put(h1, conv(0, h0, *tiles[7]), 7)
    put(h1, conv(0, h0, *tiles[0]), 0)

    y_copies = []

    def tile_copy(way, t):
        begin, end = (0, 384) if t == 0 else (128 + TILE * t, 128 + TILE * (t + 1))
        half = end - 128
        lanes = [(begin, end), (begin, end), (begin, half), (half, end)][way]
        lanes = pl.ds(lanes[0], lanes[1] - lanes[0])
        return remote(
            seg.at[(0, 0, 1, 2)[way], :, lanes],
            seg.at[(1, 2, 3, 3)[way], :, lanes],
            y_send.at[way, t],
            y_recv.at[way, t],
            y_peer((1, 3, 1, 3)[way]),
        )

    def send(way, t):
        copy = tile_copy(way, t)
        copy.start()
        y_copies.append(copy)

    def send_tile(t):
        send(0, t)
        send(1, t)

    def relay(t):
        for way in (0, 1):
            tile_copy(way, t).wait_recv()
            send(way + 2, t)

    def finish(i):
        begin, end = tiles[i]
        end = min(end, OFF + TD)
        rows = conv(2, h2, begin, end)
        points = nt_dot(proj_ref[...], rows)
        if i == 0:
            edge = jnp.where(has_left, points[:, 15:16], jnp.zeros((PATH, 1), F32))
            seg[0, :, pl.ds(0, 128)] = jnp.broadcast_to(edge, (PATH, 128)).astype(BF)
            points = points[:, 16:]
        points = points.astype(BF)
        path_ref[:, pl.ds(128 * i, 128)] = points
        seg[0, :, pl.ds(128 + 128 * i, 128)] = points
        if i % 2 == 1:
            send_tile(i // 2)
            if i > 3:
                relay(i // 2 - 2)

    weight_copies[1].wait()
    put(h2, conv(1, h1, *tiles[0]), 0)
    put(h2, conv(1, h1, *tiles[1]), 1)
    weight_copies[2].wait()
    small_copies[1].wait()
    for i in range(2, 8):
        put(h2, conv(1, h1, *tiles[i]), i)
        finish(i - 2)
    known = seg[0, :, pl.ds(128, 640)].astype(F32)
    mean = jnp.sum(known, axis=1, keepdims=True) * (1.0 / 640)
    centre[...] = jnp.broadcast_to(mean, (PATH, 128))
    finish(6)
    finish(7)

    def prepare(slot, t, buf):
        window = seg[slot, :, pl.ds(TILE * t, 384)].astype(F32)
        now, before = window[:, 128:], window[:, 127:383]
        step[buf] = now - before
        wide_centre = jnp.concatenate([centre[...]] * 2, axis=1)
        mid[buf] = 0.5 * (now + before) - wide_centre

    def step_columns(buf):
        d = step[buf]
        high = d.astype(BF)
        low = (d - high.astype(F32)).astype(BF)
        return jnp.concatenate([high, low], axis=0)

    def add_rows(at, row_begin, buf, columns):
        m = mid[buf].astype(BF)
        d = (step[buf] * (1.0 / 12.0)).astype(BF)

        def spread(ref, r):
            row = jnp.broadcast_to(ref[buf, pl.ds(row_begin + r, 1), :], (16, TILE)).astype(BF)
            return jnp.concatenate([row] * 4, axis=0)

        rows = [spread(mid, r) * m + spread(step, r) * d for r in range(8)]
        acc[pl.ds(at, 512), :] += nt_dot(jnp.concatenate(rows, axis=0), columns)

    def add_level2(buf, columns):
        m = mid[buf]
        high = m.astype(BF)
        low = (m - high.astype(F32)).astype(BF)
        ones = jnp.ones((16, TILE), BF)
        acc[pl.ds(1024, 144), :] += nt_dot(jnp.concatenate([high, low, ones], axis=0), columns)

    their_rows = y * 16 + (1 - core) * 8
    my_rows = y * 16 + core * 8
    acc[...] = jnp.zeros_like(acc)

    def wait_relayed(t):
        tile_copy(2, t).wait_recv()
        tile_copy(3, t).wait_recv()

    def everything(steps):
        for at, (slot, t) in enumerate(steps):
            prepare(slot, t, at % 4)
            columns = step_columns(at % 4)
            add_rows(0, their_rows, at % 4, columns)
            add_level2(at % 4, columns)
            add_rows(512, my_rows, at % 4, columns)

    everything([(0, t) for t in range(4)])
    relay(2)
    everything([(1, 0), (2, 0), (1, 1), (2, 1)])
    relay(3)
    wait_relayed(0)
    wait_relayed(1)
    everything([(1, 2), (2, 2), (3, 0), (3, 1), (1, 3), (2, 3)])
    wait_relayed(2)
    everything([(3, 2)])

    def their_step(slot):
        prepare(slot, 3, slot)
        columns = step_columns(slot)
        add_rows(0, their_rows, slot, columns)
        add_level2(slot, columns)

    wait_relayed(3)
    their_step(3)

    low_half = lax.broadcasted_iota(jnp.int32, (64, 128), 1) < 64

    def both_halves(v):
        return v + pltpu.roll(v, 64, 1)

    def packed_level2():
        even, odd = level2[pl.ds(0, 32, stride=2), :], level2[pl.ds(1, 32, stride=2), :]
        return jnp.where(low_half[:32], even, odd)

    local2 = both_halves(acc[pl.ds(1024, 64), :] + acc[pl.ds(1088, 64), :])
    delta = both_halves(acc[pl.ds(1152, 8), :])
    middle = centre[...]
    own2 = local2 + middle * delta[:1]
    level2[pl.ds(0, 64), :] = own2

    def third_rows(at, row_begin, dst):
        def block(r):
            rows = both_halves(acc[pl.ds(at + 64 * r, 64), :])
            c_row = centre[pl.ds(row_begin + r, 1), :]
            s_row = level2[pl.ds(row_begin + r, 1), :]
            return rows + c_row * local2 + middle * s_row

        for r in range(4):
            dst[r // 2, pl.ds(64 * (r % 2), 64), :] = jnp.where(low_half, block(r), block(r + 4))

    def low_levels(dst):
        pairs = packed_level2()
        for half in range(2):
            dst[half, pl.ds(128, 16), :] = pairs[16 * half : 16 * half + 16]
            dst[half, pl.ds(144, 8), :] = delta

    third_rows(0, their_rows, partner_out)
    low_levels(partner_out)
    swap = remote(partner_out, partner_in, p_send, p_recv, partner)
    swap.start()

    add_rows(512, my_rows, 3, step_columns(3))
    third_rows(512, my_rows, mine)
    low_levels(mine)
    swap.wait_recv()
    mine[...] += partner_in[...]

    def pack(dst, value):
        dst[pl.ds(0, 128), :] = value[:128].astype(BF)
        exact = value[128:144]
        high = exact.astype(BF)
        dst[pl.ds(128, 16), :] = high
        dst[pl.ds(144, 16), :] = (exact - high.astype(F32)).astype(BF)
        exact = value[144:152]
        high = exact.astype(BF).astype(F32)
        dst[pl.ds(160, 16), :] = jnp.concatenate([high, exact - high], axis=0).astype(BF)

    def unpack(src):
        second = src[pl.ds(128, 16), :].astype(F32) + src[pl.ds(144, 16), :].astype(F32)
        pair = src[pl.ds(160, 16), :].astype(F32)
        third = src[pl.ds(0, 128), :].astype(F32)
        return jnp.concatenate([third, second, pair[:8] + pair[8:]], axis=0)

    def x_copy(src, half, by):
        at = 3 * half + by - 1
        return remote(src, in_x.at[at], x_send.at[at], x_recv.at[at], x_peer(by))

    def z_copy(src, half, by):
        at = 3 * half + by - 1
        return remote(src, in_z.at[at], z_send.at[at], z_recv.at[at], z_peer(by))

    def up_z(src, half):
        for by in range(1, 4):

            @pl.when(z + by < NZ)
            def _():
                z_copy(src, half, by).start()

    def add_lower_z(dst, half):
        for by in range(1, 4):

            @pl.when(z >= by)
            def _():
                z_copy(out_2, half, by).wait_recv()
                dst[...] += unpack(in_z.at[3 * half + by - 1])

    pack(out_1.at[0], mine[0])
    pack(out_1.at[1], mine[1])
    for by in range(1, 4):
        x_copy(out_1.at[0], 0, by).start()
    @pl.when(z < NZ - 1)
    def _():
        pl.semaphore_wait(z_ready, NZ - 1 - z)

    up_z(out_1.at[1], 1)
    swap.wait_send()

    below = partner_out.at[1]
    below[...] = jnp.zeros((PART, 128), F32)
    add_lower_z(below, 1)
    pack(out_low, below[...])
    mine[1] += below[...]
    pack(out_2.at[1], mine[1])
    for by in range(1, 4):

        @pl.when(x + by < NX)
        def _():
            x_copy(out_2.at[1], 1, by).start()

        @pl.when(x + by >= NX)
        def _():
            x_copy(out_low, 1, by).start()

    total = upto = mine[0]
    for by in range(1, 4):
        x_copy(out_1.at[0], 0, by).wait_recv()
        other = unpack(in_x.at[by - 1])
        total = total + other
        upto = upto + jnp.where(x >= by, other, jnp.zeros_like(other))
    pack(out_2.at[0], total)
    up_z(out_2.at[0], 0)
    mine[0] = upto

    for by in range(1, 4):
        x_copy(out_low, 1, by).wait_recv()
        mine[1] += unpack(in_x.at[3 + by - 1])
    add_lower_z(mine.at[0], 0)

    scale = total_steps ** (-0.2)
    ends = mine[0, pl.ds(144, 8), :]
    ends_k = jnp.broadcast_to(ends.T[:64, :1], (64, 128))
    first_ref[...] = ends[:1, :64] * scale
    for half in range(2):
        second_ref[pl.ds(16 * half, 16), :] = mine[half, pl.ds(128, 16), :] * scale**2

    def level2_row(r):
        row = mine[lax.div(n, 4), pl.ds(128 + 4 * lax.rem(n, 4) + r // 2, 1), :]
        other = pltpu.roll(row, 64, 1)
        low = low_half[:1]
        return jnp.where(low, row, other) if r % 2 == 0 else jnp.where(low, other, row)

    for r in range(4):
        row = jnp.where(low_half[:1], level2_row(r), level2_row(r + 4))
        values = ((row * ends_k - mine[r // 2, pl.ds(64 * (r % 2), 64), :]) * scale**3).T
        turned[pl.ds(r, 64, stride=8), :] = values[:64]
        turned[pl.ds(4 + r, 64, stride=8), :] = values[64:]
    for pair in range(32):
        both = [turned[pl.ds(16 * pair + 8 * k, 8), :] for k in range(2)]
        third_ref[:, pl.ds(128 * pair, 128)] = jnp.concatenate(both, axis=1)

    @pl.when(has_left)
    def _():
        to_left.wait_send()

    @pl.when(has_right)
    def _():
        to_right.wait_send()

    for copy in y_copies:
        copy.wait_send()
    for by in range(1, 4):
        for half in range(2):
            x_copy(out_low, half, by).wait_send()

            @pl.when(z + by < NZ)
            def _():
                z_copy(out_low, half, by).wait_send()


def emit(*refs):
    copies = [
        pltpu.make_async_copy(src, dst, refs[8].at[k])
        for k, (src, dst) in enumerate(zip(refs[:4], refs[4:8]))
    ]
    for copy in copies:
        copy.start()
    for copy in copies:
        copy.wait()


def per_device(total_steps, recording, conv_weight, conv_bias, projection):
    vmem = pl.BlockSpec(memory_space=pltpu.VMEM)
    hbm = pl.BlockSpec(memory_space=pltpu.HBM)
    operands = (recording, conv_weight.reshape(3, 3 * C, C), conv_bias, projection.T)
    operands = [pltpu.with_memory_space_constraint(a, pltpu.HBM) for a in operands]
    out_shape = (
        jax.ShapeDtypeStruct((PATH, TD), BF),
        jax.ShapeDtypeStruct((8, PATH * PATH), F32),
        jax.ShapeDtypeStruct((32, 128), F32),
        jax.ShapeDtypeStruct((1, PATH), F32),
    )
    results = pl.pallas_call(
        functools.partial(kernel, total_steps),
        out_shape=out_shape,
        in_specs=[hbm, hbm, hbm, hbm],
        out_specs=(vmem, vmem, vmem, vmem),
        scratch_shapes=[
            pltpu.VMEM((3, 3 * C, C), BF),
            pltpu.VMEM((3, C), F32),
            pltpu.VMEM((PATH, C), BF),
            pltpu.VMEM((ROWS, C), BF),
            pltpu.VMEM((ROWS, C), BF),
            pltpu.VMEM((ROWS, C), BF),
            pltpu.VMEM((4, PATH, 128 + TD), BF),
            pltpu.VMEM((4, PATH, TILE), F32),
            pltpu.VMEM((4, PATH, TILE), F32),
            pltpu.VMEM((PATH, 128), F32),
            pltpu.VMEM((1168, 128), F32),
            pltpu.VMEM((64, 128), F32),
            pltpu.VMEM((2, PART, 128), F32),
            pltpu.VMEM((512, PATH), F32),
            pltpu.VMEM((2, PART, 128), F32),
            pltpu.VMEM((2, PART, 128), F32),
            pltpu.VMEM((2, PAY, 128), BF),
            pltpu.VMEM((2, PAY, 128), BF),
            pltpu.VMEM((PAY, 128), BF),
            pltpu.VMEM((6, PAY, 128), BF),
            pltpu.VMEM((6, PAY, 128), BF),
            pltpu.SemaphoreType.DMA((3,)),
            pltpu.SemaphoreType.DMA((2,)),
            pltpu.SemaphoreType.DMA,
            pltpu.SemaphoreType.DMA((2,)),
            pltpu.SemaphoreType.DMA((2,)),
            pltpu.SemaphoreType.DMA((4, 4)),
            pltpu.SemaphoreType.DMA((4, 4)),
            pltpu.SemaphoreType.DMA,
            pltpu.SemaphoreType.DMA,
            pltpu.SemaphoreType.DMA((6,)),
            pltpu.SemaphoreType.DMA((6,)),
            pltpu.SemaphoreType.DMA((6,)),
            pltpu.SemaphoreType.DMA((6,)),
            pltpu.SemaphoreType.REGULAR,
        ],
        compiler_params=pltpu.CompilerParams(
            collective_id=0, has_side_effects=True, vmem_limit_bytes=48 << 20
        ),
    )(*operands)
    path_points, third, second, first = pl.pallas_call(
        emit,
        out_shape=out_shape,
        in_specs=[vmem] * 4,
        out_specs=[hbm] * 4,
        scratch_shapes=[pltpu.SemaphoreType.DMA((4,))],
        compiler_params=pltpu.CompilerParams(vmem_limit_bytes=1 << 20),
    )(*results)
    return path_points.T, first, second.reshape(1, PATH * PATH), third[None]


def solution(mesh):
    total_steps = TD * mesh.shape["wide"] * mesh.shape["narrow"]
    return jax.shard_map(
        functools.partial(per_device, total_steps),
        mesh=mesh,
        in_specs=(P(("wide", "narrow"), None), P(), P(), P()),
        out_specs=(
            P(("wide", "narrow"), None),
            P("wide", None),
            P("wide", None),
            P("wide", "narrow", None),
        ),
        check_vma=False,
    )
```

```python
import functools

import jax
import jax.numpy as jnp
from jax import lax
from jax.experimental import pallas as pl
from jax.experimental.pallas import tpu as pltpu
from jax.sharding import PartitionSpec as P

C = 512
PATH = 64
TD = 1024
OFF = 32
ROWS = OFF + TD + 32
NX = 4
NZ = 4
NY = 4
TILE = 256
PART = 128 + 16 + 8
PAY = 128 + 32 + 16
MESH = pl.DeviceIdType.MESH
BF = jnp.bfloat16
F32 = jnp.float32


def silu(v):
    half = 0.5 * v
    return half + half * jnp.tanh(half)


def nt_dot(a, b):
    return lax.dot_general(a, b, (((1,), (1,)), ((), ())), preferred_element_type=F32)


def kernel(
    total_steps,
    rec_hbm,
    weight_hbm,
    bias_hbm,
    proj_hbm,
    path_ref,
    third_ref,
    second_ref,
    first_ref,
    weights,
    bias_ref,
    proj_ref,
    h0,
    h1,
    h2,
    seg,
    mid,
    step,
    centre,
    acc,
    level2,
    mine,
    turned,
    partner_out,
    partner_in,
    out_1,
    out_2,
    out_low,
    in_x,
    in_z,
    w_sem,
    small_sem,
    r_sem,
    halo_send,
    halo_recv,
    y_send,
    y_recv,
    p_send,
    p_recv,
    x_send,
    x_recv,
    z_send,
    z_recv,
    z_ready,
):
    w = lax.axis_index("wide")
    n = lax.axis_index("narrow")
    z, x = lax.div(w, NX), lax.rem(w, NX)
    y, core = lax.div(n, 2), lax.rem(n, 2)
    g = w * 8 + n
    last_g = NX * NZ * 8 - 1
    has_left = g > 0
    has_right = g < last_g
    left = (lax.div(g + last_g, 8) % (NX * NZ), lax.rem(g + last_g, 8))
    right = (lax.div(g + 1, 8) % (NX * NZ), lax.rem(g + 1, 8))

    def y_peer(by):
        return (w, lax.rem(y + by, NY) * 2 + core)

    def x_peer(by):
        return (z * NX + lax.rem(x + by, NX), n)

    def z_peer(by):
        return ((z + by) * NX + x, n)

    partner = (w, y * 2 + 1 - core)

    weight_copies = [
        pltpu.make_async_copy(weight_hbm.at[l], weights.at[l], w_sem.at[l]) for l in range(3)
    ]
    own_copy = pltpu.make_async_copy(rec_hbm, h0.at[pl.ds(OFF, TD)], r_sem)
    small_copies = [
        pltpu.make_async_copy(bias_hbm, bias_ref, small_sem.at[0]),
        pltpu.make_async_copy(proj_hbm, proj_ref, small_sem.at[1]),
    ]
    own_copy.start()
    small_copies[0].start()
    weight_copies[0].start()

    barrier = pltpu.get_barrier_semaphore()

    @pl.when(has_left)
    def _():
        pl.semaphore_signal(barrier, inc=1, device_id=left, device_id_type=MESH)

    @pl.when(has_right)
    def _():
        pl.semaphore_signal(barrier, inc=1, device_id=right, device_id_type=MESH)

    for by in range(1, 4):
        pl.semaphore_signal(barrier, inc=1, device_id=y_peer(by), device_id_type=MESH)
        pl.semaphore_signal(barrier, inc=1, device_id=x_peer(by), device_id_type=MESH)

        @pl.when(z + by < NZ)
        def _():
            pl.semaphore_signal(barrier, inc=1, device_id=z_peer(by), device_id_type=MESH)

    pl.semaphore_signal(barrier, inc=1, device_id=partner, device_id_type=MESH)
    greeted = has_left.astype(jnp.int32) + has_right.astype(jnp.int32) + 7 + z
    pl.semaphore_wait(barrier, greeted)
    for by in range(1, 4):

        @pl.when(z >= by)
        def _():
            pl.semaphore_signal(z_ready, inc=1, device_id=z_peer(-by), device_id_type=MESH)

    def remote(src, dst, send, recv, device):
        return pltpu.make_async_remote_copy(
            src_ref=src,
            dst_ref=dst,
            send_sem=send,
            recv_sem=recv,
            device_id=device,
            device_id_type=MESH,
        )

    to_left = remote(
        rec_hbm.at[pl.ds(0, 16)],
        h0.at[pl.ds(OFF + TD, 16)],
        halo_send.at[0],
        halo_recv.at[0],
        left,
    )
    to_right = remote(
        rec_hbm.at[pl.ds(TD - 16, 16)],
        h0.at[pl.ds(OFF - 16, 16)],
        halo_send.at[1],
        halo_recv.at[1],
        right,
    )

    @pl.when(has_left)
    def _():
        to_left.start()

    @pl.when(has_right)
    def _():
        to_right.start()

    def conv(layer, src, begin, end):
        d = 2**layer
        xs = [src[pl.ds(begin + (k - 1) * d, end - begin), :] for k in range(3)]
        centre_rows = xs[1].astype(F32)
        both = jnp.concatenate(xs, axis=1)
        totals = jnp.dot(both, weights[layer], preferred_element_type=F32)
        return (centre_rows + silu(totals + bias_ref[pl.ds(layer, 1), :])).astype(BF)

    first_tile, last_tile = (OFF - 16, OFF + 128), (OFF + TD - 128, OFF + TD + 16)
    tiles = [first_tile] + [(OFF + 128 * i, OFF + 128 * i + 128) for i in range(1, 7)] + [last_tile]

    def put(dst, rows, i):
        begin, end = tiles[i]
        dst[pl.ds(begin, end - begin), :] = rows
        if i == 0:
            dst[pl.ds(OFF - 16, 16), :] = jnp.where(has_left, rows[:16], jnp.zeros_like(rows[:16]))
        if i == 7:
            dst[pl.ds(OFF + TD, 16), :] = jnp.where(
                has_right, rows[128:], jnp.zeros_like(rows[128:])
            )

    own_copy.wait()
    small_copies[0].wait()
    weight_copies[0].wait()
    weight_copies[1].start()
    small_copies[1].start()
    weight_copies[2].start()
    for i in range(1, 7):
        put(h1, conv(0, h0, *tiles[i]), i)

    @pl.when(has_left)
    def _():
        to_right.wait_recv()

    @pl.when(jnp.logical_not(has_left))
    def _():
        h0[pl.ds(OFF - 16, 16), :] = jnp.zeros((16, C), BF)

    @pl.when(has_right)
    def _():
        to_left.wait_recv()

    @pl.when(jnp.logical_not(has_right))
    def _():
        h0[pl.ds(OFF + TD, 16), :] = jnp.zeros((16, C), BF)

    put(h1, conv(0, h0, *tiles[7]), 7)
    put(h1, conv(0, h0, *tiles[0]), 0)

    y_copies = []

    def tile_copy(way, t):
        begin, end = (0, 384) if t == 0 else (128 + TILE * t, 128 + TILE * (t + 1))
        half = end - 128
        lanes = {2: (begin, half), 3: (half, end)}.get(way, (begin, end))
        lanes = pl.ds(lanes[0], lanes[1] - lanes[0])
        at = way if way < 4 else 2
        return remote(
            seg.at[(0, 0, 1, 2, 0)[way], :, lanes],
            seg.at[(1, 2, 3, 3, 3)[way], :, lanes],
            y_send.at[at, t],
            y_recv.at[at, t],
            y_peer((1, 3, 1, 3, 2)[way]),
        )

    def send(way, t):
        copy = tile_copy(way, t)
        copy.start()
        y_copies.append(copy)

    def send_tile(t):
        if t > 1:
            send(4, t)
        send(0, t)
        send(1, t)

    def relay(t):
        for way in (0, 1):
            tile_copy(way, t).wait_recv()
            send(way + 2, t)

    def finish(i):
        begin, end = tiles[i]
        end = min(end, OFF + TD)
        rows = conv(2, h2, begin, end)
        points = nt_dot(proj_ref[...], rows)
        if i == 0:
            edge = jnp.where(has_left, points[:, 15:16], jnp.zeros((PATH, 1), F32))
            seg[0, :, pl.ds(0, 128)] = jnp.broadcast_to(edge, (PATH, 128)).astype(BF)
            points = points[:, 16:]
        points = points.astype(BF)
        path_ref[:, pl.ds(128 * i, 128)] = points
        seg[0, :, pl.ds(128 + 128 * i, 128)] = points
        if i % 2 == 1:
            send_tile(i // 2)
            if i > 3:
                relay(i // 2 - 2)

    weight_copies[1].wait()
    put(h2, conv(1, h1, *tiles[0]), 0)
    put(h2, conv(1, h1, *tiles[1]), 1)
    weight_copies[2].wait()
    small_copies[1].wait()
    for i in range(2, 8):
        put(h2, conv(1, h1, *tiles[i]), i)
        finish(i - 2)
    known = seg[0, :, pl.ds(128, 640)].astype(F32)
    mean = jnp.sum(known, axis=1, keepdims=True) * (1.0 / 640)
    centre[...] = jnp.broadcast_to(mean, (PATH, 128))
    finish(6)
    finish(7)

    def prepare(slot, t, buf):
        window = seg[slot, :, pl.ds(TILE * t, 384)].astype(F32)
        now, before = window[:, 128:], window[:, 127:383]
        step[buf] = now - before
        wide_centre = jnp.concatenate([centre[...]] * 2, axis=1)
        mid[buf] = 0.5 * (now + before) - wide_centre

    def step_columns(buf):
        d = step[buf]
        high = d.astype(BF)
        low = (d - high.astype(F32)).astype(BF)
        return jnp.concatenate([high, low], axis=0)

    def add_rows(at, row_begin, buf, columns):
        m = mid[buf].astype(BF)
        d = (step[buf] * (1.0 / 12.0)).astype(BF)

        def spread(ref, r):
            row = jnp.broadcast_to(ref[buf, pl.ds(row_begin + r, 1), :], (16, TILE)).astype(BF)
            return jnp.concatenate([row] * 4, axis=0)

        rows = [spread(mid, r) * m + spread(step, r) * d for r in range(8)]
        acc[pl.ds(at, 512), :] += nt_dot(jnp.concatenate(rows, axis=0), columns)

    def add_level2(buf, columns):
        m = mid[buf]
        high = m.astype(BF)
        low = (m - high.astype(F32)).astype(BF)
        ones = jnp.ones((16, TILE), BF)
        acc[pl.ds(1024, 144), :] += nt_dot(jnp.concatenate([high, low, ones], axis=0), columns)

    their_rows = y * 16 + (1 - core) * 8
    my_rows = y * 16 + core * 8
    acc[...] = jnp.zeros_like(acc)

    def wait_relayed(t):
        tile_copy(2, t).wait_recv()
        tile_copy(3, t).wait_recv()

    def everything(steps):
        for at, (slot, t) in enumerate(steps):
            prepare(slot, t, at % 4)
            columns = step_columns(at % 4)
            add_rows(0, their_rows, at % 4, columns)
            add_level2(at % 4, columns)
            add_rows(512, my_rows, at % 4, columns)

    everything([(0, t) for t in range(4)] + [(slot, t) for t in range(2) for slot in (1, 2)])
    wait_relayed(0)
    wait_relayed(1)
    for way in (0, 1, 4):
        tile_copy(way, 2).wait_recv()
    everything([(3, 0), (3, 1), (1, 2), (2, 2), (3, 2)])
    for way in (0, 1, 4):
        tile_copy(way, 3).wait_recv()

    def their_step(slot):
        prepare(slot, 3, slot)
        columns = step_columns(slot)
        add_rows(0, their_rows, slot, columns)
        add_level2(slot, columns)

    for slot in range(1, 4):
        their_step(slot)

    low_half = lax.broadcasted_iota(jnp.int32, (64, 128), 1) < 64

    def both_halves(v):
        return v + pltpu.roll(v, 64, 1)

    def packed_level2():
        even, odd = level2[pl.ds(0, 32, stride=2), :], level2[pl.ds(1, 32, stride=2), :]
        return jnp.where(low_half[:32], even, odd)

    local2 = both_halves(acc[pl.ds(1024, 64), :] + acc[pl.ds(1088, 64), :])
    delta = both_halves(acc[pl.ds(1152, 8), :])
    middle = centre[...]
    own2 = local2 + middle * delta[:1]
    level2[pl.ds(0, 64), :] = own2

    def third_rows(at, row_begin, dst):
        def block(r):
            rows = both_halves(acc[pl.ds(at + 64 * r, 64), :])
            c_row = centre[pl.ds(row_begin + r, 1), :]
            s_row = level2[pl.ds(row_begin + r, 1), :]
            return rows + c_row * local2 + middle * s_row

        for r in range(4):
            dst[r // 2, pl.ds(64 * (r % 2), 64), :] = jnp.where(low_half, block(r), block(r + 4))

    def low_levels(dst):
        pairs = packed_level2()
        for half in range(2):
            dst[half, pl.ds(128, 16), :] = pairs[16 * half : 16 * half + 16]
            dst[half, pl.ds(144, 8), :] = delta

    third_rows(0, their_rows, partner_out)
    low_levels(partner_out)
    swap = remote(partner_out, partner_in, p_send, p_recv, partner)
    swap.start()

    for slot in range(1, 4):
        add_rows(512, my_rows, slot, step_columns(slot))
    third_rows(512, my_rows, mine)
    low_levels(mine)
    swap.wait_recv()
    mine[...] += partner_in[...]

    def pack(dst, value):
        dst[pl.ds(0, 128), :] = value[:128].astype(BF)
        exact = value[128:144]
        high = exact.astype(BF)
        dst[pl.ds(128, 16), :] = high
        dst[pl.ds(144, 16), :] = (exact - high.astype(F32)).astype(BF)
        exact = value[144:152]
        high = exact.astype(BF).astype(F32)
        dst[pl.ds(160, 16), :] = jnp.concatenate([high, exact - high], axis=0).astype(BF)

    def unpack(src):
        second = src[pl.ds(128, 16), :].astype(F32) + src[pl.ds(144, 16), :].astype(F32)
        pair = src[pl.ds(160, 16), :].astype(F32)
        third = src[pl.ds(0, 128), :].astype(F32)
        return jnp.concatenate([third, second, pair[:8] + pair[8:]], axis=0)

    def x_copy(src, half, by):
        at = 3 * half + by - 1
        return remote(src, in_x.at[at], x_send.at[at], x_recv.at[at], x_peer(by))

    def z_copy(src, half, by):
        at = 3 * half + by - 1
        return remote(src, in_z.at[at], z_send.at[at], z_recv.at[at], z_peer(by))

    def up_z(src, half):
        for by in range(1, 4):

            @pl.when(z + by < NZ)
            def _():
                z_copy(src, half, by).start()

    def add_lower_z(dst, half):
        for by in range(1, 4):

            @pl.when(z >= by)
            def _():
                z_copy(out_2, half, by).wait_recv()
                dst[...] += unpack(in_z.at[3 * half + by - 1])

    pack(out_1.at[0], mine[0])
    pack(out_1.at[1], mine[1])
    for by in range(1, 4):
        x_copy(out_1.at[0], 0, by).start()
    @pl.when(z < NZ - 1)
    def _():
        pl.semaphore_wait(z_ready, NZ - 1 - z)

    up_z(out_1.at[1], 1)
    swap.wait_send()

    below = partner_out.at[1]
    below[...] = jnp.zeros((PART, 128), F32)
    add_lower_z(below, 1)
    pack(out_low, below[...])
    mine[1] += below[...]
    pack(out_2.at[1], mine[1])
    for by in range(1, 4):

        @pl.when(x + by < NX)
        def _():
            x_copy(out_2.at[1], 1, by).start()

        @pl.when(x + by >= NX)
        def _():
            x_copy(out_low, 1, by).start()

    total = upto = mine[0]
    for by in range(1, 4):
        x_copy(out_1.at[0], 0, by).wait_recv()
        other = unpack(in_x.at[by - 1])
        total = total + other
        upto = upto + jnp.where(x >= by, other, jnp.zeros_like(other))
    pack(out_2.at[0], total)
    up_z(out_2.at[0], 0)
    mine[0] = upto

    for by in range(1, 4):
        x_copy(out_low, 1, by).wait_recv()
        mine[1] += unpack(in_x.at[3 + by - 1])
    add_lower_z(mine.at[0], 0)

    scale = total_steps ** (-0.2)
    ends = mine[0, pl.ds(144, 8), :]
    ends_k = jnp.broadcast_to(ends.T[:64, :1], (64, 128))
    first_ref[...] = ends[:1, :64] * scale
    for half in range(2):
        second_ref[pl.ds(16 * half, 16), :] = mine[half, pl.ds(128, 16), :] * scale**2

    def level2_row(r):
        row = mine[lax.div(n, 4), pl.ds(128 + 4 * lax.rem(n, 4) + r // 2, 1), :]
        other = pltpu.roll(row, 64, 1)
        low = low_half[:1]
        return jnp.where(low, row, other) if r % 2 == 0 else jnp.where(low, other, row)

    for r in range(4):
        row = jnp.where(low_half[:1], level2_row(r), level2_row(r + 4))
        values = ((row * ends_k - mine[r // 2, pl.ds(64 * (r % 2), 64), :]) * scale**3).T
        turned[pl.ds(r, 64, stride=8), :] = values[:64]
        turned[pl.ds(4 + r, 64, stride=8), :] = values[64:]
    for pair in range(32):
        both = [turned[pl.ds(16 * pair + 8 * k, 8), :] for k in range(2)]
        third_ref[:, pl.ds(128 * pair, 128)] = jnp.concatenate(both, axis=1)

    @pl.when(has_left)
    def _():
        to_left.wait_send()

    @pl.when(has_right)
    def _():
        to_right.wait_send()

    for copy in y_copies:
        copy.wait_send()
    for by in range(1, 4):
        for half in range(2):
            x_copy(out_low, half, by).wait_send()

            @pl.when(z + by < NZ)
            def _():
                z_copy(out_low, half, by).wait_send()


def emit(*refs):
    copies = [
        pltpu.make_async_copy(src, dst, refs[8].at[k])
        for k, (src, dst) in enumerate(zip(refs[:4], refs[4:8]))
    ]
    for copy in copies:
        copy.start()
    for copy in copies:
        copy.wait()


def per_device(total_steps, recording, conv_weight, conv_bias, projection):
    vmem = pl.BlockSpec(memory_space=pltpu.VMEM)
    hbm = pl.BlockSpec(memory_space=pltpu.HBM)
    operands = (recording, conv_weight.reshape(3, 3 * C, C), conv_bias, projection.T)
    operands = [pltpu.with_memory_space_constraint(a, pltpu.HBM) for a in operands]
    out_shape = (
        jax.ShapeDtypeStruct((PATH, TD), BF),
        jax.ShapeDtypeStruct((8, PATH * PATH), F32),
        jax.ShapeDtypeStruct((32, 128), F32),
        jax.ShapeDtypeStruct((1, PATH), F32),
    )
    results = pl.pallas_call(
        functools.partial(kernel, total_steps),
        out_shape=out_shape,
        in_specs=[hbm, hbm, hbm, hbm],
        out_specs=(vmem, vmem, vmem, vmem),
        scratch_shapes=[
            pltpu.VMEM((3, 3 * C, C), BF),
            pltpu.VMEM((3, C), F32),
            pltpu.VMEM((PATH, C), BF),
            pltpu.VMEM((ROWS, C), BF),
            pltpu.VMEM((ROWS, C), BF),
            pltpu.VMEM((ROWS, C), BF),
            pltpu.VMEM((4, PATH, 128 + TD), BF),
            pltpu.VMEM((4, PATH, TILE), F32),
            pltpu.VMEM((4, PATH, TILE), F32),
            pltpu.VMEM((PATH, 128), F32),
            pltpu.VMEM((1168, 128), F32),
            pltpu.VMEM((64, 128), F32),
            pltpu.VMEM((2, PART, 128), F32),
            pltpu.VMEM((512, PATH), F32),
            pltpu.VMEM((2, PART, 128), F32),
            pltpu.VMEM((2, PART, 128), F32),
            pltpu.VMEM((2, PAY, 128), BF),
            pltpu.VMEM((2, PAY, 128), BF),
            pltpu.VMEM((PAY, 128), BF),
            pltpu.VMEM((6, PAY, 128), BF),
            pltpu.VMEM((6, PAY, 128), BF),
            pltpu.SemaphoreType.DMA((3,)),
            pltpu.SemaphoreType.DMA((2,)),
            pltpu.SemaphoreType.DMA,
            pltpu.SemaphoreType.DMA((2,)),
            pltpu.SemaphoreType.DMA((2,)),
            pltpu.SemaphoreType.DMA((4, 4)),
            pltpu.SemaphoreType.DMA((4, 4)),
            pltpu.SemaphoreType.DMA,
            pltpu.SemaphoreType.DMA,
            pltpu.SemaphoreType.DMA((6,)),
            pltpu.SemaphoreType.DMA((6,)),
            pltpu.SemaphoreType.DMA((6,)),
            pltpu.SemaphoreType.DMA((6,)),
            pltpu.SemaphoreType.REGULAR,
        ],
        compiler_params=pltpu.CompilerParams(
            collective_id=0, has_side_effects=True, vmem_limit_bytes=48 << 20
        ),
    )(*operands)
    path_points, third, second, first = pl.pallas_call(
        emit,
        out_shape=out_shape,
        in_specs=[vmem] * 4,
        out_specs=[hbm] * 4,
        scratch_shapes=[pltpu.SemaphoreType.DMA((4,))],
        compiler_params=pltpu.CompilerParams(vmem_limit_bytes=1 << 20),
    )(*results)
    return path_points.T, first, second.reshape(1, PATH * PATH), third[None]


def solution(mesh):
    total_steps = TD * mesh.shape["wide"] * mesh.shape["narrow"]
    return jax.shard_map(
        functools.partial(per_device, total_steps),
        mesh=mesh,
        in_specs=(P(("wide", "narrow"), None), P(), P(), P()),
        out_specs=(
            P(("wide", "narrow"), None),
            P("wide", None),
            P("wide", None),
            P("wide", "narrow", None),
        ),
        check_vma=False,
    )
```

```python
import functools

import jax
import jax.numpy as jnp
from jax import lax
from jax.experimental import pallas as pl
from jax.experimental.pallas import tpu as pltpu
from jax.sharding import PartitionSpec as P

C = 512
PATH = 64
TD = 1024
OFF = 32
ROWS = OFF + TD + 32
NX = 4
NZ = 4
NY = 4
TILE = 256
PART = 128 + 16 + 8
PAY = 128 + 32 + 16
MESH = pl.DeviceIdType.MESH
BF = jnp.bfloat16
F32 = jnp.float32


def silu(v):
    half = 0.5 * v
    return half + half * jnp.tanh(half)


def nt_dot(a, b):
    return lax.dot_general(a, b, (((1,), (1,)), ((), ())), preferred_element_type=F32)


def kernel(
    total_steps,
    rec_hbm,
    weight_hbm,
    bias_hbm,
    proj_hbm,
    path_ref,
    third_ref,
    second_ref,
    first_ref,
    weights,
    bias_ref,
    proj_ref,
    h0,
    h1,
    h2,
    seg,
    mid,
    step,
    centre,
    acc,
    level2,
    mine,
    turned,
    partner_out,
    partner_in,
    out_1,
    out_2,
    out_low,
    in_x,
    in_z,
    w_sem,
    small_sem,
    r_sem,
    halo_send,
    halo_recv,
    y_send,
    y_recv,
    p_send,
    p_recv,
    x_send,
    x_recv,
    z_send,
    z_recv,
    z_ready,
):
    w = lax.axis_index("wide")
    n = lax.axis_index("narrow")
    z, x = lax.div(w, NX), lax.rem(w, NX)
    y, core = lax.div(n, 2), lax.rem(n, 2)
    g = w * 8 + n
    last_g = NX * NZ * 8 - 1
    has_left = g > 0
    has_right = g < last_g
    left = (lax.div(g + last_g, 8) % (NX * NZ), lax.rem(g + last_g, 8))
    right = (lax.div(g + 1, 8) % (NX * NZ), lax.rem(g + 1, 8))

    def y_peer(by):
        return (w, lax.rem(y + by, NY) * 2 + core)

    def x_peer(by):
        return (z * NX + lax.rem(x + by, NX), n)

    def z_peer(by):
        return ((z + by) * NX + x, n)

    partner = (w, y * 2 + 1 - core)

    weight_copies = [
        pltpu.make_async_copy(weight_hbm.at[l], weights.at[l], w_sem.at[l]) for l in range(3)
    ]
    own_copy = pltpu.make_async_copy(rec_hbm, h0.at[pl.ds(OFF, TD)], r_sem)
    small_copies = [
        pltpu.make_async_copy(bias_hbm, bias_ref, small_sem.at[0]),
        pltpu.make_async_copy(proj_hbm, proj_ref, small_sem.at[1]),
    ]
    own_copy.start()
    small_copies[0].start()
    weight_copies[0].start()

    barrier = pltpu.get_barrier_semaphore()

    @pl.when(has_left)
    def _():
        pl.semaphore_signal(barrier, inc=1, device_id=left, device_id_type=MESH)

    @pl.when(has_right)
    def _():
        pl.semaphore_signal(barrier, inc=1, device_id=right, device_id_type=MESH)

    for by in range(1, 4):
        pl.semaphore_signal(barrier, inc=1, device_id=y_peer(by), device_id_type=MESH)
        pl.semaphore_signal(barrier, inc=1, device_id=x_peer(by), device_id_type=MESH)

        @pl.when(z + by < NZ)
        def _():
            pl.semaphore_signal(barrier, inc=1, device_id=z_peer(by), device_id_type=MESH)

    pl.semaphore_signal(barrier, inc=1, device_id=partner, device_id_type=MESH)
    greeted = has_left.astype(jnp.int32) + has_right.astype(jnp.int32) + 7 + z
    pl.semaphore_wait(barrier, greeted)
    for by in range(1, 4):

        @pl.when(z >= by)
        def _():
            pl.semaphore_signal(z_ready, inc=1, device_id=z_peer(-by), device_id_type=MESH)

    def remote(src, dst, send, recv, device):
        return pltpu.make_async_remote_copy(
            src_ref=src,
            dst_ref=dst,
            send_sem=send,
            recv_sem=recv,
            device_id=device,
            device_id_type=MESH,
        )

    to_left = remote(
        rec_hbm.at[pl.ds(0, 16)],
        h0.at[pl.ds(OFF + TD, 16)],
        halo_send.at[0],
        halo_recv.at[0],
        left,
    )
    to_right = remote(
        rec_hbm.at[pl.ds(TD - 16, 16)],
        h0.at[pl.ds(OFF - 16, 16)],
        halo_send.at[1],
        halo_recv.at[1],
        right,
    )

    @pl.when(has_left)
    def _():
        to_left.start()

    @pl.when(has_right)
    def _():
        to_right.start()

    def conv(layer, src, begin, end):
        d = 2**layer
        xs = [src[pl.ds(begin + (k - 1) * d, end - begin), :] for k in range(3)]
        centre_rows = xs[1].astype(F32)
        both = jnp.concatenate(xs, axis=1)
        totals = jnp.dot(both, weights[layer], preferred_element_type=F32)
        return (centre_rows + silu(totals + bias_ref[pl.ds(layer, 1), :])).astype(BF)

    first_tile, last_tile = (OFF - 16, OFF + 128), (OFF + TD - 128, OFF + TD + 16)
    tiles = [first_tile] + [(OFF + 128 * i, OFF + 128 * i + 128) for i in range(1, 7)] + [last_tile]

    def put(dst, rows, i):
        begin, end = tiles[i]
        dst[pl.ds(begin, end - begin), :] = rows
        if i == 0:
            dst[pl.ds(OFF - 16, 16), :] = jnp.where(has_left, rows[:16], jnp.zeros_like(rows[:16]))
        if i == 7:
            dst[pl.ds(OFF + TD, 16), :] = jnp.where(
                has_right, rows[128:], jnp.zeros_like(rows[128:])
            )

    own_copy.wait()
    small_copies[0].wait()
    weight_copies[0].wait()
    weight_copies[1].start()
    small_copies[1].start()
    weight_copies[2].start()
    for i in range(1, 6):
        put(h1, conv(0, h0, *tiles[i]), i)

    @pl.when(has_left)
    def _():
        to_right.wait_recv()

    @pl.when(jnp.logical_not(has_left))
    def _():
        h0[pl.ds(OFF - 16, 16), :] = jnp.zeros((16, C), BF)

    @pl.when(has_right)
    def _():
        to_left.wait_recv()

    @pl.when(jnp.logical_not(has_right))
    def _():
        h0[pl.ds(OFF + TD, 16), :] = jnp.zeros((16, C), BF)

    put(h1, conv(0, h0, *tiles[0]), 0)

    y_copies = []

    def send_tile(t):
        lanes = pl.ds(0, 384) if t == 0 else pl.ds(128 + TILE * t, TILE)
        for slot, by in ((1, 1), (2, 3), (3, 2)):
            copy = remote(
                seg.at[0, :, lanes],
                seg.at[slot, :, lanes],
                y_send.at[slot - 1, t],
                y_recv.at[slot - 1, t],
                y_peer(by),
            )
            copy.start()
            y_copies.append(copy)

    def finish(i):
        begin, end = tiles[i]
        end = min(end, OFF + TD)
        rows = conv(2, h2, begin, end)
        points = nt_dot(proj_ref[...], rows)
        if i == 0:
            edge = jnp.where(has_left, points[:, 15:16], jnp.zeros((PATH, 1), F32))
            seg[0, :, pl.ds(0, 128)] = jnp.broadcast_to(edge, (PATH, 128)).astype(BF)
            points = points[:, 16:]
        points = points.astype(BF)
        path_ref[:, pl.ds(128 * i, 128)] = points
        seg[0, :, pl.ds(128 + 128 * i, 128)] = points
        if i % 2 == 1:
            send_tile(i // 2)

    def layer_1(*which):
        for i in which:
            put(h1, conv(0, h0, *tiles[i]), i)

    def layer_2(*which):
        for i in which:
            put(h2, conv(1, h1, *tiles[i]), i)

    weight_copies[1].wait()
    layer_2(0, 1, 2)
    weight_copies[2].wait()
    small_copies[1].wait()
    finish(0)
    layer_2(3)
    finish(1)
    layer_2(4)
    finish(2)
    layer_1(6)
    finish(3)
    layer_1(7)
    layer_2(5, 6)
    finish(4)
    layer_2(7)
    finish(5)
    known = seg[0, :, pl.ds(128, 640)].astype(F32)
    mean = jnp.sum(known, axis=1, keepdims=True) * (1.0 / 640)
    centre[...] = jnp.broadcast_to(mean, (PATH, 128))
    finish(6)
    finish(7)

    def prepare(slot, t, buf):
        window = seg[slot, :, pl.ds(TILE * t, 384)].astype(F32)
        now, before = window[:, 128:], window[:, 127:383]
        step[buf] = now - before
        wide_centre = jnp.concatenate([centre[...]] * 2, axis=1)
        mid[buf] = 0.5 * (now + before) - wide_centre

    def step_columns(buf):
        d = step[buf]
        high = d.astype(BF)
        low = (d - high.astype(F32)).astype(BF)
        return jnp.concatenate([high, low], axis=0)

    def add_rows(at, row_begin, buf, columns):
        m = mid[buf].astype(BF)
        d = (step[buf] * (1.0 / 12.0)).astype(BF)

        def spread(ref, r):
            row = jnp.broadcast_to(ref[buf, pl.ds(row_begin + r, 1), :], (16, TILE)).astype(BF)
            return jnp.concatenate([row] * 4, axis=0)

        rows = [spread(mid, r) * m + spread(step, r) * d for r in range(8)]
        acc[pl.ds(at, 512), :] += nt_dot(jnp.concatenate(rows, axis=0), columns)

    def add_level2(buf, columns):
        m = mid[buf]
        high = m.astype(BF)
        low = (m - high.astype(F32)).astype(BF)
        ones = jnp.ones((16, TILE), BF)
        acc[pl.ds(1024, 144), :] += nt_dot(jnp.concatenate([high, low, ones], axis=0), columns)

    their_rows = y * 16 + (1 - core) * 8
    my_rows = y * 16 + core * 8
    acc[...] = jnp.zeros_like(acc)

    def wait_tile(slot, t):
        lanes = pl.ds(0, 384) if t == 0 else pl.ds(128 + TILE * t, TILE)
        remote(
            seg.at[0, :, lanes],
            seg.at[slot, :, lanes],
            y_send.at[slot - 1, t],
            y_recv.at[slot - 1, t],
            y_peer(1),
        ).wait_recv()

    def everything(steps):
        for at, (slot, t) in enumerate(steps):
            prepare(slot, t, at % 4)
            columns = step_columns(at % 4)
            add_rows(0, their_rows, at % 4, columns)
            add_level2(at % 4, columns)
            add_rows(512, my_rows, at % 4, columns)

    steps = [(0, t) for t in range(4)]
    for group in ((0, 1), (2,)):
        for t in group:
            for slot in range(1, 4):
                wait_tile(slot, t)
        everything(steps + [(slot, t) for t in group for slot in range(1, 4)])
        steps = []
    for slot in range(1, 4):
        wait_tile(slot, 3)
    for slot in range(1, 4):
        prepare(slot, 3, slot)
        columns = step_columns(slot)
        add_rows(0, their_rows, slot, columns)
        add_level2(slot, columns)

    low_half = lax.broadcasted_iota(jnp.int32, (64, 128), 1) < 64

    def both_halves(v):
        return v + pltpu.roll(v, 64, 1)

    def packed_level2():
        even, odd = level2[pl.ds(0, 32, stride=2), :], level2[pl.ds(1, 32, stride=2), :]
        return jnp.where(low_half[:32], even, odd)

    local2 = both_halves(acc[pl.ds(1024, 64), :] + acc[pl.ds(1088, 64), :])
    delta = both_halves(acc[pl.ds(1152, 8), :])
    middle = centre[...]
    own2 = local2 + middle * delta[:1]
    level2[pl.ds(0, 64), :] = own2

    def third_rows(at, row_begin, dst):
        def block(r):
            rows = both_halves(acc[pl.ds(at + 64 * r, 64), :])
            c_row = centre[pl.ds(row_begin + r, 1), :]
            s_row = level2[pl.ds(row_begin + r, 1), :]
            return rows + c_row * local2 + middle * s_row

        for r in range(4):
            dst[r // 2, pl.ds(64 * (r % 2), 64), :] = jnp.where(low_half, block(r), block(r + 4))

    def low_levels(dst):
        pairs = packed_level2()
        for half in range(2):
            dst[half, pl.ds(128, 16), :] = pairs[16 * half : 16 * half + 16]
            dst[half, pl.ds(144, 8), :] = delta

    third_rows(0, their_rows, partner_out)
    low_levels(partner_out)
    swap = remote(partner_out, partner_in, p_send, p_recv, partner)
    swap.start()

    for slot in range(1, 4):
        add_rows(512, my_rows, slot, step_columns(slot))
    third_rows(512, my_rows, mine)
    low_levels(mine)
    swap.wait_recv()
    mine[...] += partner_in[...]

    def pack(dst, value):
        dst[pl.ds(0, 128), :] = value[:128].astype(BF)
        exact = value[128:144]
        high = exact.astype(BF)
        dst[pl.ds(128, 16), :] = high
        dst[pl.ds(144, 16), :] = (exact - high.astype(F32)).astype(BF)
        exact = value[144:152]
        high = exact.astype(BF).astype(F32)
        dst[pl.ds(160, 16), :] = jnp.concatenate([high, exact - high], axis=0).astype(BF)

    def unpack(src):
        second = src[pl.ds(128, 16), :].astype(F32) + src[pl.ds(144, 16), :].astype(F32)
        pair = src[pl.ds(160, 16), :].astype(F32)
        third = src[pl.ds(0, 128), :].astype(F32)
        return jnp.concatenate([third, second, pair[:8] + pair[8:]], axis=0)

    def x_copy(src, half, by):
        at = 3 * half + by - 1
        return remote(src, in_x.at[at], x_send.at[at], x_recv.at[at], x_peer(by))

    def z_copy(src, half, by):
        at = 3 * half + by - 1
        return remote(src, in_z.at[at], z_send.at[at], z_recv.at[at], z_peer(by))

    def up_z(src, half):
        for by in range(1, 4):

            @pl.when(z + by < NZ)
            def _():
                z_copy(src, half, by).start()

    def add_lower_z(dst, half):
        for by in range(1, 4):

            @pl.when(z >= by)
            def _():
                z_copy(out_2, half, by).wait_recv()
                dst[...] += unpack(in_z.at[3 * half + by - 1])

    pack(out_1.at[0], mine[0])
    pack(out_1.at[1], mine[1])
    for by in range(1, 4):
        x_copy(out_1.at[0], 0, by).start()
    @pl.when(z < NZ - 1)
    def _():
        pl.semaphore_wait(z_ready, NZ - 1 - z)

    up_z(out_1.at[1], 1)
    swap.wait_send()

    below = partner_out.at[1]
    below[...] = jnp.zeros((PART, 128), F32)
    add_lower_z(below, 1)
    pack(out_low, below[...])
    mine[1] += below[...]
    pack(out_2.at[1], mine[1])
    for by in range(1, 4):

        @pl.when(x + by < NX)
        def _():
            x_copy(out_2.at[1], 1, by).start()

        @pl.when(x + by >= NX)
        def _():
            x_copy(out_low, 1, by).start()

    total = upto = mine[0]
    for by in range(1, 4):
        x_copy(out_1.at[0], 0, by).wait_recv()
        other = unpack(in_x.at[by - 1])
        total = total + other
        upto = upto + jnp.where(x >= by, other, jnp.zeros_like(other))
    pack(out_2.at[0], total)
    up_z(out_2.at[0], 0)
    mine[0] = upto

    for by in range(1, 4):
        x_copy(out_low, 1, by).wait_recv()
        mine[1] += unpack(in_x.at[3 + by - 1])
    add_lower_z(mine.at[0], 0)

    scale = total_steps ** (-0.2)
    ends = mine[0, pl.ds(144, 8), :]
    ends_k = jnp.broadcast_to(ends.T[:64, :1], (64, 128))
    first_ref[...] = ends[:1, :64] * scale
    for half in range(2):
        second_ref[pl.ds(16 * half, 16), :] = mine[half, pl.ds(128, 16), :] * scale**2

    def level2_row(r):
        row = mine[lax.div(n, 4), pl.ds(128 + 4 * lax.rem(n, 4) + r // 2, 1), :]
        other = pltpu.roll(row, 64, 1)
        low = low_half[:1]
        return jnp.where(low, row, other) if r % 2 == 0 else jnp.where(low, other, row)

    for r in range(4):
        row = jnp.where(low_half[:1], level2_row(r), level2_row(r + 4))
        values = ((row * ends_k - mine[r // 2, pl.ds(64 * (r % 2), 64), :]) * scale**3).T
        turned[pl.ds(r, 64, stride=8), :] = values[:64]
        turned[pl.ds(4 + r, 64, stride=8), :] = values[64:]
    for pair in range(32):
        both = [turned[pl.ds(16 * pair + 8 * k, 8), :] for k in range(2)]
        third_ref[:, pl.ds(128 * pair, 128)] = jnp.concatenate(both, axis=1)

    @pl.when(has_left)
    def _():
        to_left.wait_send()

    @pl.when(has_right)
    def _():
        to_right.wait_send()

    for copy in y_copies:
        copy.wait_send()
    for by in range(1, 4):
        for half in range(2):
            x_copy(out_low, half, by).wait_send()

            @pl.when(z + by < NZ)
            def _():
                z_copy(out_low, half, by).wait_send()


def emit(*refs):
    copies = [
        pltpu.make_async_copy(src, dst, refs[8].at[k])
        for k, (src, dst) in enumerate(zip(refs[:4], refs[4:8]))
    ]
    for copy in copies:
        copy.start()
    for copy in copies:
        copy.wait()


def per_device(total_steps, recording, conv_weight, conv_bias, projection):
    vmem = pl.BlockSpec(memory_space=pltpu.VMEM)
    hbm = pl.BlockSpec(memory_space=pltpu.HBM)
    operands = (recording, conv_weight.reshape(3, 3 * C, C), conv_bias, projection.T)
    operands = [pltpu.with_memory_space_constraint(a, pltpu.HBM) for a in operands]
    out_shape = (
        jax.ShapeDtypeStruct((PATH, TD), BF),
        jax.ShapeDtypeStruct((8, PATH * PATH), F32),
        jax.ShapeDtypeStruct((32, 128), F32),
        jax.ShapeDtypeStruct((1, PATH), F32),
    )
    results = pl.pallas_call(
        functools.partial(kernel, total_steps),
        out_shape=out_shape,
        in_specs=[hbm, hbm, hbm, hbm],
        out_specs=(vmem, vmem, vmem, vmem),
        scratch_shapes=[
            pltpu.VMEM((3, 3 * C, C), BF),
            pltpu.VMEM((3, C), F32),
            pltpu.VMEM((PATH, C), BF),
            pltpu.VMEM((ROWS, C), BF),
            pltpu.VMEM((ROWS, C), BF),
            pltpu.VMEM((ROWS, C), BF),
            pltpu.VMEM((4, PATH, 128 + TD), BF),
            pltpu.VMEM((4, PATH, TILE), F32),
            pltpu.VMEM((4, PATH, TILE), F32),
            pltpu.VMEM((PATH, 128), F32),
            pltpu.VMEM((1168, 128), F32),
            pltpu.VMEM((64, 128), F32),
            pltpu.VMEM((2, PART, 128), F32),
            pltpu.VMEM((512, PATH), F32),
            pltpu.VMEM((2, PART, 128), F32),
            pltpu.VMEM((2, PART, 128), F32),
            pltpu.VMEM((2, PAY, 128), BF),
            pltpu.VMEM((2, PAY, 128), BF),
            pltpu.VMEM((PAY, 128), BF),
            pltpu.VMEM((6, PAY, 128), BF),
            pltpu.VMEM((6, PAY, 128), BF),
            pltpu.SemaphoreType.DMA((3,)),
            pltpu.SemaphoreType.DMA((2,)),
            pltpu.SemaphoreType.DMA,
            pltpu.SemaphoreType.DMA((2,)),
            pltpu.SemaphoreType.DMA((2,)),
            pltpu.SemaphoreType.DMA((3, 4)),
            pltpu.SemaphoreType.DMA((3, 4)),
            pltpu.SemaphoreType.DMA,
            pltpu.SemaphoreType.DMA,
            pltpu.SemaphoreType.DMA((6,)),
            pltpu.SemaphoreType.DMA((6,)),
            pltpu.SemaphoreType.DMA((6,)),
            pltpu.SemaphoreType.DMA((6,)),
            pltpu.SemaphoreType.REGULAR,
        ],
        compiler_params=pltpu.CompilerParams(
            collective_id=0, has_side_effects=True, vmem_limit_bytes=48 << 20
        ),
    )(*operands)
    path_points, third, second, first = pl.pallas_call(
        emit,
        out_shape=out_shape,
        in_specs=[vmem] * 4,
        out_specs=[hbm] * 4,
        scratch_shapes=[pltpu.SemaphoreType.DMA((4,))],
        compiler_params=pltpu.CompilerParams(vmem_limit_bytes=1 << 20),
    )(*results)
    return path_points.T, first, second.reshape(1, PATH * PATH), third[None]


def solution(mesh):
    total_steps = TD * mesh.shape["wide"] * mesh.shape["narrow"]
    return jax.shard_map(
        functools.partial(per_device, total_steps),
        mesh=mesh,
        in_specs=(P(("wide", "narrow"), None), P(), P(), P()),
        out_specs=(
            P(("wide", "narrow"), None),
            P("wide", None),
            P("wide", None),
            P("wide", "narrow", None),
        ),
        check_vma=False,
    )
```

```python
import functools

import jax
import jax.numpy as jnp
from jax import lax
from jax.experimental import pallas as pl
from jax.experimental.pallas import tpu as pltpu
from jax.sharding import PartitionSpec as P

C = 512
PATH = 64
TD = 1024
OFF = 32
ROWS = OFF + TD + 32
NX = 4
NZ = 4
NY = 4
TILE = 256
PART = 128 + 16 + 8
PAY = 128 + 32 + 16
MESH = pl.DeviceIdType.MESH
BF = jnp.bfloat16
F32 = jnp.float32


def silu(v):
    half = 0.5 * v
    return half + half * jnp.tanh(half)


def nt_dot(a, b):
    return lax.dot_general(a, b, (((1,), (1,)), ((), ())), preferred_element_type=F32)


def kernel(
    total_steps,
    rec_hbm,
    weight_hbm,
    bias_hbm,
    proj_hbm,
    path_ref,
    third_ref,
    second_ref,
    first_ref,
    weights,
    bias_ref,
    proj_ref,
    h0,
    h1,
    h2,
    seg,
    mid,
    step,
    centre,
    acc,
    level2,
    mine,
    turned,
    partner_out,
    partner_in,
    out_1,
    out_2,
    out_low,
    in_x,
    in_z,
    w_sem,
    small_sem,
    r_sem,
    halo_send,
    halo_recv,
    y_send,
    y_recv,
    p_send,
    p_recv,
    x_send,
    x_recv,
    z_send,
    z_recv,
    z_ready,
):
    w = lax.axis_index("wide")
    n = lax.axis_index("narrow")
    z, x = lax.div(w, NX), lax.rem(w, NX)
    y, core = lax.div(n, 2), lax.rem(n, 2)
    g = w * 8 + n
    last_g = NX * NZ * 8 - 1
    has_left = g > 0
    has_right = g < last_g
    left = (lax.div(g + last_g, 8) % (NX * NZ), lax.rem(g + last_g, 8))
    right = (lax.div(g + 1, 8) % (NX * NZ), lax.rem(g + 1, 8))

    def y_peer(by):
        return (w, lax.rem(y + by, NY) * 2 + core)

    def x_peer(by):
        return (z * NX + lax.rem(x + by, NX), n)

    def z_peer(by):
        return ((z + by) * NX + x, n)

    partner = (w, y * 2 + 1 - core)

    weight_copies = [
        pltpu.make_async_copy(weight_hbm.at[l], weights.at[l], w_sem.at[l]) for l in range(3)
    ]
    own_copy = pltpu.make_async_copy(rec_hbm, h0.at[pl.ds(OFF, TD)], r_sem)
    small_copies = [
        pltpu.make_async_copy(bias_hbm, bias_ref, small_sem.at[0]),
        pltpu.make_async_copy(proj_hbm, proj_ref, small_sem.at[1]),
    ]
    own_copy.start()
    small_copies[0].start()
    weight_copies[0].start()

    barrier = pltpu.get_barrier_semaphore()

    @pl.when(has_left)
    def _():
        pl.semaphore_signal(barrier, inc=1, device_id=left, device_id_type=MESH)

    @pl.when(has_right)
    def _():
        pl.semaphore_signal(barrier, inc=1, device_id=right, device_id_type=MESH)

    for by in range(1, 4):
        pl.semaphore_signal(barrier, inc=1, device_id=y_peer(by), device_id_type=MESH)
        pl.semaphore_signal(barrier, inc=1, device_id=x_peer(by), device_id_type=MESH)

        @pl.when(z + by < NZ)
        def _():
            pl.semaphore_signal(barrier, inc=1, device_id=z_peer(by), device_id_type=MESH)

    pl.semaphore_signal(barrier, inc=1, device_id=partner, device_id_type=MESH)
    greeted = has_left.astype(jnp.int32) + has_right.astype(jnp.int32) + 7 + z
    pl.semaphore_wait(barrier, greeted)
    for by in range(1, 4):

        @pl.when(z >= by)
        def _():
            pl.semaphore_signal(z_ready, inc=1, device_id=z_peer(-by), device_id_type=MESH)

    def remote(src, dst, send, recv, device):
        return pltpu.make_async_remote_copy(
            src_ref=src,
            dst_ref=dst,
            send_sem=send,
            recv_sem=recv,
            device_id=device,
            device_id_type=MESH,
        )

    to_left = remote(
        rec_hbm.at[pl.ds(0, 16)],
        h0.at[pl.ds(OFF + TD, 16)],
        halo_send.at[0],
        halo_recv.at[0],
        left,
    )
    to_right = remote(
        rec_hbm.at[pl.ds(TD - 16, 16)],
        h0.at[pl.ds(OFF - 16, 16)],
        halo_send.at[1],
        halo_recv.at[1],
        right,
    )

    @pl.when(has_left)
    def _():
        to_left.start()

    @pl.when(has_right)
    def _():
        to_right.start()

    def conv(layer, src, begin, end):
        d = 2**layer
        xs = [src[pl.ds(begin + (k - 1) * d, end - begin), :] for k in range(3)]
        centre_rows = xs[1].astype(F32)
        both = jnp.concatenate(xs, axis=1)
        totals = jnp.dot(both, weights[layer], preferred_element_type=F32)
        return (centre_rows + silu(totals + bias_ref[pl.ds(layer, 1), :])).astype(BF)

    first_tile, last_tile = (OFF - 16, OFF + 128), (OFF + TD - 128, OFF + TD + 16)
    tiles = [first_tile] + [(OFF + 128 * i, OFF + 128 * i + 128) for i in range(1, 7)] + [last_tile]

    def put(dst, rows, i):
        begin, end = tiles[i]
        dst[pl.ds(begin, end - begin), :] = rows
        if i == 0:
            dst[pl.ds(OFF - 16, 16), :] = jnp.where(has_left, rows[:16], jnp.zeros_like(rows[:16]))
        if i == 7:
            dst[pl.ds(OFF + TD, 16), :] = jnp.where(
                has_right, rows[128:], jnp.zeros_like(rows[128:])
            )

    own_copy.wait()
    small_copies[0].wait()
    weight_copies[0].wait()
    weight_copies[1].start()
    small_copies[1].start()
    weight_copies[2].start()
    for i in range(1, 6):
        put(h1, conv(0, h0, *tiles[i]), i)

    @pl.when(has_left)
    def _():
        to_right.wait_recv()

    @pl.when(jnp.logical_not(has_left))
    def _():
        h0[pl.ds(OFF - 16, 16), :] = jnp.zeros((16, C), BF)

    @pl.when(has_right)
    def _():
        to_left.wait_recv()

    @pl.when(jnp.logical_not(has_right))
    def _():
        h0[pl.ds(OFF + TD, 16), :] = jnp.zeros((16, C), BF)

    put(h1, conv(0, h0, *tiles[0]), 0)

    y_copies = []
    sent_lanes = (pl.ds(0, 640), pl.ds(640, TILE), pl.ds(896, TILE))

    def send_tile(t):
        lanes = sent_lanes[t]
        for slot, by in ((1, 1), (2, 3), (3, 2)):
            copy = remote(
                seg.at[0, :, lanes],
                seg.at[slot, :, lanes],
                y_send.at[slot - 1, t],
                y_recv.at[slot - 1, t],
                y_peer(by),
            )
            copy.start()
            y_copies.append(copy)

    def finish(i):
        begin, end = tiles[i]
        end = min(end, OFF + TD)
        rows = conv(2, h2, begin, end)
        points = nt_dot(proj_ref[...], rows)
        if i == 0:
            edge = jnp.where(has_left, points[:, 15:16], jnp.zeros((PATH, 1), F32))
            seg[0, :, pl.ds(0, 128)] = jnp.broadcast_to(edge, (PATH, 128)).astype(BF)
            points = points[:, 16:]
        points = points.astype(BF)
        path_ref[:, pl.ds(128 * i, 128)] = points
        seg[0, :, pl.ds(128 + 128 * i, 128)] = points
        if i in (3, 5, 7):
            send_tile(i // 2 - 1)

    def layer_1(*which):
        for i in which:
            put(h1, conv(0, h0, *tiles[i]), i)

    def layer_2(*which):
        for i in which:
            put(h2, conv(1, h1, *tiles[i]), i)

    weight_copies[1].wait()
    layer_2(0, 1, 2)
    weight_copies[2].wait()
    small_copies[1].wait()
    finish(0)
    layer_2(3)
    finish(1)
    layer_2(4)
    finish(2)
    layer_1(6)
    finish(3)
    layer_1(7)
    layer_2(5, 6)
    finish(4)
    layer_2(7)
    finish(5)
    known = seg[0, :, pl.ds(128, 640)].astype(F32)
    mean = jnp.sum(known, axis=1, keepdims=True) * (1.0 / 640)
    centre[...] = jnp.broadcast_to(mean, (PATH, 128))
    finish(6)
    finish(7)

    def prepare(slot, t, buf):
        window = seg[slot, :, pl.ds(TILE * t, 384)].astype(F32)
        now, before = window[:, 128:], window[:, 127:383]
        step[buf] = now - before
        wide_centre = jnp.concatenate([centre[...]] * 2, axis=1)
        mid[buf] = 0.5 * (now + before) - wide_centre

    def step_columns(buf):
        d = step[buf]
        high = d.astype(BF)
        low = (d - high.astype(F32)).astype(BF)
        return jnp.concatenate([high, low], axis=0)

    def add_rows(at, row_begin, buf, columns):
        m = mid[buf].astype(BF)
        d = (step[buf] * (1.0 / 12.0)).astype(BF)

        def spread(ref, r):
            row = jnp.broadcast_to(ref[buf, pl.ds(row_begin + r, 1), :], (16, TILE)).astype(BF)
            return jnp.concatenate([row] * 4, axis=0)

        rows = [spread(mid, r) * m + spread(step, r) * d for r in range(8)]
        acc[pl.ds(at, 512), :] += nt_dot(jnp.concatenate(rows, axis=0), columns)

    def add_level2(buf, columns):
        m = mid[buf]
        high = m.astype(BF)
        low = (m - high.astype(F32)).astype(BF)
        ones = jnp.ones((16, TILE), BF)
        acc[pl.ds(1024, 144), :] += nt_dot(jnp.concatenate([high, low, ones], axis=0), columns)

    their_rows = y * 16 + (1 - core) * 8
    my_rows = y * 16 + core * 8
    acc[...] = jnp.zeros_like(acc)

    def wait_tile(slot, t):
        lanes = sent_lanes[t]
        remote(
            seg.at[0, :, lanes],
            seg.at[slot, :, lanes],
            y_send.at[slot - 1, t],
            y_recv.at[slot - 1, t],
            y_peer(1),
        ).wait_recv()

    def everything(steps):
        for at, (slot, t) in enumerate(steps):
            prepare(slot, t, at % 4)
            columns = step_columns(at % 4)
            add_rows(0, their_rows, at % 4, columns)
            add_level2(at % 4, columns)
            add_rows(512, my_rows, at % 4, columns)

    steps = [(0, t) for t in range(4)]
    for sent, group in enumerate(((0, 1), (2,))):
        for slot in range(1, 4):
            wait_tile(slot, sent)
        everything(steps + [(slot, t) for t in group for slot in range(1, 4)])
        steps = []
    for slot in range(1, 4):
        wait_tile(slot, 2)
    for slot in range(1, 4):
        prepare(slot, 3, slot)
        columns = step_columns(slot)
        add_rows(0, their_rows, slot, columns)
        add_level2(slot, columns)

    low_half = lax.broadcasted_iota(jnp.int32, (64, 128), 1) < 64

    def both_halves(v):
        return v + pltpu.roll(v, 64, 1)

    def packed_level2():
        even, odd = level2[pl.ds(0, 32, stride=2), :], level2[pl.ds(1, 32, stride=2), :]
        return jnp.where(low_half[:32], even, odd)

    local2 = both_halves(acc[pl.ds(1024, 64), :] + acc[pl.ds(1088, 64), :])
    delta = both_halves(acc[pl.ds(1152, 8), :])
    middle = centre[...]
    own2 = local2 + middle * delta[:1]
    level2[pl.ds(0, 64), :] = own2

    def third_rows(at, row_begin, dst):
        def block(r):
            rows = both_halves(acc[pl.ds(at + 64 * r, 64), :])
            c_row = centre[pl.ds(row_begin + r, 1), :]
            s_row = level2[pl.ds(row_begin + r, 1), :]
            return rows + c_row * local2 + middle * s_row

        for r in range(4):
            dst[r // 2, pl.ds(64 * (r % 2), 64), :] = jnp.where(low_half, block(r), block(r + 4))

    def low_levels(dst):
        pairs = packed_level2()
        for half in range(2):
            dst[half, pl.ds(128, 16), :] = pairs[16 * half : 16 * half + 16]
            dst[half, pl.ds(144, 8), :] = delta

    third_rows(0, their_rows, partner_out)
    low_levels(partner_out)
    swap = remote(partner_out, partner_in, p_send, p_recv, partner)
    swap.start()

    for slot in range(1, 4):
        add_rows(512, my_rows, slot, step_columns(slot))
    third_rows(512, my_rows, mine)
    low_levels(mine)
    swap.wait_recv()
    mine[...] += partner_in[...]

    def pack(dst, value):
        dst[pl.ds(0, 128), :] = value[:128].astype(BF)
        exact = value[128:144]
        high = exact.astype(BF)
        dst[pl.ds(128, 16), :] = high
        dst[pl.ds(144, 16), :] = (exact - high.astype(F32)).astype(BF)
        exact = value[144:152]
        high = exact.astype(BF).astype(F32)
        dst[pl.ds(160, 16), :] = jnp.concatenate([high, exact - high], axis=0).astype(BF)

    def unpack(src):
        second = src[pl.ds(128, 16), :].astype(F32) + src[pl.ds(144, 16), :].astype(F32)
        pair = src[pl.ds(160, 16), :].astype(F32)
        third = src[pl.ds(0, 128), :].astype(F32)
        return jnp.concatenate([third, second, pair[:8] + pair[8:]], axis=0)

    def x_copy(src, half, by):
        at = 3 * half + by - 1
        return remote(src, in_x.at[at], x_send.at[at], x_recv.at[at], x_peer(by))

    def z_copy(src, half, by):
        at = 3 * half + by - 1
        return remote(src, in_z.at[at], z_send.at[at], z_recv.at[at], z_peer(by))

    def up_z(src, half):
        for by in range(1, 4):

            @pl.when(z + by < NZ)
            def _():
                z_copy(src, half, by).start()

    def add_lower_z(dst, half):
        for by in range(1, 4):

            @pl.when(z >= by)
            def _():
                z_copy(out_2, half, by).wait_recv()
                dst[...] += unpack(in_z.at[3 * half + by - 1])

    pack(out_1.at[0], mine[0])
    pack(out_1.at[1], mine[1])
    for by in range(1, 4):
        x_copy(out_1.at[0], 0, by).start()
    @pl.when(z < NZ - 1)
    def _():
        pl.semaphore_wait(z_ready, NZ - 1 - z)

    up_z(out_1.at[1], 1)
    swap.wait_send()

    below = partner_out.at[1]
    below[...] = jnp.zeros((PART, 128), F32)
    add_lower_z(below, 1)
    pack(out_low, below[...])
    mine[1] += below[...]
    pack(out_2.at[1], mine[1])
    for by in range(1, 4):

        @pl.when(x + by < NX)
        def _():
            x_copy(out_2.at[1], 1, by).start()

        @pl.when(x + by >= NX)
        def _():
            x_copy(out_low, 1, by).start()

    total = upto = mine[0]
    for by in range(1, 4):
        x_copy(out_1.at[0], 0, by).wait_recv()
        other = unpack(in_x.at[by - 1])
        total = total + other
        upto = upto + jnp.where(x >= by, other, jnp.zeros_like(other))
    pack(out_2.at[0], total)
    up_z(out_2.at[0], 0)
    mine[0] = upto

    for by in range(1, 4):
        x_copy(out_low, 1, by).wait_recv()
        mine[1] += unpack(in_x.at[3 + by - 1])
    add_lower_z(mine.at[0], 0)

    scale = total_steps ** (-0.2)
    ends = mine[0, pl.ds(144, 8), :]
    ends_k = jnp.broadcast_to(ends.T[:64, :1], (64, 128))
    first_ref[...] = ends[:1, :64] * scale
    for half in range(2):
        second_ref[pl.ds(16 * half, 16), :] = mine[half, pl.ds(128, 16), :] * scale**2

    def level2_row(r):
        row = mine[lax.div(n, 4), pl.ds(128 + 4 * lax.rem(n, 4) + r // 2, 1), :]
        other = pltpu.roll(row, 64, 1)
        low = low_half[:1]
        return jnp.where(low, row, other) if r % 2 == 0 else jnp.where(low, other, row)

    for r in range(4):
        row = jnp.where(low_half[:1], level2_row(r), level2_row(r + 4))
        values = ((row * ends_k - mine[r // 2, pl.ds(64 * (r % 2), 64), :]) * scale**3).T
        turned[pl.ds(r, 64, stride=8), :] = values[:64]
        turned[pl.ds(4 + r, 64, stride=8), :] = values[64:]
    for pair in range(32):
        both = [turned[pl.ds(16 * pair + 8 * k, 8), :] for k in range(2)]
        third_ref[:, pl.ds(128 * pair, 128)] = jnp.concatenate(both, axis=1)

    @pl.when(has_left)
    def _():
        to_left.wait_send()

    @pl.when(has_right)
    def _():
        to_right.wait_send()

    for copy in y_copies:
        copy.wait_send()
    for by in range(1, 4):
        for half in range(2):
            x_copy(out_low, half, by).wait_send()

            @pl.when(z + by < NZ)
            def _():
                z_copy(out_low, half, by).wait_send()


def emit(*refs):
    copies = [
        pltpu.make_async_copy(src, dst, refs[8].at[k])
        for k, (src, dst) in enumerate(zip(refs[:4], refs[4:8]))
    ]
    for copy in copies:
        copy.start()
    for copy in copies:
        copy.wait()


def per_device(total_steps, recording, conv_weight, conv_bias, projection):
    vmem = pl.BlockSpec(memory_space=pltpu.VMEM)
    hbm = pl.BlockSpec(memory_space=pltpu.HBM)
    operands = (recording, conv_weight.reshape(3, 3 * C, C), conv_bias, projection.T)
    operands = [pltpu.with_memory_space_constraint(a, pltpu.HBM) for a in operands]
    out_shape = (
        jax.ShapeDtypeStruct((PATH, TD), BF),
        jax.ShapeDtypeStruct((8, PATH * PATH), F32),
        jax.ShapeDtypeStruct((32, 128), F32),
        jax.ShapeDtypeStruct((1, PATH), F32),
    )
    results = pl.pallas_call(
        functools.partial(kernel, total_steps),
        out_shape=out_shape,
        in_specs=[hbm, hbm, hbm, hbm],
        out_specs=(vmem, vmem, vmem, vmem),
        scratch_shapes=[
            pltpu.VMEM((3, 3 * C, C), BF),
            pltpu.VMEM((3, C), F32),
            pltpu.VMEM((PATH, C), BF),
            pltpu.VMEM((ROWS, C), BF),
            pltpu.VMEM((ROWS, C), BF),
            pltpu.VMEM((ROWS, C), BF),
            pltpu.VMEM((4, PATH, 128 + TD), BF),
            pltpu.VMEM((4, PATH, TILE), F32),
            pltpu.VMEM((4, PATH, TILE), F32),
            pltpu.VMEM((PATH, 128), F32),
            pltpu.VMEM((1168, 128), F32),
            pltpu.VMEM((64, 128), F32),
            pltpu.VMEM((2, PART, 128), F32),
            pltpu.VMEM((512, PATH), F32),
            pltpu.VMEM((2, PART, 128), F32),
            pltpu.VMEM((2, PART, 128), F32),
            pltpu.VMEM((2, PAY, 128), BF),
            pltpu.VMEM((2, PAY, 128), BF),
            pltpu.VMEM((PAY, 128), BF),
            pltpu.VMEM((6, PAY, 128), BF),
            pltpu.VMEM((6, PAY, 128), BF),
            pltpu.SemaphoreType.DMA((3,)),
            pltpu.SemaphoreType.DMA((2,)),
            pltpu.SemaphoreType.DMA,
            pltpu.SemaphoreType.DMA((2,)),
            pltpu.SemaphoreType.DMA((2,)),
            pltpu.SemaphoreType.DMA((3, 3)),
            pltpu.SemaphoreType.DMA((3, 3)),
            pltpu.SemaphoreType.DMA,
            pltpu.SemaphoreType.DMA,
            pltpu.SemaphoreType.DMA((6,)),
            pltpu.SemaphoreType.DMA((6,)),
            pltpu.SemaphoreType.DMA((6,)),
            pltpu.SemaphoreType.DMA((6,)),
            pltpu.SemaphoreType.REGULAR,
        ],
        compiler_params=pltpu.CompilerParams(
            collective_id=0, has_side_effects=True, vmem_limit_bytes=48 << 20
        ),
    )(*operands)
    path_points, third, second, first = pl.pallas_call(
        emit,
        out_shape=out_shape,
        in_specs=[vmem] * 4,
        out_specs=[hbm] * 4,
        scratch_shapes=[pltpu.SemaphoreType.DMA((4,))],
        compiler_params=pltpu.CompilerParams(vmem_limit_bytes=1 << 20),
    )(*results)
    return path_points.T, first, second.reshape(1, PATH * PATH), third[None]


def solution(mesh):
    total_steps = TD * mesh.shape["wide"] * mesh.shape["narrow"]
    return jax.shard_map(
        functools.partial(per_device, total_steps),
        mesh=mesh,
        in_specs=(P(("wide", "narrow"), None), P(), P(), P()),
        out_specs=(
            P(("wide", "narrow"), None),
            P("wide", None),
            P("wide", None),
            P("wide", "narrow", None),
        ),
        check_vma=False,
    )
```

```python
import functools

import jax
import jax.numpy as jnp
from jax import lax
from jax.experimental import pallas as pl
from jax.experimental.pallas import tpu as pltpu
from jax.sharding import PartitionSpec as P

C = 512
PATH = 64
TD = 1024
OFF = 32
ROWS = OFF + TD + 32
NX = 4
NZ = 4
NY = 4
TILE = 256
PART = 128 + 16 + 8
PAY = 128 + 32 + 16
MESH = pl.DeviceIdType.MESH
BF = jnp.bfloat16
F32 = jnp.float32


def silu(v):
    half = 0.5 * v
    return half + half * jnp.tanh(half)


def nt_dot(a, b):
    return lax.dot_general(a, b, (((1,), (1,)), ((), ())), preferred_element_type=F32)


def kernel(
    total_steps,
    rec_hbm,
    weight_hbm,
    bias_hbm,
    proj_hbm,
    path_ref,
    third_ref,
    second_ref,
    first_ref,
    weights,
    bias_ref,
    proj_ref,
    h0,
    h1,
    h2,
    seg,
    mid,
    step,
    centre,
    acc,
    level2,
    mine,
    turned,
    partner_out,
    partner_in,
    out_1,
    out_2,
    out_low,
    in_x,
    in_z,
    w_sem,
    small_sem,
    r_sem,
    halo_send,
    halo_recv,
    y_send,
    y_recv,
    p_send,
    p_recv,
    x_send,
    x_recv,
    z_send,
    z_recv,
    z_ready,
):
    w = lax.axis_index("wide")
    n = lax.axis_index("narrow")
    z, x = lax.div(w, NX), lax.rem(w, NX)
    y, core = lax.div(n, 2), lax.rem(n, 2)
    g = w * 8 + n
    last_g = NX * NZ * 8 - 1
    has_left = g > 0
    has_right = g < last_g
    left = (lax.div(g + last_g, 8) % (NX * NZ), lax.rem(g + last_g, 8))
    right = (lax.div(g + 1, 8) % (NX * NZ), lax.rem(g + 1, 8))

    def y_peer(by):
        return (w, lax.rem(y + by, NY) * 2 + core)

    def x_peer(by):
        return (z * NX + lax.rem(x + by, NX), n)

    def z_peer(by):
        return ((z + by) * NX + x, n)

    partner = (w, y * 2 + 1 - core)

    weight_copies = [
        pltpu.make_async_copy(weight_hbm.at[l], weights.at[l], w_sem.at[l]) for l in range(3)
    ]
    own_copy = pltpu.make_async_copy(rec_hbm, h0.at[pl.ds(OFF, TD)], r_sem)
    small_copies = [
        pltpu.make_async_copy(bias_hbm, bias_ref, small_sem.at[0]),
        pltpu.make_async_copy(proj_hbm, proj_ref, small_sem.at[1]),
    ]
    own_copy.start()
    small_copies[0].start()
    weight_copies[0].start()

    barrier = pltpu.get_barrier_semaphore()

    @pl.when(has_left)
    def _():
        pl.semaphore_signal(barrier, inc=1, device_id=left, device_id_type=MESH)

    @pl.when(has_right)
    def _():
        pl.semaphore_signal(barrier, inc=1, device_id=right, device_id_type=MESH)

    for by in range(1, 4):
        pl.semaphore_signal(barrier, inc=1, device_id=y_peer(by), device_id_type=MESH)
        pl.semaphore_signal(barrier, inc=1, device_id=x_peer(by), device_id_type=MESH)

        @pl.when(z + by < NZ)
        def _():
            pl.semaphore_signal(barrier, inc=1, device_id=z_peer(by), device_id_type=MESH)

    pl.semaphore_signal(barrier, inc=1, device_id=partner, device_id_type=MESH)
    greeted = has_left.astype(jnp.int32) + has_right.astype(jnp.int32) + 7 + z
    pl.semaphore_wait(barrier, greeted)
    for by in range(1, 4):

        @pl.when(z >= by)
        def _():
            pl.semaphore_signal(z_ready, inc=1, device_id=z_peer(-by), device_id_type=MESH)

    def remote(src, dst, send, recv, device):
        return pltpu.make_async_remote_copy(
            src_ref=src,
            dst_ref=dst,
            send_sem=send,
            recv_sem=recv,
            device_id=device,
            device_id_type=MESH,
        )

    to_left = remote(
        rec_hbm.at[pl.ds(0, 16)],
        h0.at[pl.ds(OFF + TD, 16)],
        halo_send.at[0],
        halo_recv.at[0],
        left,
    )
    to_right = remote(
        rec_hbm.at[pl.ds(TD - 16, 16)],
        h0.at[pl.ds(OFF - 16, 16)],
        halo_send.at[1],
        halo_recv.at[1],
        right,
    )

    @pl.when(has_left)
    def _():
        to_left.start()

    @pl.when(has_right)
    def _():
        to_right.start()

    def conv(layer, src, begin, end):
        d = 2**layer
        xs = [src[pl.ds(begin + (k - 1) * d, end - begin), :] for k in range(3)]
        centre_rows = xs[1].astype(F32)
        both = jnp.concatenate(xs, axis=1)
        totals = jnp.dot(both, weights[layer], preferred_element_type=F32)
        return (centre_rows + silu(totals + bias_ref[pl.ds(layer, 1), :])).astype(BF)

    first_tile, last_tile = (OFF - 16, OFF + 128), (OFF + TD - 128, OFF + TD + 16)
    tiles = [first_tile] + [(OFF + 128 * i, OFF + 128 * i + 128) for i in range(1, 7)] + [last_tile]

    def put(dst, rows, i):
        begin, end = tiles[i]
        dst[pl.ds(begin, end - begin), :] = rows
        if i == 0:
            dst[pl.ds(OFF - 16, 16), :] = jnp.where(has_left, rows[:16], jnp.zeros_like(rows[:16]))
        if i == 7:
            dst[pl.ds(OFF + TD, 16), :] = jnp.where(
                has_right, rows[128:], jnp.zeros_like(rows[128:])
            )

    own_copy.wait()
    small_copies[0].wait()
    weight_copies[0].wait()
    weight_copies[1].start()
    small_copies[1].start()
    weight_copies[2].start()
    for i in range(1, 6):
        put(h1, conv(0, h0, *tiles[i]), i)

    @pl.when(has_left)
    def _():
        to_right.wait_recv()

    @pl.when(jnp.logical_not(has_left))
    def _():
        h0[pl.ds(OFF - 16, 16), :] = jnp.zeros((16, C), BF)

    @pl.when(has_right)
    def _():
        to_left.wait_recv()

    @pl.when(jnp.logical_not(has_right))
    def _():
        h0[pl.ds(OFF + TD, 16), :] = jnp.zeros((16, C), BF)

    put(h1, conv(0, h0, *tiles[0]), 0)

    y_copies = []

    def send_tile(t):
        lanes = pl.ds(0, 384) if t == 0 else pl.ds(128 + TILE * t, TILE)
        for slot, by in ((1, 1), (2, 3), (3, 2)):
            copy = remote(
                seg.at[0, :, lanes],
                seg.at[slot, :, lanes],
                y_send.at[slot - 1, t],
                y_recv.at[slot - 1, t],
                y_peer(by),
            )
            copy.start()
            y_copies.append(copy)

    def finish(i):
        begin, end = tiles[i]
        end = min(end, OFF + TD)
        rows = conv(2, h2, begin, end)
        points = nt_dot(proj_ref[...], rows)
        if i == 0:
            edge = jnp.where(has_left, points[:, 15:16], jnp.zeros((PATH, 1), F32))
            seg[0, :, pl.ds(0, 128)] = jnp.broadcast_to(edge, (PATH, 128)).astype(BF)
            points = points[:, 16:]
        points = points.astype(BF)
        path_ref[:, pl.ds(128 * i, 128)] = points
        seg[0, :, pl.ds(128 + 128 * i, 128)] = points
        if i % 2 == 1:
            send_tile(i // 2)

    def layer_1(*which):
        for i in which:
            put(h1, conv(0, h0, *tiles[i]), i)

    def layer_2(*which):
        for i in which:
            put(h2, conv(1, h1, *tiles[i]), i)

    weight_copies[1].wait()
    layer_2(0, 1, 2)
    weight_copies[2].wait()
    small_copies[1].wait()
    finish(0)
    layer_2(3)
    finish(1)
    layer_2(4)
    finish(2)
    layer_1(6)
    finish(3)
    layer_1(7)
    layer_2(5, 6)
    finish(4)
    layer_2(7)
    finish(5)
    known = seg[0, :, pl.ds(128, 640)].astype(F32)
    mean = jnp.sum(known, axis=1, keepdims=True) * (1.0 / 640)
    centre[...] = jnp.broadcast_to(mean, (PATH, 128))
    finish(6)
    finish(7)

    def prepare(slot, t, buf):
        window = seg[slot, :, pl.ds(TILE * t, 384)].astype(F32)
        now, before = window[:, 128:], window[:, 127:383]
        step[buf] = now - before
        wide_centre = jnp.concatenate([centre[...]] * 2, axis=1)
        mid[buf] = 0.5 * (now + before) - wide_centre

    def step_columns(buf):
        d = step[buf]
        high = d.astype(BF)
        low = (d - high.astype(F32)).astype(BF)
        return jnp.concatenate([high, low], axis=0)

    def add_rows(at, row_begin, buf, columns):
        m = mid[buf].astype(BF)
        d = (step[buf] * (1.0 / 12.0)).astype(BF)

        def spread(ref, r):
            row = jnp.broadcast_to(ref[buf, pl.ds(row_begin + r, 1), :], (16, TILE)).astype(BF)
            return jnp.concatenate([row] * 4, axis=0)

        rows = [spread(mid, r) * m + spread(step, r) * d for r in range(8)]
        acc[pl.ds(at, 512), :] += nt_dot(jnp.concatenate(rows, axis=0), columns)

    def add_level2(buf, columns):
        m = mid[buf]
        high = m.astype(BF)
        low = (m - high.astype(F32)).astype(BF)
        ones = jnp.ones((16, TILE), BF)
        acc[pl.ds(1024, 144), :] += nt_dot(jnp.concatenate([high, low, ones], axis=0), columns)

    their_rows = y * 16 + (1 - core) * 8
    my_rows = y * 16 + core * 8
    acc[...] = jnp.zeros_like(acc)

    def wait_tile(slot, t):
        lanes = pl.ds(0, 384) if t == 0 else pl.ds(128 + TILE * t, TILE)
        remote(
            seg.at[0, :, lanes],
            seg.at[slot, :, lanes],
            y_send.at[slot - 1, t],
            y_recv.at[slot - 1, t],
            y_peer(1),
        ).wait_recv()

    def everything(steps):
        for at, (slot, t) in enumerate(steps):
            prepare(slot, t, at % 4)
            columns = step_columns(at % 4)
            add_rows(0, their_rows, at % 4, columns)
            add_level2(at % 4, columns)
            add_rows(512, my_rows, at % 4, columns)

    for t in range(2):
        for slot in range(1, 4):
            wait_tile(slot, t)
    everything(
        [(0, t) for t in range(4)] + [(slot, t) for t in range(2) for slot in range(1, 4)]
    )
    for t in (2, 3):
        wait_tile(1, t)
        wait_tile(2, t)
        everything([(1, t), (2, t)])
    wait_tile(3, 2)
    everything([(3, 2)])
    wait_tile(3, 3)
    prepare(3, 3, 3)
    last_columns = step_columns(3)
    add_rows(0, their_rows, 3, last_columns)
    add_level2(3, last_columns)

    low_half = lax.broadcasted_iota(jnp.int32, (64, 128), 1) < 64

    def both_halves(v):
        return v + pltpu.roll(v, 64, 1)

    def packed_level2():
        even, odd = level2[pl.ds(0, 32, stride=2), :], level2[pl.ds(1, 32, stride=2), :]
        return jnp.where(low_half[:32], even, odd)

    local2 = both_halves(acc[pl.ds(1024, 64), :] + acc[pl.ds(1088, 64), :])
    delta = both_halves(acc[pl.ds(1152, 8), :])
    middle = centre[...]
    own2 = local2 + middle * delta[:1]
    level2[pl.ds(0, 64), :] = own2

    def third_rows(at, row_begin, dst):
        def block(r):
            rows = both_halves(acc[pl.ds(at + 64 * r, 64), :])
            c_row = centre[pl.ds(row_begin + r, 1), :]
            s_row = level2[pl.ds(row_begin + r, 1), :]
            return rows + c_row * local2 + middle * s_row

        for r in range(4):
            dst[r // 2, pl.ds(64 * (r % 2), 64), :] = jnp.where(low_half, block(r), block(r + 4))

    def low_levels(dst):
        pairs = packed_level2()
        for half in range(2):
            dst[half, pl.ds(128, 16), :] = pairs[16 * half : 16 * half + 16]
            dst[half, pl.ds(144, 8), :] = delta

    third_rows(0, their_rows, partner_out)
    low_levels(partner_out)
    swap = remote(partner_out, partner_in, p_send, p_recv, partner)
    swap.start()

    add_rows(512, my_rows, 3, step_columns(3))
    third_rows(512, my_rows, mine)
    low_levels(mine)
    swap.wait_recv()
    mine[...] += partner_in[...]

    def pack(dst, value):
        dst[pl.ds(0, 128), :] = value[:128].astype(BF)
        exact = value[128:144]
        high = exact.astype(BF)
        dst[pl.ds(128, 16), :] = high
        dst[pl.ds(144, 16), :] = (exact - high.astype(F32)).astype(BF)
        exact = value[144:152]
        high = exact.astype(BF).astype(F32)
        dst[pl.ds(160, 16), :] = jnp.concatenate([high, exact - high], axis=0).astype(BF)

    def unpack(src):
        second = src[pl.ds(128, 16), :].astype(F32) + src[pl.ds(144, 16), :].astype(F32)
        pair = src[pl.ds(160, 16), :].astype(F32)
        third = src[pl.ds(0, 128), :].astype(F32)
        return jnp.concatenate([third, second, pair[:8] + pair[8:]], axis=0)

    def x_copy(src, half, by):
        at = 3 * half + by - 1
        return remote(src, in_x.at[at], x_send.at[at], x_recv.at[at], x_peer(by))

    def z_copy(src, half, by):
        at = 3 * half + by - 1
        return remote(src, in_z.at[at], z_send.at[at], z_recv.at[at], z_peer(by))

    def up_z(src, half):
        for by in range(1, 4):

            @pl.when(z + by < NZ)
            def _():
                z_copy(src, half, by).start()

    def add_lower_z(dst, half):
        for by in range(1, 4):

            @pl.when(z >= by)
            def _():
                z_copy(out_2, half, by).wait_recv()
                dst[...] += unpack(in_z.at[3 * half + by - 1])

    pack(out_1.at[0], mine[0])
    pack(out_1.at[1], mine[1])
    for by in range(1, 4):
        x_copy(out_1.at[0], 0, by).start()
    @pl.when(z < NZ - 1)
    def _():
        pl.semaphore_wait(z_ready, NZ - 1 - z)

    up_z(out_1.at[1], 1)
    swap.wait_send()

    below = partner_out.at[1]
    below[...] = jnp.zeros((PART, 128), F32)
    add_lower_z(below, 1)
    pack(out_low, below[...])
    mine[1] += below[...]
    pack(out_2.at[1], mine[1])
    for by in range(1, 4):

        @pl.when(x + by < NX)
        def _():
            x_copy(out_2.at[1], 1, by).start()

        @pl.when(x + by >= NX)
        def _():
            x_copy(out_low, 1, by).start()

    total = upto = mine[0]
    for by in range(1, 4):
        x_copy(out_1.at[0], 0, by).wait_recv()
        other = unpack(in_x.at[by - 1])
        total = total + other
        upto = upto + jnp.where(x >= by, other, jnp.zeros_like(other))
    pack(out_2.at[0], total)
    up_z(out_2.at[0], 0)
    mine[0] = upto

    for by in range(1, 4):
        x_copy(out_low, 1, by).wait_recv()
        mine[1] += unpack(in_x.at[3 + by - 1])
    add_lower_z(mine.at[0], 0)

    scale = total_steps ** (-0.2)
    ends = mine[0, pl.ds(144, 8), :]
    ends_k = jnp.broadcast_to(ends.T[:64, :1], (64, 128))
    first_ref[...] = ends[:1, :64] * scale
    for half in range(2):
        second_ref[pl.ds(16 * half, 16), :] = mine[half, pl.ds(128, 16), :] * scale**2

    def level2_row(r):
        row = mine[lax.div(n, 4), pl.ds(128 + 4 * lax.rem(n, 4) + r // 2, 1), :]
        other = pltpu.roll(row, 64, 1)
        low = low_half[:1]
        return jnp.where(low, row, other) if r % 2 == 0 else jnp.where(low, other, row)

    for r in range(4):
        row = jnp.where(low_half[:1], level2_row(r), level2_row(r + 4))
        values = ((row * ends_k - mine[r // 2, pl.ds(64 * (r % 2), 64), :]) * scale**3).T
        turned[pl.ds(r, 64, stride=8), :] = values[:64]
        turned[pl.ds(4 + r, 64, stride=8), :] = values[64:]
    for pair in range(32):
        both = [turned[pl.ds(16 * pair + 8 * k, 8), :] for k in range(2)]
        third_ref[:, pl.ds(128 * pair, 128)] = jnp.concatenate(both, axis=1)

    @pl.when(has_left)
    def _():
        to_left.wait_send()

    @pl.when(has_right)
    def _():
        to_right.wait_send()

    for copy in y_copies:
        copy.wait_send()
    for by in range(1, 4):
        for half in range(2):
            x_copy(out_low, half, by).wait_send()

            @pl.when(z + by < NZ)
            def _():
                z_copy(out_low, half, by).wait_send()


def emit(*refs):
    copies = [
        pltpu.make_async_copy(src, dst, refs[8].at[k])
        for k, (src, dst) in enumerate(zip(refs[:4], refs[4:8]))
    ]
    for copy in copies:
        copy.start()
    for copy in copies:
        copy.wait()


def per_device(total_steps, recording, conv_weight, conv_bias, projection):
    vmem = pl.BlockSpec(memory_space=pltpu.VMEM)
    hbm = pl.BlockSpec(memory_space=pltpu.HBM)
    operands = (recording, conv_weight.reshape(3, 3 * C, C), conv_bias, projection.T)
    operands = [pltpu.with_memory_space_constraint(a, pltpu.HBM) for a in operands]
    out_shape = (
        jax.ShapeDtypeStruct((PATH, TD), BF),
        jax.ShapeDtypeStruct((8, PATH * PATH), F32),
        jax.ShapeDtypeStruct((32, 128), F32),
        jax.ShapeDtypeStruct((1, PATH), F32),
    )
    results = pl.pallas_call(
        functools.partial(kernel, total_steps),
        out_shape=out_shape,
        in_specs=[hbm, hbm, hbm, hbm],
        out_specs=(vmem, vmem, vmem, vmem),
        scratch_shapes=[
            pltpu.VMEM((3, 3 * C, C), BF),
            pltpu.VMEM((3, C), F32),
            pltpu.VMEM((PATH, C), BF),
            pltpu.VMEM((ROWS, C), BF),
            pltpu.VMEM((ROWS, C), BF),
            pltpu.VMEM((ROWS, C), BF),
            pltpu.VMEM((4, PATH, 128 + TD), BF),
            pltpu.VMEM((4, PATH, TILE), F32),
            pltpu.VMEM((4, PATH, TILE), F32),
            pltpu.VMEM((PATH, 128), F32),
            pltpu.VMEM((1168, 128), F32),
            pltpu.VMEM((64, 128), F32),
            pltpu.VMEM((2, PART, 128), F32),
            pltpu.VMEM((512, PATH), F32),
            pltpu.VMEM((2, PART, 128), F32),
            pltpu.VMEM((2, PART, 128), F32),
            pltpu.VMEM((2, PAY, 128), BF),
            pltpu.VMEM((2, PAY, 128), BF),
            pltpu.VMEM((PAY, 128), BF),
            pltpu.VMEM((6, PAY, 128), BF),
            pltpu.VMEM((6, PAY, 128), BF),
            pltpu.SemaphoreType.DMA((3,)),
            pltpu.SemaphoreType.DMA((2,)),
            pltpu.SemaphoreType.DMA,
            pltpu.SemaphoreType.DMA((2,)),
            pltpu.SemaphoreType.DMA((2,)),
            pltpu.SemaphoreType.DMA((3, 4)),
            pltpu.SemaphoreType.DMA((3, 4)),
            pltpu.SemaphoreType.DMA,
            pltpu.SemaphoreType.DMA,
            pltpu.SemaphoreType.DMA((6,)),
            pltpu.SemaphoreType.DMA((6,)),
            pltpu.SemaphoreType.DMA((6,)),
            pltpu.SemaphoreType.DMA((6,)),
            pltpu.SemaphoreType.REGULAR,
        ],
        compiler_params=pltpu.CompilerParams(
            collective_id=0, has_side_effects=True, vmem_limit_bytes=48 << 20
        ),
    )(*operands)
    path_points, third, second, first = pl.pallas_call(
        emit,
        out_shape=out_shape,
        in_specs=[vmem] * 4,
        out_specs=[hbm] * 4,
        scratch_shapes=[pltpu.SemaphoreType.DMA((4,))],
        compiler_params=pltpu.CompilerParams(vmem_limit_bytes=1 << 20),
    )(*results)
    return path_points.T, first, second.reshape(1, PATH * PATH), third[None]


def solution(mesh):
    total_steps = TD * mesh.shape["wide"] * mesh.shape["narrow"]
    return jax.shard_map(
        functools.partial(per_device, total_steps),
        mesh=mesh,
        in_specs=(P(("wide", "narrow"), None), P(), P(), P()),
        out_specs=(
            P(("wide", "narrow"), None),
            P("wide", None),
            P("wide", None),
            P("wide", "narrow", None),
        ),
        check_vma=False,
    )
```
